32 devices in a mesh: tok: 16 (over z, x, core), head: 2 (over y).
Axes of the slice: x: 2, y: 2, z: 4, core: 2. Of those that a mesh axis runs over, the one named last changes fastest.
Arguments:
- qkv: bfloat16 [2048, 3, 7168], P(('tok', 'head')), may hold values from -80 to 80
- prefix_cache: bfloat16 [16, 256, 2, 7168], P('tok', None, None, 'head'), may hold values from -80 to 80
- suffix_lengths: int32 [16, 8], P('tok'), may hold values from 1 to 24, 128 in all within a row
- request_groups: int32 [16, 8], P('tok'), may hold values from 0 to 15, all different within a row
- prefix_owner: int32 [16], replicated, may hold values from 0 to 15, each once
Outputs:
- attended: bfloat16 [2048, 7168], P(('tok', 'head'))
- suffix_cache: bfloat16 [2048, 2, 7168], P('tok', None, 'head')
The draws below stay inside these ranges and needn't reach their ends.
Inputs may be any that keep to these rules, and one draw needn't show every extreme that they name: `suffix_lengths`: each row sums to 128; in each row the longest request has exactly 24 tokens. `request_groups`: the 8 requests of one row belong to 8 different groups; every group is read by some request. `prefix_owner`: every slot holds exactly one group.
All inputs are finite; a program needn't handle non-finite values.
Results may differ from the reference program's by a relative error of at most 0.003.
Values may be sent and summed in bfloat16 or wider, within the bound.
A program may use at most 64 MiB of HBM per device.

```python
import math
import jax
import jax.numpy as jnp
import numpy as np
from jax import lax

H = 32
HD = 224
TOK_DEV = 128
PRE = 256
HH = 7168
TOKENS = 2048
G = 16
REQ = 8
CAP = 24
N_TOK = 16


def draw_qkv(key, part):
    keys = jax.random.split(jax.random.fold_in(key, 11), 2)
    noise = jax.random.normal(keys[0], (TOKENS, 3, HH), jnp.float32)
    base = jax.random.normal(keys[1], (TOKENS + 3, HH), jnp.float32)
    nearby = 0.3 * (base[3:] + base[2:-1] + base[1:-2] + base[:-3])
    query = noise[:, 0] + nearby
    keyrows = noise[:, 1] + nearby
    values = noise[:, 2]
    stacked = jnp.stack([query, keyrows, values], axis=1)
    return jnp.clip(stacked, -80.0, 80.0).astype(jnp.bfloat16)


def draw_prefix_cache(key, part):
    keys = jax.random.split(jax.random.fold_in(key, 13), 1)
    cache = jax.random.normal(keys[0], (G, PRE, 2, HH), jnp.float32)
    return jnp.clip(cache, -80.0, 80.0).astype(jnp.bfloat16)


def choose_distinct(key, rows, amount, top, lift):
    ranking = jax.random.permutation(jax.random.fold_in(key, 1), amount)
    pull = ranking
    for power in range(3):
        pull = pull * pull // amount
    pull = pull * lift // amount
    tickets = jax.random.randint(jax.random.fold_in(key, 2), (rows, amount), 0, 4096) + pull
    holders = jax.random.permutation(jax.random.fold_in(key, 3), rows)[jnp.arange(amount) % rows]
    tickets = jnp.where(jnp.arange(rows)[:, None] == holders[None, :], 1 << 14, tickets)
    priority = tickets * amount + jnp.arange(amount)
    return lax.top_k(priority.astype(jnp.int32), top)[1].astype(jnp.int32)


def profile(count, total, most, skew):
    portions = [(1 << 20) // math.isqrt(standing ** skew) + 1 for standing in range(2, count + 1)]
    spare, holding = total - most - (count - 1), [1] * (count - 1)
    while spare > 0:
        free = [i for i in range(count - 1) if holding[i] < most]
        pool, left = sum([portions[i] for i in free]), spare
        for i in free:
            extra = min(most - holding[i], max(1, left * portions[i] // pool), spare)
            holding[i] = holding[i] + extra
            spare = spare - extra
    return np.array([most] + holding)


def uneven(own_key, number_of, total, reach, skew):
    if number_of == 2:
        one = jax.random.randint(own_key, (), max(1, total - reach), min(reach, total - 1) + 1)
        return jnp.stack([one, total - one])
    sizes = jnp.asarray(profile(number_of, total, reach, skew), jnp.int32)
    pairs = (number_of - 1) // 2
    giver, sink = sizes[1:1 + 2 * pairs:2], sizes[2:2 + 2 * pairs:2]
    room = jnp.minimum(giver - 1, reach - sink)
    shifted = jax.random.randint(jax.random.fold_in(own_key, 1), (pairs,), 0, 1 << 20) % (room + 1)
    sizes = sizes.at[1:1 + 2 * pairs:2].set(giver - shifted).at[2:2 + 2 * pairs:2].set(sink + shifted)
    return sizes[jax.random.permutation(jax.random.fold_in(own_key, 2), number_of)]


def setup_inputs(seed: int = 0) -> dict:
    key_of = jax.random.split(jax.random.key(seed), 6)
    return {
        "qkv": draw_qkv(jax.random.fold_in(key_of[5], 71), 0),
        "prefix_cache": draw_prefix_cache(jax.random.fold_in(key_of[5], 71), 0),
        "suffix_lengths": jax.vmap(lambda own: uneven(own, REQ, TOK_DEV, CAP, 2))(jax.random.split(key_of[2], N_TOK)).reshape((N_TOK, REQ)).astype(jnp.int32),
        "request_groups": choose_distinct(key_of[3], N_TOK, G, REQ, 8192),
        "prefix_owner": jax.random.permutation(key_of[4], G).astype(jnp.int32),
    }


def reference(qkv, prefix_cache, suffix_lengths, request_groups, prefix_owner):
    scale = 1.0 / math.sqrt(HD)
    blocks = qkv.reshape(N_TOK, TOK_DEV, 3, H, HD)

    def one_device(args):
        rows, lengths, groups = args
        ends = jnp.cumsum(lengths).astype(jnp.int32)
        starts = (ends - lengths).astype(jnp.int32)
        position = jnp.arange(TOK_DEV, dtype=jnp.int32)
        request = lax.optimization_barrier(jnp.sum((position[:, None] >= ends[None, :]).astype(jnp.int32), axis=1))
        query = rows[:, 0].astype(jnp.float32)
        keyrows = rows[:, 1].astype(jnp.float32)
        values = rows[:, 2]
        scores = jnp.einsum('thd,shd->hts', query, keyrows) * scale
        allowed = (request[:, None] == request[None, :]) & (position[None, :] <= position[:, None])
        scores = jnp.where(allowed[None], scores, -jnp.inf)
        peak_s = lax.optimization_barrier(jnp.max(scores, axis=2))
        weights = jnp.exp(scores - peak_s[:, :, None])
        total_s = lax.optimization_barrier(jnp.sum(weights, axis=2))
        mixed_s = jnp.einsum('hts,shd->thd', weights.astype(jnp.bfloat16).astype(jnp.float32), values.astype(jnp.float32))

        def one_request(index):
            slot = jnp.sum(jnp.where(jnp.arange(G, dtype=jnp.int32) == groups[index], prefix_owner, 0)).astype(jnp.int32)
            cache = lax.dynamic_index_in_dim(prefix_cache, slot, 0, keepdims=False)
            cache_keys = cache[:, 0].reshape(PRE, H, HD).astype(jnp.float32)
            cache_values = cache[:, 1].reshape(PRE, H, HD).astype(jnp.float32)
            picks = jnp.clip(starts[index] + jnp.arange(CAP, dtype=jnp.int32), 0, TOK_DEV - 1)
            chosen = query[picks]
            prefix_scores = jnp.einsum('chd,phd->hcp', chosen, cache_keys) * scale
            peak = lax.optimization_barrier(jnp.max(prefix_scores, axis=2))
            raised = jnp.exp(prefix_scores - peak[:, :, None])
            total = lax.optimization_barrier(jnp.sum(raised, axis=2))
            mixed = jnp.einsum('hcp,phd->chd', raised.astype(jnp.bfloat16).astype(jnp.float32), cache_values)
            mixed = mixed / jnp.transpose(total)[:, :, None]
            return (mixed, jnp.transpose(peak), jnp.transpose(total))
        mixed_p, peak_p, total_p = lax.map(one_request, jnp.arange(REQ, dtype=jnp.int32))
        offset = position - starts[request]
        o_tok = mixed_p[request, offset]
        m_tok = peak_p[request, offset]
        l_tok = total_p[request, offset]
        m_s = jnp.transpose(peak_s)
        l_s = jnp.transpose(total_s)
        top = jnp.maximum(m_tok, m_s)
        first = l_tok * jnp.exp(m_tok - top)
        second = jnp.exp(m_s - top)
        merged = (first[:, :, None] * o_tok + second[:, :, None] * mixed_s) / (first + second * l_s)[:, :, None]
        return merged.reshape(TOK_DEV, HH).astype(jnp.bfloat16)
    attended = lax.map(one_device, (blocks, suffix_lengths, request_groups))
    attended = attended.reshape(TOKENS, HH)
    suffix_cache = qkv[:, 1:3]
    return (attended, suffix_cache)
```

```python
import functools
import math

import jax
import jax.numpy as jnp
from jax import lax
from jax.experimental import pallas as pl
from jax.experimental.pallas import tpu as pltpu
from jax.sharding import PartitionSpec as P

HD = 224
LANES = 128
BAND = math.lcm(HD, LANES)
PER = BAND // HD
LSPLIT = 16
PIECE = 2 * LSPLIT


def window(j):
    low = j * HD // LANES * LANES
    high = -(-(j + 1) * HD // LANES) * LANES
    return low, high


def owners_of(tile):
    first = tile * LANES // HD
    last = ((tile + 1) * LANES - 1) // HD
    return first, last


def lane_iota(shape):
    return lax.broadcasted_iota(jnp.int32, shape, len(shape) - 1)


def by_tile(tile, pick):
    first, last = owners_of(tile)
    left = pick(first)
    if first == last:
        return left
    right = pick(last)
    edge = last * HD - tile * LANES
    return jnp.where(lane_iota((right.shape[0], LANES)) < edge, left, right)


def masked_query(query, j):
    low, high = window(j)
    cols = lane_iota((query.shape[0], high - low)) + low
    keep = (cols >= j * HD) & (cols < (j + 1) * HD)
    return jnp.where(keep, query[:, low:high], jnp.zeros((), query.dtype))


def dot_nt(a, b):
    return lax.dot_general(a, b, (((1,), (1,)), ((), ())), preferred_element_type=jnp.float32)


def dot_nn(a, b):
    return lax.dot_general(a, b, (((1,), (0,)), ((), ())), preferred_element_type=jnp.float32)


def spread_kernel(target_ref, query_ref, out_ref):
    rows = out_ref.shape[0]
    toks = target_ref.shape[1]
    place = lax.broadcasted_iota(jnp.int32, (rows, toks), 0)
    pick = jnp.where(place == target_ref[...], 1.0, 0.0).astype(jnp.bfloat16)
    out_ref[...] = dot_nn(pick, query_ref[...]).astype(jnp.bfloat16)


def attend(query, keys, values, allowed, scale, normalise, put, stats_ref, band=None):
    band = pl.program_id(0) if band is None else band
    rows = query.shape[0]
    lanes = lane_iota((rows, LANES))

    if isinstance(band, int):
        stats = jnp.zeros_like(stats_ref) if band == 0 else stats_ref[...]
    else:

        @pl.when(band == 0)
        def _():
            stats_ref[...] = jnp.zeros_like(stats_ref)

        stats = stats_ref[...]
    mixed = []
    for j in range(PER):
        low, high = window(j)
        scores = dot_nt(masked_query(query, j), keys[:, low:high]) * scale
        if allowed is not None:
            scores = jnp.where(allowed, scores, -jnp.inf)
        peak = jnp.max(scores, axis=1, keepdims=True)
        raised = jnp.exp(scores - peak)
        total = jnp.sum(raised, axis=1, keepdims=True)
        out = dot_nn(raised.astype(jnp.bfloat16), values[:, low:high])
        if normalise:
            out = out / total
        mixed.append(out)
        head = band * PER + j
        stats = jnp.where(lanes == head, peak, stats)
        stats = jnp.where(lanes == head + LSPLIT, total, stats)
    stats_ref[...] = stats
    for tile in range(BAND // LANES):
        put(tile, by_tile(tile, lambda j: mixed[j][:, tile * LANES - window(j)[0]:][:, :LANES]))


def prefix_kernel(scale, query_ref, key_ref, value_ref, out_ref, stats_ref):
    band = pl.program_id(0)
    bands = pl.num_programs(0)
    width = out_ref.shape[1] - LANES

    def put(tile, cols):
        at = pl.multiple_of(band * BAND + tile * LANES, LANES)
        out_ref[:, pl.ds(at, LANES)] = cols.astype(out_ref.dtype)

    attend(query_ref[...], key_ref[...], value_ref[...], None, scale, True, put, stats_ref)

    @pl.when(band == bands - 1)
    def _():
        full = stats_ref[...]
        high = full.astype(jnp.bfloat16).astype(jnp.float32)
        rest = full - high
        mid = rest.astype(jnp.bfloat16).astype(jnp.float32)
        low = rest - mid
        packed = high + pltpu.roll(mid, PIECE, 1) + pltpu.roll(low, 2 * PIECE, 1)
        out_ref[:, width:] = packed.astype(out_ref.dtype)


def suffix_kernel(scale, reqc_ref, reqr_ref, query_ref, key_ref, value_ref, out_ref, stats_ref):
    toks = query_ref.shape[0]
    shape = (toks, toks)
    allowed = (reqc_ref[...] == reqr_ref[...]) & (
        lax.broadcasted_iota(jnp.int32, shape, 1) <= lax.broadcasted_iota(jnp.int32, shape, 0)
    )

    def put(tile, cols):
        out_ref[:, tile * LANES:(tile + 1) * LANES] = cols

    keys = key_ref[...].reshape(toks, BAND)
    values = value_ref[...].reshape(toks, BAND)
    attend(query_ref[...], keys, values, allowed, scale, False, put, stats_ref)


def merge_kernel(target_ref, back_ref, pstats_ref, mixed_ref, sstats_ref, out_ref):
    band = pl.program_id(0)
    rows = back_ref.shape[0]
    toks = target_ref.shape[0]
    place = lane_iota((toks, rows))
    pick = jnp.where(place == target_ref[...], 1.0, 0.0).astype(jnp.bfloat16)
    packed = dot_nn(pick, pstats_ref[...])
    prefix = (packed + pltpu.roll(packed, LANES - PIECE, 1)) + pltpu.roll(
        packed, LANES - 2 * PIECE, 1
    )
    suffix = sstats_ref[...]
    top = jnp.maximum(prefix, suffix)
    first = pltpu.roll(prefix, LANES - LSPLIT, 1) * jnp.exp(prefix - top)
    second = jnp.exp(suffix - top)
    below = first + second * pltpu.roll(suffix, LANES - LSPLIT, 1)
    wp = first / below
    ws = second / below
    lanes = lane_iota((toks, LANES))

    def column(weights, j):
        return jnp.sum(jnp.where(lanes == band * PER + j, weights, 0.0), axis=1, keepdims=True)

    cp = [column(wp, j) for j in range(PER)]
    cs = [column(ws, j) for j in range(PER)]
    for tile in range(BAND // LANES):
        cols = slice(tile * LANES, (tile + 1) * LANES)
        back = dot_nn(pick, back_ref[:, cols])
        merged = by_tile(tile, lambda j: cp[j]) * back + by_tile(tile, lambda j: cs[j]) * mixed_ref[:, cols]
        out_ref[:, cols] = merged.astype(out_ref.dtype)


def whole_block(array):
    return pl.BlockSpec(array.shape, lambda g: (0,) * array.ndim)


def band_block(rows, off=0):
    return pl.BlockSpec((rows, BAND), lambda g: (0, g + off))


def cost(flops, moved):
    return pl.CostEstimate(flops=flops, bytes_accessed=moved, transcendentals=0)


def room():
    return pltpu.CompilerParams(vmem_limit_bytes=48 * 1024 * 1024)


def exchange(x, axis):
    return lax.all_to_all(x, axis, split_axis=0, concat_axis=0, tiled=True)


def shift_exchange(x, axis):
    n = lax.axis_size(axis)
    me = lax.axis_index(axis)
    parts = [lax.dynamic_index_in_dim(x, me, 0, keepdims=False)]
    for d in range(1, n):
        ring = [(i, (i + d) % n) for i in range(n)]
        sent = lax.dynamic_index_in_dim(x, lax.rem(me + d, n), 0, keepdims=False)
        parts.append(lax.ppermute(sent, axis, ring))
    out = []
    for source in range(n):
        picked = parts[0]
        for d in range(1, n):
            picked = jnp.where(lax.rem(me + n - source, n) == d, parts[d], picked)
        out.append(picked)
    return jnp.stack(out)


def generic_device(qkv, prefix_cache, suffix_lengths, request_groups, prefix_owner):
    n_head = lax.axis_size("head")
    n_tok = lax.axis_size("tok")
    here = qkv.shape[0]
    width = qkv.shape[2] // n_head
    toks = here * n_head
    scale = 1.0 / math.sqrt(HD)
    bands = width // BAND
    parts = 1
    each = bands // parts
    cols = each * BAND
    capacity = 3 * toks // n_tok
    rows = n_tok * capacity
    planes = jnp.transpose(qkv, (1, 0, 2)).reshape(3, here, n_head, width)
    queries = [
        exchange(
            jnp.stack([qkv[:, 0, h * width:(h + 1) * width] for h in range(n_head)]), "head"
        ).reshape(toks, cols)
        for p in range(parts)
    ]
    kv_send = jnp.transpose(planes[1:], (2, 0, 1, 3))

    lengths = suffix_lengths[0]
    groups = request_groups[0]
    requests = lengths.shape[0]
    ends = jnp.sum(jnp.where(jnp.arange(requests)[:, None] <= jnp.arange(requests)[None, :], lengths[:, None], 0), axis=0)
    starts = ends - lengths
    slots = jnp.sum(jnp.where(groups[:, None] == jnp.arange(n_tok)[None, :], prefix_owner[None, :], 0), axis=1)
    position = jnp.arange(toks, dtype=jnp.int32)
    request = jnp.sum((position[:, None] >= ends[None, :]).astype(jnp.int32), axis=1)
    base = slots * capacity - starts
    inside = request[:, None] == jnp.arange(requests, dtype=jnp.int32)[None, :]
    target = (position + jnp.sum(jnp.where(inside, base[None, :], 0), axis=1)).astype(jnp.int32)
    target_row = target[None, :]
    target_col = target[:, None]
    reqc, reqr = request[:, None], request[None, :]

    prefix_len = prefix_cache.shape[1]
    queries[0], cache_keys, cache_values = lax.optimization_barrier(
        (queries[0], prefix_cache[0, :, 0], prefix_cache[0, :, 1])
    )
    received = []
    for p in range(parts):
        outgoing = pl.pallas_call(
            spread_kernel,
            grid=(each,),
            out_shape=jax.ShapeDtypeStruct((rows, cols), jnp.bfloat16),
            in_specs=[whole_block(target_row), band_block(toks)],
            out_specs=band_block(rows),
            cost_estimate=cost(2 * rows * toks * cols, 2 * (rows + toks) * cols),
            compiler_params=room(),
            name="spread",
        )(target_row, queries[p])
        if p == 0:
            outgoing, kv_send = lax.optimization_barrier((outgoing, kv_send))
        received.append(exchange(outgoing.reshape(n_tok, capacity, cols), "tok").reshape(rows, cols))
    kv = shift_exchange(kv_send, "head")

    back = []
    for p in range(parts):
        mixed = pl.pallas_call(
            functools.partial(prefix_kernel, scale),
            grid=(each,),
            out_shape=jax.ShapeDtypeStruct((rows, cols + LANES), jnp.bfloat16),
            in_specs=[band_block(rows), band_block(prefix_len, p * each), band_block(prefix_len, p * each)],
            out_specs=pl.BlockSpec((rows, cols + LANES), lambda g: (0, 0)),
            scratch_shapes=[pltpu.VMEM((rows, LANES), jnp.float32)],
            cost_estimate=cost(4 * rows * prefix_len * cols, 4 * (rows + prefix_len) * cols),
            compiler_params=room(),
            name="prefix",
        )(received[p], cache_keys, cache_values)
        back.append(exchange(mixed.reshape(n_tok, capacity, cols + LANES), "tok").reshape(rows, cols + LANES))

    finals = []
    for p in range(parts):
        key_spec = pl.BlockSpec((n_head, None, here, BAND), lambda g, p=p: (0, 0, 0, g + p * each))
        value_spec = pl.BlockSpec((n_head, None, here, BAND), lambda g, p=p: (0, 1, 0, g + p * each))
        mixed_s, stats_s = pl.pallas_call(
            functools.partial(suffix_kernel, scale),
            grid=(each,),
            out_shape=[
                jax.ShapeDtypeStruct((toks, cols), jnp.float32),
                jax.ShapeDtypeStruct((toks, LANES), jnp.float32),
            ],
            in_specs=[whole_block(reqc), whole_block(reqr), band_block(toks), key_spec, value_spec],
            out_specs=[band_block(toks), pl.BlockSpec((toks, LANES), lambda g: (0, 0))],
            cost_estimate=cost(4 * toks * toks * cols, 10 * toks * cols),
            compiler_params=room(),
            name="suffix",
        )(reqc, reqr, queries[p], kv, kv)
        merged = pl.pallas_call(
            merge_kernel,
            grid=(each,),
            out_shape=jax.ShapeDtypeStruct((toks, cols), jnp.bfloat16),
            in_specs=[
                whole_block(target_col),
                band_block(rows),
                pl.BlockSpec((rows, LANES), lambda g: (0, cols // LANES)),
                band_block(toks),
                whole_block(stats_s),
            ],
            out_specs=band_block(toks),
            cost_estimate=cost(2 * rows * toks * cols, 2 * (rows + 3 * toks) * cols),
            compiler_params=room(),
            name="merge",
        )(target_col, back[p], back[p], mixed_s, stats_s)
        finals.append(exchange(merged.reshape(n_head, here, cols), "head"))
    attended = jnp.transpose(jnp.stack(finals, axis=2), (1, 0, 2, 3)).reshape(here, n_head * width)
    suffix_cache = jnp.transpose(kv, (0, 2, 1, 3)).reshape(toks, 2, width)
    return (attended, suffix_cache)


TEAM = 4
FEATURES = 7168
CODE = 1024
CAPS = (208, 256, 384)
FIRST = 512
MIDDLE = 384
STAT = 8
MESH = pl.DeviceIdType.MESH


def place():
    tok = lax.axis_index("tok")
    half = lax.axis_index("head")
    return lax.div(tok, TEAM), lax.rem(tok, TEAM), half


def team_at(member, level):
    return {"tok": level * TEAM + lax.rem(member, TEAM), "head": lax.div(member, TEAM)}


def team_rows(member, rows):
    at = (lax.rem(member, TEAM) * 2 + lax.div(member, TEAM)) * rows
    return pl.ds(pl.multiple_of(at, 16), rows)


def band_cols(member, low=0, wide=BAND):
    return pl.ds(pl.multiple_of(member * BAND + low, LANES), wide)


def gather_kernel(
    qkv_ref, meta_ref, owner_ref, cache_ref, pool_ref, kv_ref, slot_ref, code_ref, req_ref, peak_ref,
    table, cache, sm, rm, sq, rq, sl,
):
    level, work, half = place()
    tok = level * TEAM + work
    team = 2 * TEAM
    mine = half * TEAM + work
    n = lax.axis_size("tok")
    rows = qkv_ref.shape[1]

    def meta_copy(d, landing):
        return pltpu.make_async_remote_copy(
            src_ref=meta_ref,
            dst_ref=table.at[landing],
            send_sem=sm.at[d],
            recv_sem=rm.at[d],
            device_id={"tok": lax.rem(tok + d, n), "head": half},
            device_id_type=MESH,
        )

    def query_copy(e, landing):
        peer = lax.rem(mine + e, team)
        return pltpu.make_async_remote_copy(
            src_ref=qkv_ref.at[0, :, band_cols(peer)],
            dst_ref=pool_ref.at[team_rows(landing, rows), :],
            send_sem=sq.at[e],
            recv_sem=rq.at[e],
            device_id=team_at(peer, level),
            device_id_type=MESH,
        )

    barrier = pltpu.get_barrier_semaphore()
    for d in range(1, n):
        pl.semaphore_signal(
            barrier, inc=1, device_id={"tok": lax.rem(tok + d, n), "head": half}, device_id_type=MESH
        )
    for w in range(TEAM):
        pl.semaphore_signal(
            barrier, inc=1, device_id={"tok": level * TEAM + w, "head": 1 - half}, device_id_type=MESH
        )
    bring = pltpu.make_async_copy(cache_ref, cache, sl.at[0])
    bring.start()
    own = pltpu.make_async_copy(
        qkv_ref.at[0, :, band_cols(mine)], pool_ref.at[team_rows(mine, rows), :], sl.at[1]
    )
    own.start()
    pl.semaphore_wait(barrier, n - 1 + TEAM)
    for d in range(1, n):
        meta_copy(d, tok).start()
    for e in range(1, team):
        query_copy(e, mine).start()
    table[tok] = meta_ref[...]
    bring.wait()
    width = kv_ref.shape[2]

    def split(c, carry):
        cols = pl.ds(pl.multiple_of(c * LANES, LANES), LANES)
        kv_ref[0, :, cols] = cache[:, 0, cols]
        kv_ref[1, :, cols] = cache[:, 1, cols]
        return carry

    lax.fori_loop(0, width // LANES, split, 0)
    for d in range(1, n):
        meta_copy(d, lax.rem(tok + n - d, n)).wait_recv()

    lengths = table[:, 0, :]
    groups = table[:, 1, :]
    slots = jnp.zeros_like(groups)
    for g in range(owner_ref.shape[0]):
        slots = jnp.where(groups == g, owner_ref[g], slots)
    spot = lane_iota((n, LANES))
    slot = jnp.zeros((n, LANES), jnp.int32)
    request = jnp.zeros((n, LANES), jnp.int32)
    end = jnp.zeros((n, 1), jnp.int32)
    for r in range(REQUESTS):
        start = end
        end = start + lengths[:, r:r + 1]
        inside = (spot >= start) & (spot < end)
        slot = jnp.where(inside, slots[:, r:r + 1], slot)
        request = jnp.where(inside, r, request)
    goal = lax.div(slot, TEAM)
    marks = [jnp.where(goal == z, 1.0, 0.0) for z in range(TEAM)]
    hot = jnp.concatenate(marks, axis=0).astype(jnp.bfloat16)
    down = lax.broadcasted_iota(jnp.int32, (LANES, LANES), 0)
    upto = jnp.where(down <= lane_iota((LANES, LANES)), 1.0, 0.0).astype(jnp.bfloat16)
    running = dot_nn(hot, upto)
    totals = dot_nn(hot, jnp.ones((LANES, LANES), jnp.bfloat16))
    m = TEAM * n
    a = lax.broadcasted_iota(jnp.int32, (m, m), 0)
    b = lax.broadcasted_iota(jnp.int32, (m, m), 1)
    earlier = (lax.div(a, TEAM) == lax.div(b, TEAM)) & (b < a)
    before = dot_nn(jnp.where(earlier, 1.0, 0.0).astype(jnp.bfloat16), totals.astype(jnp.bfloat16))
    count = (running + before).astype(jnp.int32)
    code = jnp.zeros((n, LANES), jnp.int32)
    for z in range(TEAM):
        code = jnp.where(goal == z, z * CODE + count[z * n:(z + 1) * n] - 1, code)
    slot = slot - goal * TEAM
    for z in range(TEAM):
        part = slice(z * TEAM, (z + 1) * TEAM)
        slot_ref[z] = slot[part]
        code_ref[z] = code[part]
        req_ref[z] = request[part]
    most = jnp.max(jnp.max(count, axis=0, keepdims=True), axis=1, keepdims=True)
    peak_ref[...] = jnp.broadcast_to(most, peak_ref.shape)

    own.wait()
    for e in range(1, team):
        query_copy(e, lax.rem(mine + team - e, team)).wait_recv()
    for d in range(1, n):
        meta_copy(d, tok).wait_send()
    for e in range(1, team):
        query_copy(e, mine).wait_send()


def pool_kernel(
    scale, cap, pool_ref, slot_ref, code_ref, req_ref, qkv_ref, kv_ref, out_ref,
    outgo, income, result, back, stats, cols, keep, fresh, final,
    s1, r1, s2, r2, s3, r3, s4, r4, s5, r5, sl,
):
    level, work, half = place()
    team = 2 * TEAM
    mine = half * TEAM + work
    rows = qkv_ref.shape[1]
    toks = 2 * rows

    def level_id(d):
        return {"tok": lax.rem(level + d, TEAM) * TEAM + work, "head": half}

    def forth_copy(d):
        return pltpu.make_async_remote_copy(
            src_ref=outgo.at[d], dst_ref=income.at[d], send_sem=s1.at[d], recv_sem=r1.at[d],
            device_id=level_id(d), device_id_type=MESH,
        )

    def back_copy(d, part):
        span = slice(0, MIDDLE) if part == 0 else slice(MIDDLE, BAND + LANES)
        return pltpu.make_async_remote_copy(
            src_ref=result.at[d, :, span], dst_ref=back.at[d, :, span],
            send_sem=s2.at[part, d], recv_sem=r2.at[part, d],
            device_id=level_id(TEAM - d), device_id_type=MESH,
        )

    def cache_copy(e, part, landing):
        peer = lax.rem(work + e, TEAM)
        low, high = (0, FIRST) if part == 0 else (FIRST, BAND)
        return pltpu.make_async_remote_copy(
            src_ref=kv_ref.at[:, :, band_cols(peer, low, high - low)],
            dst_ref=keep.at[landing, :, :, low:high],
            send_sem=s3.at[part, e], recv_sem=r3.at[part, e],
            device_id={"tok": level * TEAM + peer, "head": half}, device_id_type=MESH,
        )

    def fresh_copy(e, landing):
        peer = lax.rem(mine + e, team)
        return pltpu.make_async_remote_copy(
            src_ref=qkv_ref.at[1:3, :, band_cols(peer)],
            dst_ref=fresh.at[:, team_rows(landing, rows), :],
            send_sem=s4.at[e], recv_sem=r4.at[e],
            device_id=team_at(peer, level), device_id_type=MESH,
        )

    def final_copy(e, landing):
        peer = lax.rem(mine + e, team)
        return pltpu.make_async_remote_copy(
            src_ref=final.at[team_rows(peer, rows), :],
            dst_ref=out_ref.at[:, band_cols(landing)],
            send_sem=s5.at[e], recv_sem=r5.at[e],
            device_id=team_at(peer, level), device_id_type=MESH,
        )

    barrier = pltpu.get_barrier_semaphore()
    for e in range(1, team):
        pl.semaphore_signal(barrier, inc=1, device_id=team_at(lax.rem(mine + e, team), level), device_id_type=MESH)
    for d in range(1, TEAM):
        pl.semaphore_signal(barrier, inc=1, device_id=level_id(d), device_id_type=MESH)
    own_cache = pltpu.make_async_copy(kv_ref.at[:, :, band_cols(work)], keep.at[work], sl.at[0])
    own_cache.start()
    own_fresh = pltpu.make_async_copy(
        qkv_ref.at[1:3, :, band_cols(mine)], fresh.at[:, team_rows(mine, rows), :], sl.at[1]
    )
    own_fresh.start()
    pl.semaphore_wait(barrier, team - 1 + TEAM - 1)
    for part in range(2):
        for e in range(1, TEAM):
            cache_copy(e, part, work).start()

    def flat(ref, z):
        block = ref[z]
        return jnp.concatenate([block[i:i + 1] for i in range(TEAM)], axis=1)

    down = lax.broadcasted_iota(jnp.int32, (cap, TEAM * toks), 0)
    code = flat(code_ref, level)

    def send(d):
        goal = lax.rem(level + d, TEAM)
        pick = jnp.where(down == code - goal * CODE, 1.0, 0.0).astype(jnp.bfloat16)
        packed = dot_nn(pick, pool_ref[...]).astype(jnp.bfloat16)
        if d:
            outgo[d] = packed
            forth_copy(d).start()
        else:
            income[0] = packed

    for d in (2, 3, 1, 0):
        send(d)
    for d in range(TEAM):
        origin = lax.rem(level + TEAM - d, TEAM)
        hit = down == flat(code_ref, origin) - level * CODE
        local = flat(slot_ref, origin).astype(jnp.float32)
        found = jnp.sum(jnp.where(hit, local, 0.0), axis=1, keepdims=True)
        cols[d] = jnp.broadcast_to(found, (cap, LANES))
    stats[...] = jnp.zeros_like(stats)
    own_cache.wait()

    def prefix(part):
        heads = range(2) if part == 0 else range(2, PER)

        def run(d, carry):
            which = cols[d][:, :1]
            query = income[d]
            lanes = lane_iota((cap, LANES))
            noted = stats[d]
            mixed = {}
            for j in heads:
                low, high = window(j)
                asked = masked_query(query, j)
                scores = None
                for s in range(TEAM):
                    part_scores = dot_nt(asked, keep[s, 0, :, low:high])
                    scores = part_scores if s == 0 else jnp.where(which == s, part_scores, scores)
                scores = scores * scale
                top = jnp.max(scores, axis=1, keepdims=True)
                raised = jnp.exp(scores - top)
                total = jnp.sum(raised, axis=1, keepdims=True)
                out = None
                for s in range(TEAM):
                    weights = jnp.where(which == s, raised, 0.0).astype(jnp.bfloat16)
                    term = dot_nn(weights, keep[s, 1, :, low:high])
                    out = term if s == 0 else out + term
                mixed[j] = out / total
                noted = jnp.where(lanes == j, top, noted)
                noted = jnp.where(lanes == PER + j, total, noted)

            def cut(j, tile):
                return mixed[j][:, tile * LANES - window(j)[0]:][:, :LANES]

            tiles = range(4) if part == 0 else range(3, BAND // LANES)
            for tile in tiles:
                first, last = owners_of(tile)
                span = slice(tile * LANES, (tile + 1) * LANES)
                if tile != 3:
                    values = by_tile(tile, lambda j: cut(j, tile)).astype(jnp.bfloat16)
                elif part == 0:
                    values = cut(first, tile).astype(jnp.bfloat16)
                else:
                    edge = last * HD - tile * LANES
                    values = jnp.where(
                        lanes < edge, result[d, :, span].astype(jnp.float32), cut(last, tile)
                    ).astype(jnp.bfloat16)
                result[d, :, span] = values
            stats[d] = noted
            if part == 1:
                high = noted.astype(jnp.bfloat16).astype(jnp.float32)
                rest = noted - high
                mid = rest.astype(jnp.bfloat16).astype(jnp.float32)
                packed = high + pltpu.roll(mid, STAT, 1) + pltpu.roll(rest - mid, 2 * STAT, 1)
                result[d, :, BAND:] = packed.astype(jnp.bfloat16)
            return carry

        lax.fori_loop(0, TEAM, run, 0)

    for d in range(1, TEAM):
        forth_copy(d).wait_recv()
    for part in range(2):
        for e in range(1, TEAM):
            cache_copy(e, part, lax.rem(work + TEAM - e, TEAM)).wait_recv()
        if part == 1:
            for e in range(1, team):
                fresh_copy(e, mine).start()
        prefix(part)
        for d in (2, 3, 1):
            back_copy(d, part).start()
    back[0] = result[0]
    own_fresh.wait()
    for e in range(1, team):
        fresh_copy(e, lax.rem(mine + team - e, team)).wait_recv()
    for part in range(2):
        for d in range(1, TEAM):
            back_copy(d, part).wait_recv()

    eye = lax.broadcasted_iota(jnp.int32, (toks, toks), 0) == lax.broadcasted_iota(jnp.int32, (toks, toks), 1)
    causal = lax.broadcasted_iota(jnp.int32, (toks, toks), 1) <= lax.broadcasted_iota(jnp.int32, (toks, toks), 0)

    def column(row):
        return jnp.sum(jnp.where(eye, row, 0.0), axis=1, keepdims=True)

    def finish(i, carry):
        span = pl.ds(pl.multiple_of(i * toks, toks), toks)
        codes = code_ref[level, pl.ds(i, 1), :]
        goal = lax.div(codes, CODE)
        seat = lax.rem(goal - level + TEAM, TEAM) * cap + (codes - goal * CODE)
        seat = column(seat.astype(jnp.float32)).astype(jnp.int32)
        pick = jnp.where(lane_iota((toks, TEAM * cap)) == seat, 1.0, 0.0).astype(jnp.bfloat16)
        ready = dot_nn(pick, back[...].reshape(TEAM * cap, BAND + LANES))
        packed = ready[:, BAND:]
        prior = (packed + pltpu.roll(packed, LANES - STAT, 1)) + pltpu.roll(packed, LANES - 2 * STAT, 1)
        asks = req_ref[level, pl.ds(i, 1), :].astype(jnp.float32)
        allowed = (column(asks) == asks) & causal
        query = pool_ref[span, :]
        merged = []
        for j in range(PER):
            low, high = window(j)
            scores = dot_nt(masked_query(query, j), fresh[0, span, low:high]) * scale
            scores = jnp.where(allowed, scores, -jnp.inf)
            peak = jnp.max(scores, axis=1, keepdims=True)
            raised = jnp.exp(scores - peak)
            total = jnp.sum(raised, axis=1, keepdims=True)
            out = dot_nn(raised.astype(jnp.bfloat16), fresh[1, span, low:high])
            ppeak = prior[:, j:j + 1]
            ptotal = prior[:, PER + j:PER + j + 1]
            top = jnp.maximum(ppeak, peak)
            first = ptotal * jnp.exp(ppeak - top)
            second = jnp.exp(peak - top)
            below = first + second * total
            merged.append((first / below) * ready[:, low:high] + (second / below) * out)
        for tile in range(BAND // LANES):
            values = by_tile(tile, lambda j: merged[j][:, tile * LANES - window(j)[0]:][:, :LANES])
            final[span, tile * LANES:(tile + 1) * LANES] = values.astype(jnp.bfloat16)
        return carry

    lax.fori_loop(0, TEAM, finish, 0)
    for e in range(1, team):
        final_copy(e, mine).start()
    out_ref[:, band_cols(mine)] = final[team_rows(mine, rows), :]
    for e in range(1, team):
        final_copy(e, lax.rem(mine + team - e, team)).wait_recv()
    for d in range(1, TEAM):
        forth_copy(d).wait_send()
        for part in range(2):
            back_copy(d, part).wait_send()
    for e in range(1, TEAM):
        for part in range(2):
            cache_copy(e, part, work).wait_send()
    for e in range(1, team):
        fresh_copy(e, mine).wait_send()
        final_copy(e, mine).wait_send()


REQUESTS = 8


def pooled_device(qkv, prefix_cache, suffix_lengths, request_groups, prefix_owner):
    n_head = lax.axis_size("head")
    n_tok = lax.axis_size("tok")
    here = qkv.shape[0]
    width = qkv.shape[2] // n_head
    toks = here * n_head
    scale = 1.0 / math.sqrt(HD)
    past = prefix_cache.shape[1]
    planes = jnp.transpose(qkv, (1, 0, 2))
    meta = jnp.pad(jnp.concatenate([suffix_lengths, request_groups], 0), ((0, 6), (0, LANES - suffix_lengths.shape[1])))
    vmem = pl.BlockSpec(memory_space=pltpu.VMEM)
    smem = pl.BlockSpec(memory_space=pltpu.SMEM)
    hbm = pl.BlockSpec(memory_space=pl.ANY)
    dma = pltpu.SemaphoreType.DMA
    table = jax.ShapeDtypeStruct((TEAM, TEAM, LANES), jnp.int32)

    pool, kv, slot, code, request, peak = pl.pallas_call(
        gather_kernel,
        out_shape=[
            jax.ShapeDtypeStruct((TEAM * toks, BAND), jnp.bfloat16),
            jax.ShapeDtypeStruct((2, past, width), jnp.bfloat16),
            table, table, table,
            jax.ShapeDtypeStruct((8, LANES), jnp.int32),
        ],
        in_specs=[hbm, vmem, smem, hbm],
        out_specs=[vmem] * 6,
        scratch_shapes=[
            pltpu.VMEM((n_tok, 8, LANES), jnp.int32),
            pltpu.VMEM((past, 2, width), jnp.bfloat16),
            dma((n_tok,)), dma((n_tok,)), dma((2 * TEAM,)), dma((2 * TEAM,)), dma((2,)),
        ],
        compiler_params=pltpu.CompilerParams(
            collective_id=0, has_side_effects=True, vmem_limit_bytes=48 * 1024 * 1024
        ),
        name="gather",
    )(planes, meta, prefix_owner, prefix_cache[0])

    def pooled(cap, number):
        def call(pool, slot, code, request, planes, kv):
            return pl.pallas_call(
                functools.partial(pool_kernel, scale, cap),
                out_shape=jax.ShapeDtypeStruct((here, n_head * width), jnp.bfloat16),
                in_specs=[vmem, vmem, vmem, vmem, hbm, hbm],
                out_specs=vmem,
                scratch_shapes=[
                    pltpu.VMEM((TEAM, cap, BAND), jnp.bfloat16),
                    pltpu.VMEM((TEAM, cap, BAND), jnp.bfloat16),
                    pltpu.VMEM((TEAM, cap, BAND + LANES), jnp.bfloat16),
                    pltpu.VMEM((TEAM, cap, BAND + LANES), jnp.bfloat16),
                    pltpu.VMEM((TEAM, cap, LANES), jnp.float32),
                    pltpu.VMEM((TEAM, cap, LANES), jnp.float32),
                    pltpu.VMEM((TEAM, 2, past, BAND), jnp.bfloat16),
                    pltpu.VMEM((2, TEAM * toks, BAND), jnp.bfloat16),
                    pltpu.VMEM((TEAM * toks, BAND), jnp.bfloat16),
                    dma((TEAM,)), dma((TEAM,)), dma((2, TEAM)), dma((2, TEAM)),
                    dma((2, TEAM)), dma((2, TEAM)), dma((2 * TEAM,)), dma((2 * TEAM,)),
                    dma((2 * TEAM,)), dma((2 * TEAM,)), dma((2,)),
                ],
                compiler_params=pltpu.CompilerParams(
                    collective_id=number, has_side_effects=True, vmem_limit_bytes=52 * 1024 * 1024
                ),
                name="pooled",
            )(pool, slot, code, request, planes, kv)

        return call

    most = peak[0, 0]
    index = sum((most > cap).astype(jnp.int32) for cap in CAPS[:-1])
    attended = lax.switch(
        index, [pooled(cap, 1 + i) for i, cap in enumerate(CAPS)], pool, slot, code, request, planes, kv
    )

    split = planes[1:].reshape(2, here, n_head, width)
    swapped = shift_exchange(jnp.transpose(split, (2, 0, 1, 3)), "head")
    suffix_cache = jnp.transpose(swapped, (0, 2, 1, 3)).reshape(toks, 2, width)
    return (attended, suffix_cache)


def solution(mesh):
    in_specs = (
        P(("tok", "head"), None, None),
        P("tok", None, None, "head"),
        P("tok", None),
        P("tok", None),
        P(),
    )
    out_specs = (P(("tok", "head"), None), P("tok", None, "head"))
    pooled = mesh.shape["tok"] == TEAM * TEAM and BAND * TEAM * mesh.shape["head"] == FEATURES
    body = pooled_device if pooled else generic_device
    return jax.shard_map(
        body, mesh=mesh, in_specs=in_specs, out_specs=out_specs, check_vma=False
    )
```

```python
import functools
import math

import jax
import jax.numpy as jnp
from jax import lax
from jax.experimental import pallas as pl
from jax.experimental.pallas import tpu as pltpu
from jax.sharding import PartitionSpec as P

HD = 224
LANES = 128
BAND = math.lcm(HD, LANES)
PER = BAND // HD
LSPLIT = 16
PIECE = 2 * LSPLIT


def window(j):
    low = j * HD // LANES * LANES
    high = -(-(j + 1) * HD // LANES) * LANES
    return low, high


def owners_of(tile):
    first = tile * LANES // HD
    last = ((tile + 1) * LANES - 1) // HD
    return first, last


def lane_iota(shape):
    return lax.broadcasted_iota(jnp.int32, shape, len(shape) - 1)


def by_tile(tile, pick):
    first, last = owners_of(tile)
    left = pick(first)
    if first == last:
        return left
    right = pick(last)
    edge = last * HD - tile * LANES
    return jnp.where(lane_iota((right.shape[0], LANES)) < edge, left, right)


def masked_query(query, j):
    low, high = window(j)
    cols = lane_iota((query.shape[0], high - low)) + low
    keep = (cols >= j * HD) & (cols < (j + 1) * HD)
    return jnp.where(keep, query[:, low:high], jnp.zeros((), query.dtype))


def dot_nt(a, b):
    return lax.dot_general(a, b, (((1,), (1,)), ((), ())), preferred_element_type=jnp.float32)


def dot_nn(a, b):
    return lax.dot_general(a, b, (((1,), (0,)), ((), ())), preferred_element_type=jnp.float32)


def spread_kernel(target_ref, query_ref, out_ref):
    rows = out_ref.shape[0]
    toks = target_ref.shape[1]
    place = lax.broadcasted_iota(jnp.int32, (rows, toks), 0)
    pick = jnp.where(place == target_ref[...], 1.0, 0.0).astype(jnp.bfloat16)
    out_ref[...] = dot_nn(pick, query_ref[...]).astype(jnp.bfloat16)


def attend(query, keys, values, allowed, scale, normalise, put, stats_ref, band=None):
    band = pl.program_id(0) if band is None else band
    rows = query.shape[0]
    lanes = lane_iota((rows, LANES))

    if isinstance(band, int):
        stats = jnp.zeros_like(stats_ref) if band == 0 else stats_ref[...]
    else:

        @pl.when(band == 0)
        def _():
            stats_ref[...] = jnp.zeros_like(stats_ref)

        stats = stats_ref[...]
    mixed = []
    for j in range(PER):
        low, high = window(j)
        scores = dot_nt(masked_query(query, j), keys[:, low:high]) * scale
        if allowed is not None:
            scores = jnp.where(allowed, scores, -jnp.inf)
        peak = jnp.max(scores, axis=1, keepdims=True)
        raised = jnp.exp(scores - peak)
        total = jnp.sum(raised, axis=1, keepdims=True)
        out = dot_nn(raised.astype(jnp.bfloat16), values[:, low:high])
        if normalise:
            out = out / total
        mixed.append(out)
        head = band * PER + j
        stats = jnp.where(lanes == head, peak, stats)
        stats = jnp.where(lanes == head + LSPLIT, total, stats)
    stats_ref[...] = stats
    for tile in range(BAND // LANES):
        put(tile, by_tile(tile, lambda j: mixed[j][:, tile * LANES - window(j)[0]:][:, :LANES]))


def prefix_kernel(scale, query_ref, key_ref, value_ref, out_ref, stats_ref):
    band = pl.program_id(0)
    bands = pl.num_programs(0)
    width = out_ref.shape[1] - LANES

    def put(tile, cols):
        at = pl.multiple_of(band * BAND + tile * LANES, LANES)
        out_ref[:, pl.ds(at, LANES)] = cols.astype(out_ref.dtype)

    attend(query_ref[...], key_ref[...], value_ref[...], None, scale, True, put, stats_ref)

    @pl.when(band == bands - 1)
    def _():
        full = stats_ref[...]
        high = full.astype(jnp.bfloat16).astype(jnp.float32)
        rest = full - high
        mid = rest.astype(jnp.bfloat16).astype(jnp.float32)
        low = rest - mid
        packed = high + pltpu.roll(mid, PIECE, 1) + pltpu.roll(low, 2 * PIECE, 1)
        out_ref[:, width:] = packed.astype(out_ref.dtype)


def suffix_kernel(scale, reqc_ref, reqr_ref, query_ref, key_ref, value_ref, out_ref, stats_ref):
    toks = query_ref.shape[0]
    shape = (toks, toks)
    allowed = (reqc_ref[...] == reqr_ref[...]) & (
        lax.broadcasted_iota(jnp.int32, shape, 1) <= lax.broadcasted_iota(jnp.int32, shape, 0)
    )

    def put(tile, cols):
        out_ref[:, tile * LANES:(tile + 1) * LANES] = cols

    keys = key_ref[...].reshape(toks, BAND)
    values = value_ref[...].reshape(toks, BAND)
    attend(query_ref[...], keys, values, allowed, scale, False, put, stats_ref)


def merge_kernel(target_ref, back_ref, pstats_ref, mixed_ref, sstats_ref, out_ref):
    band = pl.program_id(0)
    rows = back_ref.shape[0]
    toks = target_ref.shape[0]
    place = lane_iota((toks, rows))
    pick = jnp.where(place == target_ref[...], 1.0, 0.0).astype(jnp.bfloat16)
    packed = dot_nn(pick, pstats_ref[...])
    prefix = (packed + pltpu.roll(packed, LANES - PIECE, 1)) + pltpu.roll(
        packed, LANES - 2 * PIECE, 1
    )
    suffix = sstats_ref[...]
    top = jnp.maximum(prefix, suffix)
    first = pltpu.roll(prefix, LANES - LSPLIT, 1) * jnp.exp(prefix - top)
    second = jnp.exp(suffix - top)
    below = first + second * pltpu.roll(suffix, LANES - LSPLIT, 1)
    wp = first / below
    ws = second / below
    lanes = lane_iota((toks, LANES))

    def column(weights, j):
        return jnp.sum(jnp.where(lanes == band * PER + j, weights, 0.0), axis=1, keepdims=True)

    cp = [column(wp, j) for j in range(PER)]
    cs = [column(ws, j) for j in range(PER)]
    for tile in range(BAND // LANES):
        cols = slice(tile * LANES, (tile + 1) * LANES)
        back = dot_nn(pick, back_ref[:, cols])
        merged = by_tile(tile, lambda j: cp[j]) * back + by_tile(tile, lambda j: cs[j]) * mixed_ref[:, cols]
        out_ref[:, cols] = merged.astype(out_ref.dtype)


def whole_block(array):
    return pl.BlockSpec(array.shape, lambda g: (0,) * array.ndim)


def band_block(rows, off=0):
    return pl.BlockSpec((rows, BAND), lambda g: (0, g + off))


def cost(flops, moved):
    return pl.CostEstimate(flops=flops, bytes_accessed=moved, transcendentals=0)


def room():
    return pltpu.CompilerParams(vmem_limit_bytes=48 * 1024 * 1024)


def exchange(x, axis):
    return lax.all_to_all(x, axis, split_axis=0, concat_axis=0, tiled=True)


def shift_exchange(x, axis):
    n = lax.axis_size(axis)
    me = lax.axis_index(axis)
    parts = [lax.dynamic_index_in_dim(x, me, 0, keepdims=False)]
    for d in range(1, n):
        ring = [(i, (i + d) % n) for i in range(n)]
        sent = lax.dynamic_index_in_dim(x, lax.rem(me + d, n), 0, keepdims=False)
        parts.append(lax.ppermute(sent, axis, ring))
    out = []
    for source in range(n):
        picked = parts[0]
        for d in range(1, n):
            picked = jnp.where(lax.rem(me + n - source, n) == d, parts[d], picked)
        out.append(picked)
    return jnp.stack(out)


def generic_device(qkv, prefix_cache, suffix_lengths, request_groups, prefix_owner):
    n_head = lax.axis_size("head")
    n_tok = lax.axis_size("tok")
    here = qkv.shape[0]
    width = qkv.shape[2] // n_head
    toks = here * n_head
    scale = 1.0 / math.sqrt(HD)
    bands = width // BAND
    parts = 1
    each = bands // parts
    cols = each * BAND
    capacity = 3 * toks // n_tok
    rows = n_tok * capacity
    planes = jnp.transpose(qkv, (1, 0, 2)).reshape(3, here, n_head, width)
    queries = [
        exchange(
            jnp.stack([qkv[:, 0, h * width:(h + 1) * width] for h in range(n_head)]), "head"
        ).reshape(toks, cols)
        for p in range(parts)
    ]
    kv_send = jnp.transpose(planes[1:], (2, 0, 1, 3))

    lengths = suffix_lengths[0]
    groups = request_groups[0]
    requests = lengths.shape[0]
    ends = jnp.sum(jnp.where(jnp.arange(requests)[:, None] <= jnp.arange(requests)[None, :], lengths[:, None], 0), axis=0)
    starts = ends - lengths
    slots = jnp.sum(jnp.where(groups[:, None] == jnp.arange(n_tok)[None, :], prefix_owner[None, :], 0), axis=1)
    position = jnp.arange(toks, dtype=jnp.int32)
    request = jnp.sum((position[:, None] >= ends[None, :]).astype(jnp.int32), axis=1)
    base = slots * capacity - starts
    inside = request[:, None] == jnp.arange(requests, dtype=jnp.int32)[None, :]
    target = (position + jnp.sum(jnp.where(inside, base[None, :], 0), axis=1)).astype(jnp.int32)
    target_row = target[None, :]
    target_col = target[:, None]
    reqc, reqr = request[:, None], request[None, :]

    prefix_len = prefix_cache.shape[1]
    queries[0], cache_keys, cache_values = lax.optimization_barrier(
        (queries[0], prefix_cache[0, :, 0], prefix_cache[0, :, 1])
    )
    received = []
    for p in range(parts):
        outgoing = pl.pallas_call(
            spread_kernel,
            grid=(each,),
            out_shape=jax.ShapeDtypeStruct((rows, cols), jnp.bfloat16),
            in_specs=[whole_block(target_row), band_block(toks)],
            out_specs=band_block(rows),
            cost_estimate=cost(2 * rows * toks * cols, 2 * (rows + toks) * cols),
            compiler_params=room(),
            name="spread",
        )(target_row, queries[p])
        if p == 0:
            outgoing, kv_send = lax.optimization_barrier((outgoing, kv_send))
        received.append(exchange(outgoing.reshape(n_tok, capacity, cols), "tok").reshape(rows, cols))
    kv = shift_exchange(kv_send, "head")

    back = []
    for p in range(parts):
        mixed = pl.pallas_call(
            functools.partial(prefix_kernel, scale),
            grid=(each,),
            out_shape=jax.ShapeDtypeStruct((rows, cols + LANES), jnp.bfloat16),
            in_specs=[band_block(rows), band_block(prefix_len, p * each), band_block(prefix_len, p * each)],
            out_specs=pl.BlockSpec((rows, cols + LANES), lambda g: (0, 0)),
            scratch_shapes=[pltpu.VMEM((rows, LANES), jnp.float32)],
            cost_estimate=cost(4 * rows * prefix_len * cols, 4 * (rows + prefix_len) * cols),
            compiler_params=room(),
            name="prefix",
        )(received[p], cache_keys, cache_values)
        back.append(exchange(mixed.reshape(n_tok, capacity, cols + LANES), "tok").reshape(rows, cols + LANES))

    finals = []
    for p in range(parts):
        key_spec = pl.BlockSpec((n_head, None, here, BAND), lambda g, p=p: (0, 0, 0, g + p * each))
        value_spec = pl.BlockSpec((n_head, None, here, BAND), lambda g, p=p: (0, 1, 0, g + p * each))
        mixed_s, stats_s = pl.pallas_call(
            functools.partial(suffix_kernel, scale),
            grid=(each,),
            out_shape=[
                jax.ShapeDtypeStruct((toks, cols), jnp.float32),
                jax.ShapeDtypeStruct((toks, LANES), jnp.float32),
            ],
            in_specs=[whole_block(reqc), whole_block(reqr), band_block(toks), key_spec, value_spec],
            out_specs=[band_block(toks), pl.BlockSpec((toks, LANES), lambda g: (0, 0))],
            cost_estimate=cost(4 * toks * toks * cols, 10 * toks * cols),
            compiler_params=room(),
            name="suffix",
        )(reqc, reqr, queries[p], kv, kv)
        merged = pl.pallas_call(
            merge_kernel,
            grid=(each,),
            out_shape=jax.ShapeDtypeStruct((toks, cols), jnp.bfloat16),
            in_specs=[
                whole_block(target_col),
                band_block(rows),
                pl.BlockSpec((rows, LANES), lambda g: (0, cols // LANES)),
                band_block(toks),
                whole_block(stats_s),
            ],
            out_specs=band_block(toks),
            cost_estimate=cost(2 * rows * toks * cols, 2 * (rows + 3 * toks) * cols),
            compiler_params=room(),
            name="merge",
        )(target_col, back[p], back[p], mixed_s, stats_s)
        finals.append(exchange(merged.reshape(n_head, here, cols), "head"))
    attended = jnp.transpose(jnp.stack(finals, axis=2), (1, 0, 2, 3)).reshape(here, n_head * width)
    suffix_cache = jnp.transpose(kv, (0, 2, 1, 3)).reshape(toks, 2, width)
    return (attended, suffix_cache)


TEAM = 4
FEATURES = 7168
CODE = 1024
CAPS = (192, 208, 224, 256, 384)
FIRST = 512
MIDDLE = 384
STAT = 8
MESH = pl.DeviceIdType.MESH


def place():
    tok = lax.axis_index("tok")
    half = lax.axis_index("head")
    return lax.div(tok, TEAM), lax.rem(tok, TEAM), half


def team_at(member, level):
    return {"tok": level * TEAM + lax.rem(member, TEAM), "head": lax.div(member, TEAM)}


def team_rows(member, rows):
    at = (lax.rem(member, TEAM) * 2 + lax.div(member, TEAM)) * rows
    return pl.ds(pl.multiple_of(at, 16), rows)


def band_cols(member, low=0, wide=BAND):
    return pl.ds(pl.multiple_of(member * BAND + low, LANES), wide)


def fold(cap):
    return max(g for g in (1, 2, 4, 8, 16) if cap % (8 * g) == 0)


def masked_window(query, j):
    low, high = window(j)
    cols = lane_iota((query.shape[0], high - low)) + low
    keep = (cols >= j * HD) & (cols < (j + 1) * HD)
    return jnp.where(keep, query, jnp.zeros((), query.dtype))


def gather_kernel(
    qkv_ref, meta_ref, owner_ref, cache_ref, pool_ref, kv_ref, slot_ref, code_ref, req_ref, peak_ref,
    table, cache, sm, rm, sq, rq, sl,
):
    level, work, half = place()
    tok = level * TEAM + work
    team = 2 * TEAM
    mine = half * TEAM + work
    n = lax.axis_size("tok")
    rows = qkv_ref.shape[1]

    def meta_copy(d, landing):
        return pltpu.make_async_remote_copy(
            src_ref=meta_ref,
            dst_ref=table.at[landing],
            send_sem=sm.at[d],
            recv_sem=rm.at[d],
            device_id={"tok": lax.rem(tok + d, n), "head": half},
            device_id_type=MESH,
        )

    def query_copy(e, landing):
        peer = lax.rem(mine + e, team)
        return pltpu.make_async_remote_copy(
            src_ref=qkv_ref.at[0, :, band_cols(peer)],
            dst_ref=pool_ref.at[team_rows(landing, rows), :],
            send_sem=sq.at[e],
            recv_sem=rq.at[e],
            device_id=team_at(peer, level),
            device_id_type=MESH,
        )

    barrier = pltpu.get_barrier_semaphore()
    for d in range(1, n):
        pl.semaphore_signal(
            barrier, inc=1, device_id={"tok": lax.rem(tok + d, n), "head": half}, device_id_type=MESH
        )
    for w in range(TEAM):
        pl.semaphore_signal(
            barrier, inc=1, device_id={"tok": level * TEAM + w, "head": 1 - half}, device_id_type=MESH
        )
    bring = pltpu.make_async_copy(cache_ref, cache, sl.at[0])
    bring.start()
    own = pltpu.make_async_copy(
        qkv_ref.at[0, :, band_cols(mine)], pool_ref.at[team_rows(mine, rows), :], sl.at[1]
    )
    own.start()
    pl.semaphore_wait(barrier, n - 1 + TEAM)
    for d in range(1, n):
        meta_copy(d, tok).start()
    for e in range(1, team):
        query_copy(e, mine).start()
    table[tok] = meta_ref[...]
    bring.wait()
    width = kv_ref.shape[2]

    def split(c, carry):
        cols = pl.ds(pl.multiple_of(c * LANES, LANES), LANES)
        kv_ref[0, :, cols] = cache[:, 0, cols]
        kv_ref[1, :, cols] = cache[:, 1, cols]
        return carry

    lax.fori_loop(0, width // LANES, split, 0)
    for d in range(1, n):
        meta_copy(d, lax.rem(tok + n - d, n)).wait_recv()

    lengths = table[:, 0, :]
    groups = table[:, 1, :]
    slots = jnp.zeros_like(groups)
    for g in range(owner_ref.shape[0]):
        slots = jnp.where(groups == g, owner_ref[g], slots)
    spot = lane_iota((n, LANES))
    slot = jnp.zeros((n, LANES), jnp.int32)
    request = jnp.zeros((n, LANES), jnp.int32)
    end = jnp.zeros((n, 1), jnp.int32)
    for r in range(REQUESTS):
        start = end
        end = start + lengths[:, r:r + 1]
        inside = (spot >= start) & (spot < end)
        slot = jnp.where(inside, slots[:, r:r + 1], slot)
        request = jnp.where(inside, r, request)
    goal = lax.div(slot, TEAM)
    marks = [jnp.where(goal == z, 1.0, 0.0) for z in range(TEAM)]
    hot = jnp.concatenate(marks, axis=0).astype(jnp.bfloat16)
    down = lax.broadcasted_iota(jnp.int32, (LANES, LANES), 0)
    upto = jnp.where(down <= lane_iota((LANES, LANES)), 1.0, 0.0).astype(jnp.bfloat16)
    running = dot_nn(hot, upto)
    totals = dot_nn(hot, jnp.ones((LANES, LANES), jnp.bfloat16))
    m = TEAM * n
    a = lax.broadcasted_iota(jnp.int32, (m, m), 0)
    b = lax.broadcasted_iota(jnp.int32, (m, m), 1)
    earlier = (lax.div(a, TEAM) == lax.div(b, TEAM)) & (b < a)
    before = dot_nn(jnp.where(earlier, 1.0, 0.0).astype(jnp.bfloat16), totals.astype(jnp.bfloat16))
    count = (running + before).astype(jnp.int32)
    code = jnp.zeros((n, LANES), jnp.int32)
    for z in range(TEAM):
        code = jnp.where(goal == z, z * CODE + count[z * n:(z + 1) * n] - 1, code)
    slot = slot - goal * TEAM
    for z in range(TEAM):
        part = slice(z * TEAM, (z + 1) * TEAM)
        slot_ref[z] = slot[part]
        code_ref[z] = code[part]
        req_ref[z] = request[part]
    most = jnp.max(jnp.max(count, axis=0, keepdims=True), axis=1, keepdims=True)
    peak_ref[...] = jnp.broadcast_to(most, peak_ref.shape)

    own.wait()
    for e in range(1, team):
        query_copy(e, lax.rem(mine + team - e, team)).wait_recv()
    for d in range(1, n):
        meta_copy(d, tok).wait_send()
    for e in range(1, team):
        query_copy(e, mine).wait_send()


def pool_kernel(
    scale, cap, pool_ref, slot_ref, code_ref, req_ref, qkv_ref, kv_ref, out_ref, pair_ref,
    outgo, income, result, back, stats, cols, keep, fresh, final, note_out, note_in, notes, pair,
    s1, r1, s2, r2, s3, r3, s4, r4, s5, r5, s6, r6, s7, r7, sl,
):
    level, work, half = place()
    team = 2 * TEAM
    mine = half * TEAM + work
    rows = qkv_ref.shape[1]
    toks = 2 * rows

    def level_id(d):
        return {"tok": lax.rem(level + d, TEAM) * TEAM + work, "head": half}

    width = kv_ref.shape[2]
    groups = fold(cap)
    high_rows = cap // groups

    def forth_copy(d, part):
        span = slice(0, FIRST) if part == 0 else slice(FIRST, BAND)
        return pltpu.make_async_remote_copy(
            src_ref=outgo.at[d, :, span], dst_ref=income.at[d, :, span],
            send_sem=s1.at[part, d], recv_sem=r1.at[part, d],
            device_id=level_id(d), device_id_type=MESH,
        )

    def note_copy(d):
        return pltpu.make_async_remote_copy(
            src_ref=note_out.at[d], dst_ref=note_in.at[d], send_sem=s6.at[d], recv_sem=r6.at[d],
            device_id=level_id(TEAM - d), device_id_type=MESH,
        )

    def half_cols(which):
        return pl.ds(pl.multiple_of(which * width, LANES), width)

    swap = pltpu.make_async_remote_copy(
        src_ref=qkv_ref.at[1:3, :, half_cols(1 - half)], dst_ref=pair.at[1],
        send_sem=s7.at[0], recv_sem=r7.at[0],
        device_id={"tok": level * TEAM + work, "head": 1 - half}, device_id_type=MESH,
    )

    def weave(which, owner):
        where = pl.ds(pl.multiple_of(owner * rows, 16), rows)

        def step(c, carry):
            span = pl.ds(pl.multiple_of(c * LANES, LANES), LANES)
            pair_ref[where, 0, span] = pair[which, 0, :, span]
            pair_ref[where, 1, span] = pair[which, 1, :, span]
            return carry

        lax.fori_loop(0, width // LANES, step, 0)

    def back_copy(d, part):
        span = slice(0, MIDDLE) if part == 0 else slice(MIDDLE, BAND)
        return pltpu.make_async_remote_copy(
            src_ref=result.at[d, :, span], dst_ref=back.at[d, :, span],
            send_sem=s2.at[part, d], recv_sem=r2.at[part, d],
            device_id=level_id(TEAM - d), device_id_type=MESH,
        )

    def cache_copy(e, part, landing):
        peer = lax.rem(work + e, TEAM)
        low, high = (0, FIRST) if part == 0 else (FIRST, BAND)
        return pltpu.make_async_remote_copy(
            src_ref=kv_ref.at[:, :, band_cols(peer, low, high - low)],
            dst_ref=keep.at[landing, :, :, low:high],
            send_sem=s3.at[part, e], recv_sem=r3.at[part, e],
            device_id={"tok": level * TEAM + peer, "head": half}, device_id_type=MESH,
        )

    def fresh_copy(e, landing):
        peer = lax.rem(mine + e, team)
        return pltpu.make_async_remote_copy(
            src_ref=qkv_ref.at[1:3, :, band_cols(peer)],
            dst_ref=fresh.at[:, team_rows(landing, rows), :],
            send_sem=s4.at[e], recv_sem=r4.at[e],
            device_id=team_at(peer, level), device_id_type=MESH,
        )

    def final_copy(e, landing):
        peer = lax.rem(mine + e, team)
        return pltpu.make_async_remote_copy(
            src_ref=final.at[team_rows(peer, rows), :],
            dst_ref=out_ref.at[:, band_cols(landing)],
            send_sem=s5.at[e], recv_sem=r5.at[e],
            device_id=team_at(peer, level), device_id_type=MESH,
        )

    barrier = pltpu.get_barrier_semaphore()
    for e in range(1, team):
        pl.semaphore_signal(barrier, inc=1, device_id=team_at(lax.rem(mine + e, team), level), device_id_type=MESH)
    for d in range(1, TEAM):
        pl.semaphore_signal(barrier, inc=1, device_id=level_id(d), device_id_type=MESH)
    own_cache = pltpu.make_async_copy(kv_ref.at[:, :, band_cols(work)], keep.at[work], sl.at[0])
    own_cache.start()
    own_fresh = pltpu.make_async_copy(
        qkv_ref.at[1:3, :, band_cols(mine)], fresh.at[:, team_rows(mine, rows), :], sl.at[1]
    )
    own_fresh.start()
    own_pair = pltpu.make_async_copy(qkv_ref.at[1:3, :, half_cols(half)], pair.at[0], sl.at[2])
    own_pair.start()
    pl.semaphore_wait(barrier, team - 1 + TEAM - 1)
    for part in range(2):
        for e in range(1, TEAM):
            cache_copy(e, part, work).start()

    def flat(ref, z):
        block = ref[z]
        return jnp.concatenate([block[i:i + 1] for i in range(TEAM)], axis=1)

    down = lax.broadcasted_iota(jnp.int32, (cap, TEAM * toks), 0)
    code = flat(code_ref, level)

    def send(d):
        goal = lax.rem(level + d, TEAM)
        pick = jnp.where(down == code - goal * CODE, 1.0, 0.0).astype(jnp.bfloat16)
        packed = dot_nn(pick, pool_ref[...]).astype(jnp.bfloat16)
        if d:
            outgo[d] = packed
            forth_copy(d, 0).start()
        else:
            income[0] = packed

    for d in (2, 3, 1):
        send(d)
    for d in (2, 3, 1):
        forth_copy(d, 1).start()
    swap.start()
    send(0)
    for d in range(TEAM):
        origin = lax.rem(level + TEAM - d, TEAM)
        hit = down == flat(code_ref, origin) - level * CODE
        local = flat(slot_ref, origin).astype(jnp.float32)
        found = jnp.sum(jnp.where(hit, local, 0.0), axis=1, keepdims=True)
        cols[d] = jnp.broadcast_to(found, (cap, LANES))
    stats[...] = jnp.zeros_like(stats)
    own_pair.wait()
    weave(0, half)
    own_cache.wait()

    def prefix(part):
        heads = range(2) if part == 0 else range(2, PER)

        def run(d, carry):
            which = cols[d][:, :1]
            lanes = lane_iota((cap, LANES))
            noted = stats[d]
            mixed = {}
            for j in heads:
                low, high = window(j)
                asked = masked_window(income[d, :, low:high], j)
                scores = None
                for s in range(TEAM):
                    part_scores = dot_nt(asked, keep[s, 0, :, low:high])
                    scores = part_scores if s == 0 else jnp.where(which == s, part_scores, scores)
                scores = scores * scale
                top = jnp.max(scores, axis=1, keepdims=True)
                raised = jnp.exp(scores - top)
                total = jnp.sum(raised, axis=1, keepdims=True)
                out = None
                for s in range(TEAM):
                    weights = jnp.where(which == s, raised, 0.0).astype(jnp.bfloat16)
                    term = dot_nn(weights, keep[s, 1, :, low:high])
                    out = term if s == 0 else out + term
                mixed[j] = out / total
                noted = jnp.where(lanes == j, top, noted)
                noted = jnp.where(lanes == PER + j, total, noted)

            def cut(j, tile):
                return mixed[j][:, tile * LANES - window(j)[0]:][:, :LANES]

            tiles = range(4) if part == 0 else range(3, BAND // LANES)
            for tile in tiles:
                first, last = owners_of(tile)
                span = slice(tile * LANES, (tile + 1) * LANES)
                if tile != 3:
                    values = by_tile(tile, lambda j: cut(j, tile)).astype(jnp.bfloat16)
                elif part == 0:
                    values = cut(first, tile).astype(jnp.bfloat16)
                else:
                    edge = last * HD - tile * LANES
                    values = jnp.where(
                        lanes < edge, result[d, :, span].astype(jnp.float32), cut(last, tile)
                    ).astype(jnp.bfloat16)
                result[d, :, span] = values
            stats[d] = noted
            if part == 1:
                folded = noted[:high_rows]
                for k in range(1, groups):
                    folded = folded + pltpu.roll(noted[k * high_rows:(k + 1) * high_rows], k * STAT, 1)
                note_out[d] = folded
            return carry

        lax.fori_loop(0, TEAM, run, 0)

    for part in range(2):
        for d in range(1, TEAM):
            forth_copy(d, part).wait_recv()
        for e in range(1, TEAM):
            cache_copy(e, part, lax.rem(work + TEAM - e, TEAM)).wait_recv()
        if part == 1:
            for e in range(1, team):
                fresh_copy(e, mine).start()
        prefix(part)
        for d in (2, 3, 1):
            back_copy(d, part).start()
        if part == 1:
            for d in range(1, TEAM):
                note_copy(d).start()
        else:
            swap.wait_recv()
            weave(1, 1 - half)
    back[0] = result[0]
    note_in[0] = note_out[0]
    own_fresh.wait()
    for e in range(1, team):
        fresh_copy(e, lax.rem(mine + team - e, team)).wait_recv()
    for part in range(2):
        for d in range(1, TEAM):
            back_copy(d, part).wait_recv()
    for d in range(1, TEAM):
        note_copy(d).wait_recv()
    for d in range(TEAM):
        block = note_in[d]
        turned = [block] + [pltpu.roll(block, LANES - k * STAT, 1) for k in range(1, groups)]
        full = jnp.where(lane_iota((cap, LANES)) < STAT, jnp.concatenate(turned, axis=0), 0.0)
        high = full.astype(jnp.bfloat16).astype(jnp.float32)
        rest = full - high
        mid = rest.astype(jnp.bfloat16).astype(jnp.float32)
        notes[d] = (high + pltpu.roll(mid, STAT, 1) + pltpu.roll(rest - mid, 2 * STAT, 1)).astype(jnp.bfloat16)

    eye = lax.broadcasted_iota(jnp.int32, (toks, toks), 0) == lax.broadcasted_iota(jnp.int32, (toks, toks), 1)
    causal = lax.broadcasted_iota(jnp.int32, (toks, toks), 1) <= lax.broadcasted_iota(jnp.int32, (toks, toks), 0)

    def column(row):
        return jnp.sum(jnp.where(eye, row, 0.0), axis=1, keepdims=True)

    def finish(i, carry):
        span = pl.ds(pl.multiple_of(i * toks, toks), toks)
        codes = code_ref[level, pl.ds(i, 1), :]
        goal = lax.div(codes, CODE)
        seat = lax.rem(goal - level + TEAM, TEAM) * cap + (codes - goal * CODE)
        seat = column(seat.astype(jnp.float32)).astype(jnp.int32)
        pick = jnp.where(lane_iota((toks, TEAM * cap)) == seat, 1.0, 0.0).astype(jnp.bfloat16)
        ready = dot_nn(pick, back[...].reshape(TEAM * cap, BAND))
        packed = dot_nn(pick, notes[...].reshape(TEAM * cap, LANES))
        prior = (packed + pltpu.roll(packed, LANES - STAT, 1)) + pltpu.roll(packed, LANES - 2 * STAT, 1)
        asks = req_ref[level, pl.ds(i, 1), :].astype(jnp.float32)
        allowed = (column(asks) == asks) & causal
        query = pool_ref[span, :]
        merged = []
        for j in range(PER):
            low, high = window(j)
            scores = dot_nt(masked_query(query, j), fresh[0, span, low:high]) * scale
            scores = jnp.where(allowed, scores, -jnp.inf)
            peak = jnp.max(scores, axis=1, keepdims=True)
            raised = jnp.exp(scores - peak)
            total = jnp.sum(raised, axis=1, keepdims=True)
            out = dot_nn(raised.astype(jnp.bfloat16), fresh[1, span, low:high])
            ppeak = prior[:, j:j + 1]
            ptotal = prior[:, PER + j:PER + j + 1]
            top = jnp.maximum(ppeak, peak)
            first = ptotal * jnp.exp(ppeak - top)
            second = jnp.exp(peak - top)
            below = first + second * total
            merged.append((first / below) * ready[:, low:high] + (second / below) * out)
        for tile in range(BAND // LANES):
            values = by_tile(tile, lambda j: merged[j][:, tile * LANES - window(j)[0]:][:, :LANES])
            final[span, tile * LANES:(tile + 1) * LANES] = values.astype(jnp.bfloat16)
        return carry

    lax.fori_loop(0, TEAM, finish, 0)
    for e in range(1, team):
        final_copy(e, mine).start()
    out_ref[:, band_cols(mine)] = final[team_rows(mine, rows), :]
    for e in range(1, team):
        final_copy(e, lax.rem(mine + team - e, team)).wait_recv()
    for d in range(1, TEAM):
        note_copy(d).wait_send()
        for part in range(2):
            forth_copy(d, part).wait_send()
            back_copy(d, part).wait_send()
    for e in range(1, TEAM):
        for part in range(2):
            cache_copy(e, part, work).wait_send()
    swap.wait_send()
    for e in range(1, team):
        fresh_copy(e, mine).wait_send()
        final_copy(e, mine).wait_send()


REQUESTS = 8


def pooled_device(qkv, prefix_cache, suffix_lengths, request_groups, prefix_owner):
    n_head = lax.axis_size("head")
    n_tok = lax.axis_size("tok")
    here = qkv.shape[0]
    width = qkv.shape[2] // n_head
    toks = here * n_head
    scale = 1.0 / math.sqrt(HD)
    past = prefix_cache.shape[1]
    planes = jnp.transpose(qkv, (1, 0, 2))
    meta = jnp.pad(jnp.concatenate([suffix_lengths, request_groups], 0), ((0, 6), (0, LANES - suffix_lengths.shape[1])))
    vmem = pl.BlockSpec(memory_space=pltpu.VMEM)
    smem = pl.BlockSpec(memory_space=pltpu.SMEM)
    hbm = pl.BlockSpec(memory_space=pl.ANY)
    dma = pltpu.SemaphoreType.DMA
    table = jax.ShapeDtypeStruct((TEAM, TEAM, LANES), jnp.int32)

    pool, kv, slot, code, request, peak = pl.pallas_call(
        gather_kernel,
        out_shape=[
            jax.ShapeDtypeStruct((TEAM * toks, BAND), jnp.bfloat16),
            jax.ShapeDtypeStruct((2, past, width), jnp.bfloat16),
            table, table, table,
            jax.ShapeDtypeStruct((8, LANES), jnp.int32),
        ],
        in_specs=[hbm, vmem, smem, hbm],
        out_specs=[vmem] * 6,
        scratch_shapes=[
            pltpu.VMEM((n_tok, 8, LANES), jnp.int32),
            pltpu.VMEM((past, 2, width), jnp.bfloat16),
            dma((n_tok,)), dma((n_tok,)), dma((2 * TEAM,)), dma((2 * TEAM,)), dma((2,)),
        ],
        compiler_params=pltpu.CompilerParams(
            collective_id=0, has_side_effects=True, vmem_limit_bytes=48 * 1024 * 1024
        ),
        name="gather",
    )(planes, meta, prefix_owner, prefix_cache[0])

    def pooled(cap, number):
        def call(pool, slot, code, request, planes, kv):
            return pl.pallas_call(
                functools.partial(pool_kernel, scale, cap),
                out_shape=[
                    jax.ShapeDtypeStruct((here, n_head * width), jnp.bfloat16),
                    jax.ShapeDtypeStruct((toks, 2, width), jnp.bfloat16),
                ],
                in_specs=[vmem, vmem, vmem, vmem, hbm, hbm],
                out_specs=[vmem] * 2,
                scratch_shapes=[
                    pltpu.VMEM((TEAM, cap, BAND), jnp.bfloat16),
                    pltpu.VMEM((TEAM, cap, BAND), jnp.bfloat16),
                    pltpu.VMEM((TEAM, cap, BAND), jnp.bfloat16),
                    pltpu.VMEM((TEAM, cap, BAND), jnp.bfloat16),
                    pltpu.VMEM((TEAM, cap, LANES), jnp.float32),
                    pltpu.VMEM((TEAM, cap, LANES), jnp.float32),
                    pltpu.VMEM((TEAM, 2, past, BAND), jnp.bfloat16),
                    pltpu.VMEM((2, TEAM * toks, BAND), jnp.bfloat16),
                    pltpu.VMEM((TEAM * toks, BAND), jnp.bfloat16),
                    pltpu.VMEM((TEAM, cap // fold(cap), LANES), jnp.float32),
                    pltpu.VMEM((TEAM, cap // fold(cap), LANES), jnp.float32),
                    pltpu.VMEM((TEAM, cap, LANES), jnp.bfloat16),
                    pltpu.VMEM((2, 2, here, width), jnp.bfloat16),
                    dma((2, TEAM)), dma((2, TEAM)), dma((2, TEAM)), dma((2, TEAM)),
                    dma((2, TEAM)), dma((2, TEAM)), dma((2 * TEAM,)), dma((2 * TEAM,)),
                    dma((2 * TEAM,)), dma((2 * TEAM,)), dma((TEAM,)), dma((TEAM,)),
                    dma((1,)), dma((1,)), dma((3,)),
                ],
                compiler_params=pltpu.CompilerParams(
                    collective_id=number, has_side_effects=True, vmem_limit_bytes=52 * 1024 * 1024
                ),
                name="pooled",
            )(pool, slot, code, request, planes, kv)

        return call

    most = peak[0, 0]
    index = sum((most > cap).astype(jnp.int32) for cap in CAPS[:-1])
    return lax.switch(
        index, [pooled(cap, 1 + i) for i, cap in enumerate(CAPS)], pool, slot, code, request, planes, kv
    )


def solution(mesh):
    in_specs = (
        P(("tok", "head"), None, None),
        P("tok", None, None, "head"),
        P("tok", None),
        P("tok", None),
        P(),
    )
    out_specs = (P(("tok", "head"), None), P("tok", None, "head"))
    pooled = mesh.shape["tok"] == TEAM * TEAM and BAND * TEAM * mesh.shape["head"] == FEATURES
    body = pooled_device if pooled else generic_device
    return jax.shard_map(
        body, mesh=mesh, in_specs=in_specs, out_specs=out_specs, check_vma=False
    )
```

```python
import functools
import math

import jax
import jax.numpy as jnp
from jax import lax
from jax.experimental import pallas as pl
from jax.experimental.pallas import tpu as pltpu
from jax.sharding import PartitionSpec as P

HD = 224
LANES = 128
BAND = math.lcm(HD, LANES)
PER = BAND // HD
LSPLIT = 16
PIECE = 2 * LSPLIT


def window(j):
    low = j * HD // LANES * LANES
    high = -(-(j + 1) * HD // LANES) * LANES
    return low, high


def owners_of(tile):
    first = tile * LANES // HD
    last = ((tile + 1) * LANES - 1) // HD
    return first, last


def lane_iota(shape):
    return lax.broadcasted_iota(jnp.int32, shape, len(shape) - 1)


def by_tile(tile, pick):
    first, last = owners_of(tile)
    left = pick(first)
    if first == last:
        return left
    right = pick(last)
    edge = last * HD - tile * LANES
    return jnp.where(lane_iota((right.shape[0], LANES)) < edge, left, right)


def masked_query(query, j):
    low, high = window(j)
    cols = lane_iota((query.shape[0], high - low)) + low
    keep = (cols >= j * HD) & (cols < (j + 1) * HD)
    return jnp.where(keep, query[:, low:high], jnp.zeros((), query.dtype))


def dot_nt(a, b):
    return lax.dot_general(a, b, (((1,), (1,)), ((), ())), preferred_element_type=jnp.float32)


def dot_nn(a, b):
    return lax.dot_general(a, b, (((1,), (0,)), ((), ())), preferred_element_type=jnp.float32)


def spread_kernel(target_ref, query_ref, out_ref):
    rows = out_ref.shape[0]
    toks = target_ref.shape[1]
    place = lax.broadcasted_iota(jnp.int32, (rows, toks), 0)
    pick = jnp.where(place == target_ref[...], 1.0, 0.0).astype(jnp.bfloat16)
    out_ref[...] = dot_nn(pick, query_ref[...]).astype(jnp.bfloat16)


def attend(query, keys, values, allowed, scale, normalise, put, stats_ref, band=None):
    band = pl.program_id(0) if band is None else band
    rows = query.shape[0]
    lanes = lane_iota((rows, LANES))

    if isinstance(band, int):
        stats = jnp.zeros_like(stats_ref) if band == 0 else stats_ref[...]
    else:

        @pl.when(band == 0)
        def _():
            stats_ref[...] = jnp.zeros_like(stats_ref)

        stats = stats_ref[...]
    mixed = []
    for j in range(PER):
        low, high = window(j)
        scores = dot_nt(masked_query(query, j), keys[:, low:high]) * scale
        if allowed is not None:
            scores = jnp.where(allowed, scores, -jnp.inf)
        peak = jnp.max(scores, axis=1, keepdims=True)
        raised = jnp.exp(scores - peak)
        total = jnp.sum(raised, axis=1, keepdims=True)
        out = dot_nn(raised.astype(jnp.bfloat16), values[:, low:high])
        if normalise:
            out = out / total
        mixed.append(out)
        head = band * PER + j
        stats = jnp.where(lanes == head, peak, stats)
        stats = jnp.where(lanes == head + LSPLIT, total, stats)
    stats_ref[...] = stats
    for tile in range(BAND // LANES):
        put(tile, by_tile(tile, lambda j: mixed[j][:, tile * LANES - window(j)[0]:][:, :LANES]))


def prefix_kernel(scale, query_ref, key_ref, value_ref, out_ref, stats_ref):
    band = pl.program_id(0)
    bands = pl.num_programs(0)
    width = out_ref.shape[1] - LANES

    def put(tile, cols):
        at = pl.multiple_of(band * BAND + tile * LANES, LANES)
        out_ref[:, pl.ds(at, LANES)] = cols.astype(out_ref.dtype)

    attend(query_ref[...], key_ref[...], value_ref[...], None, scale, True, put, stats_ref)

    @pl.when(band == bands - 1)
    def _():
        full = stats_ref[...]
        high = full.astype(jnp.bfloat16).astype(jnp.float32)
        rest = full - high
        mid = rest.astype(jnp.bfloat16).astype(jnp.float32)
        low = rest - mid
        packed = high + pltpu.roll(mid, PIECE, 1) + pltpu.roll(low, 2 * PIECE, 1)
        out_ref[:, width:] = packed.astype(out_ref.dtype)


def suffix_kernel(scale, reqc_ref, reqr_ref, query_ref, key_ref, value_ref, out_ref, stats_ref):
    toks = query_ref.shape[0]
    shape = (toks, toks)
    allowed = (reqc_ref[...] == reqr_ref[...]) & (
        lax.broadcasted_iota(jnp.int32, shape, 1) <= lax.broadcasted_iota(jnp.int32, shape, 0)
    )

    def put(tile, cols):
        out_ref[:, tile * LANES:(tile + 1) * LANES] = cols

    keys = key_ref[...].reshape(toks, BAND)
    values = value_ref[...].reshape(toks, BAND)
    attend(query_ref[...], keys, values, allowed, scale, False, put, stats_ref)


def merge_kernel(target_ref, back_ref, pstats_ref, mixed_ref, sstats_ref, out_ref):
    band = pl.program_id(0)
    rows = back_ref.shape[0]
    toks = target_ref.shape[0]
    place = lane_iota((toks, rows))
    pick = jnp.where(place == target_ref[...], 1.0, 0.0).astype(jnp.bfloat16)
    packed = dot_nn(pick, pstats_ref[...])
    prefix = (packed + pltpu.roll(packed, LANES - PIECE, 1)) + pltpu.roll(
        packed, LANES - 2 * PIECE, 1
    )
    suffix = sstats_ref[...]
    top = jnp.maximum(prefix, suffix)
    first = pltpu.roll(prefix, LANES - LSPLIT, 1) * jnp.exp(prefix - top)
    second = jnp.exp(suffix - top)
    below = first + second * pltpu.roll(suffix, LANES - LSPLIT, 1)
    wp = first / below
    ws = second / below
    lanes = lane_iota((toks, LANES))

    def column(weights, j):
        return jnp.sum(jnp.where(lanes == band * PER + j, weights, 0.0), axis=1, keepdims=True)

    cp = [column(wp, j) for j in range(PER)]
    cs = [column(ws, j) for j in range(PER)]
    for tile in range(BAND // LANES):
        cols = slice(tile * LANES, (tile + 1) * LANES)
        back = dot_nn(pick, back_ref[:, cols])
        merged = by_tile(tile, lambda j: cp[j]) * back + by_tile(tile, lambda j: cs[j]) * mixed_ref[:, cols]
        out_ref[:, cols] = merged.astype(out_ref.dtype)


def whole_block(array):
    return pl.BlockSpec(array.shape, lambda g: (0,) * array.ndim)


def band_block(rows, off=0):
    return pl.BlockSpec((rows, BAND), lambda g: (0, g + off))


def cost(flops, moved):
    return pl.CostEstimate(flops=flops, bytes_accessed=moved, transcendentals=0)


def room():
    return pltpu.CompilerParams(vmem_limit_bytes=48 * 1024 * 1024)


def exchange(x, axis):
    return lax.all_to_all(x, axis, split_axis=0, concat_axis=0, tiled=True)


def shift_exchange(x, axis):
    n = lax.axis_size(axis)
    me = lax.axis_index(axis)
    parts = [lax.dynamic_index_in_dim(x, me, 0, keepdims=False)]
    for d in range(1, n):
        ring = [(i, (i + d) % n) for i in range(n)]
        sent = lax.dynamic_index_in_dim(x, lax.rem(me + d, n), 0, keepdims=False)
        parts.append(lax.ppermute(sent, axis, ring))
    out = []
    for source in range(n):
        picked = parts[0]
        for d in range(1, n):
            picked = jnp.where(lax.rem(me + n - source, n) == d, parts[d], picked)
        out.append(picked)
    return jnp.stack(out)


def generic_device(qkv, prefix_cache, suffix_lengths, request_groups, prefix_owner):
    n_head = lax.axis_size("head")
    n_tok = lax.axis_size("tok")
    here = qkv.shape[0]
    width = qkv.shape[2] // n_head
    toks = here * n_head
    scale = 1.0 / math.sqrt(HD)
    bands = width // BAND
    parts = 1
    each = bands // parts
    cols = each * BAND
    capacity = 3 * toks // n_tok
    rows = n_tok * capacity
    planes = jnp.transpose(qkv, (1, 0, 2)).reshape(3, here, n_head, width)
    queries = [
        exchange(
            jnp.stack([qkv[:, 0, h * width:(h + 1) * width] for h in range(n_head)]), "head"
        ).reshape(toks, cols)
        for p in range(parts)
    ]
    kv_send = jnp.transpose(planes[1:], (2, 0, 1, 3))

    lengths = suffix_lengths[0]
    groups = request_groups[0]
    requests = lengths.shape[0]
    ends = jnp.sum(jnp.where(jnp.arange(requests)[:, None] <= jnp.arange(requests)[None, :], lengths[:, None], 0), axis=0)
    starts = ends - lengths
    slots = jnp.sum(jnp.where(groups[:, None] == jnp.arange(n_tok)[None, :], prefix_owner[None, :], 0), axis=1)
    position = jnp.arange(toks, dtype=jnp.int32)
    request = jnp.sum((position[:, None] >= ends[None, :]).astype(jnp.int32), axis=1)
    base = slots * capacity - starts
    inside = request[:, None] == jnp.arange(requests, dtype=jnp.int32)[None, :]
    target = (position + jnp.sum(jnp.where(inside, base[None, :], 0), axis=1)).astype(jnp.int32)
    target_row = target[None, :]
    target_col = target[:, None]
    reqc, reqr = request[:, None], request[None, :]

    prefix_len = prefix_cache.shape[1]
    queries[0], cache_keys, cache_values = lax.optimization_barrier(
        (queries[0], prefix_cache[0, :, 0], prefix_cache[0, :, 1])
    )
    received = []
    for p in range(parts):
        outgoing = pl.pallas_call(
            spread_kernel,
            grid=(each,),
            out_shape=jax.ShapeDtypeStruct((rows, cols), jnp.bfloat16),
            in_specs=[whole_block(target_row), band_block(toks)],
            out_specs=band_block(rows),
            cost_estimate=cost(2 * rows * toks * cols, 2 * (rows + toks) * cols),
            compiler_params=room(),
            name="spread",
        )(target_row, queries[p])
        if p == 0:
            outgoing, kv_send = lax.optimization_barrier((outgoing, kv_send))
        received.append(exchange(outgoing.reshape(n_tok, capacity, cols), "tok").reshape(rows, cols))
    kv = shift_exchange(kv_send, "head")

    back = []
    for p in range(parts):
        mixed = pl.pallas_call(
            functools.partial(prefix_kernel, scale),
            grid=(each,),
            out_shape=jax.ShapeDtypeStruct((rows, cols + LANES), jnp.bfloat16),
            in_specs=[band_block(rows), band_block(prefix_len, p * each), band_block(prefix_len, p * each)],
            out_specs=pl.BlockSpec((rows, cols + LANES), lambda g: (0, 0)),
            scratch_shapes=[pltpu.VMEM((rows, LANES), jnp.float32)],
            cost_estimate=cost(4 * rows * prefix_len * cols, 4 * (rows + prefix_len) * cols),
            compiler_params=room(),
            name="prefix",
        )(received[p], cache_keys, cache_values)
        back.append(exchange(mixed.reshape(n_tok, capacity, cols + LANES), "tok").reshape(rows, cols + LANES))

    finals = []
    for p in range(parts):
        key_spec = pl.BlockSpec((n_head, None, here, BAND), lambda g, p=p: (0, 0, 0, g + p * each))
        value_spec = pl.BlockSpec((n_head, None, here, BAND), lambda g, p=p: (0, 1, 0, g + p * each))
        mixed_s, stats_s = pl.pallas_call(
            functools.partial(suffix_kernel, scale),
            grid=(each,),
            out_shape=[
                jax.ShapeDtypeStruct((toks, cols), jnp.float32),
                jax.ShapeDtypeStruct((toks, LANES), jnp.float32),
            ],
            in_specs=[whole_block(reqc), whole_block(reqr), band_block(toks), key_spec, value_spec],
            out_specs=[band_block(toks), pl.BlockSpec((toks, LANES), lambda g: (0, 0))],
            cost_estimate=cost(4 * toks * toks * cols, 10 * toks * cols),
            compiler_params=room(),
            name="suffix",
        )(reqc, reqr, queries[p], kv, kv)
        merged = pl.pallas_call(
            merge_kernel,
            grid=(each,),
            out_shape=jax.ShapeDtypeStruct((toks, cols), jnp.bfloat16),
            in_specs=[
                whole_block(target_col),
                band_block(rows),
                pl.BlockSpec((rows, LANES), lambda g: (0, cols // LANES)),
                band_block(toks),
                whole_block(stats_s),
            ],
            out_specs=band_block(toks),
            cost_estimate=cost(2 * rows * toks * cols, 2 * (rows + 3 * toks) * cols),
            compiler_params=room(),
            name="merge",
        )(target_col, back[p], back[p], mixed_s, stats_s)
        finals.append(exchange(merged.reshape(n_head, here, cols), "head"))
    attended = jnp.transpose(jnp.stack(finals, axis=2), (1, 0, 2, 3)).reshape(here, n_head * width)
    suffix_cache = jnp.transpose(kv, (0, 2, 1, 3)).reshape(toks, 2, width)
    return (attended, suffix_cache)


TEAM = 4
FEATURES = 7168
CODE = 1024
CAPS = (192, 208, 240, 384)
FIRST = 512
MIDDLE = 384
STAT = 8
MESH = pl.DeviceIdType.MESH


def place():
    tok = lax.axis_index("tok")
    half = lax.axis_index("head")
    return lax.div(tok, TEAM), lax.rem(tok, TEAM), half


def team_at(member, level):
    return {"tok": level * TEAM + lax.rem(member, TEAM), "head": lax.div(member, TEAM)}


def team_rows(member, rows):
    at = (lax.rem(member, TEAM) * 2 + lax.div(member, TEAM)) * rows
    return pl.ds(pl.multiple_of(at, 16), rows)


def band_cols(member, low=0, wide=BAND):
    return pl.ds(pl.multiple_of(member * BAND + low, LANES), wide)


def fold(cap):
    return max(g for g in (1, 2, 4, 8, 16) if cap % (8 * g) == 0)


def masked_window(query, j):
    low, high = window(j)
    cols = lane_iota((query.shape[0], high - low)) + low
    keep = (cols >= j * HD) & (cols < (j + 1) * HD)
    return jnp.where(keep, query, jnp.zeros((), query.dtype))


def tables_kernel(meta_ref, owner_ref, slot_ref, code_ref, req_ref, peak_ref, table, sm, rm):
    tok = lax.axis_index("tok")
    n = lax.axis_size("tok")

    def meta_copy(d, landing):
        return pltpu.make_async_remote_copy(
            src_ref=meta_ref,
            dst_ref=table.at[landing],
            send_sem=sm.at[d],
            recv_sem=rm.at[d],
            device_id={"tok": lax.rem(tok + d, n), "head": lax.axis_index("head")},
            device_id_type=MESH,
        )

    def each(body):
        def step(d, carry):
            body(d)
            return carry

        lax.fori_loop(1, n, step, 0)

    barrier = pltpu.get_barrier_semaphore()
    each(
        lambda d: pl.semaphore_signal(
            barrier, inc=1, device_id={"tok": lax.rem(tok + d, n), "head": lax.axis_index("head")},
            device_id_type=MESH,
        )
    )
    pl.semaphore_wait(barrier, n - 1)
    each(lambda d: meta_copy(d, tok).start())
    table[tok] = meta_ref[...]
    each(lambda d: meta_copy(d, lax.rem(tok + n - d, n)).wait_recv())

    lengths = table[:, 0, :]
    groups = table[:, 1, :]
    slots = jnp.zeros_like(groups)
    for g in range(owner_ref.shape[0]):
        slots = jnp.where(groups == g, owner_ref[g], slots)
    spot = lane_iota((n, LANES))
    slot = jnp.zeros((n, LANES), jnp.int32)
    request = jnp.zeros((n, LANES), jnp.int32)
    end = jnp.zeros((n, 1), jnp.int32)
    for r in range(REQUESTS):
        start = end
        end = start + lengths[:, r:r + 1]
        inside = (spot >= start) & (spot < end)
        slot = jnp.where(inside, slots[:, r:r + 1], slot)
        request = jnp.where(inside, r, request)
    goal = lax.div(slot, TEAM)
    marks = [jnp.where(goal == z, 1.0, 0.0) for z in range(TEAM)]
    hot = jnp.concatenate(marks, axis=0).astype(jnp.bfloat16)
    down = lax.broadcasted_iota(jnp.int32, (LANES, LANES), 0)
    upto = jnp.where(down <= lane_iota((LANES, LANES)), 1.0, 0.0).astype(jnp.bfloat16)
    running = dot_nn(hot, upto)
    totals = dot_nn(hot, jnp.ones((LANES, LANES), jnp.bfloat16))
    m = TEAM * n
    a = lax.broadcasted_iota(jnp.int32, (m, m), 0)
    b = lax.broadcasted_iota(jnp.int32, (m, m), 1)
    earlier = (lax.div(a, TEAM) == lax.div(b, TEAM)) & (b < a)
    before = dot_nn(jnp.where(earlier, 1.0, 0.0).astype(jnp.bfloat16), totals.astype(jnp.bfloat16))
    count = (running + before).astype(jnp.int32)
    code = jnp.zeros((n, LANES), jnp.int32)
    for z in range(TEAM):
        code = jnp.where(goal == z, z * CODE + count[z * n:(z + 1) * n] - 1, code)
    slot = slot - goal * TEAM
    for z in range(TEAM):
        part = slice(z * TEAM, (z + 1) * TEAM)
        slot_ref[z] = slot[part]
        code_ref[z] = code[part]
        req_ref[z] = request[part]
    most = jnp.max(jnp.max(count, axis=0, keepdims=True), axis=1, keepdims=True)
    peak_ref[...] = jnp.broadcast_to(most, peak_ref.shape)

    each(lambda d: meta_copy(d, tok).wait_send())


def pool_kernel(
    scale, cap, slot_ref, code_ref, req_ref, qkv_ref, cache_ref, out_ref, pair_ref,
    pool_ref, cache, kv_ref, mixed, local, outgo, income, result, back, stats, cols, keep, fresh, final, note_out, note_in, notes, pair,
    s1, r1, s2, r2, s3, r3, s4, r4, s5, r5, s6, r6, s7, r7, s8, r8, sl,
):
    level, work, half = place()
    team = 2 * TEAM
    mine = half * TEAM + work
    rows = qkv_ref.shape[1]
    toks = 2 * rows

    def level_id(d):
        return {"tok": lax.rem(level + d, TEAM) * TEAM + work, "head": half}

    width = kv_ref.shape[2]
    groups = fold(cap)
    high_rows = cap // groups

    def query_copy(e, part, landing):
        peer = lax.rem(mine + e, team)
        low, high = (0, FIRST) if part == 0 else (FIRST, BAND)
        return pltpu.make_async_remote_copy(
            src_ref=qkv_ref.at[0, :, band_cols(peer, low, high - low)],
            dst_ref=pool_ref.at[team_rows(landing, rows), low:high],
            send_sem=s8.at[part, e], recv_sem=r8.at[part, e],
            device_id=team_at(peer, level), device_id_type=MESH,
        )

    def forth_copy(d, part):
        span = slice(0, FIRST) if part == 0 else slice(FIRST, BAND)
        return pltpu.make_async_remote_copy(
            src_ref=outgo.at[d, :, span], dst_ref=income.at[d, :, span],
            send_sem=s1.at[part, d], recv_sem=r1.at[part, d],
            device_id=level_id(d), device_id_type=MESH,
        )

    def note_copy(d):
        return pltpu.make_async_remote_copy(
            src_ref=note_out.at[d], dst_ref=note_in.at[d], send_sem=s6.at[d], recv_sem=r6.at[d],
            device_id=level_id(TEAM - d), device_id_type=MESH,
        )

    def half_cols(which):
        return pl.ds(pl.multiple_of(which * width, LANES), width)

    swap = pltpu.make_async_remote_copy(
        src_ref=qkv_ref.at[1:3, :, half_cols(1 - half)], dst_ref=pair.at[1],
        send_sem=s7.at[0], recv_sem=r7.at[0],
        device_id={"tok": level * TEAM + work, "head": 1 - half}, device_id_type=MESH,
    )

    def weave(which, owner):
        where = pl.ds(pl.multiple_of(owner * rows, 16), rows)

        def step(c, carry):
            span = pl.ds(pl.multiple_of(c * LANES, LANES), LANES)
            pair_ref[where, 0, span] = pair[which, 0, :, span]
            pair_ref[where, 1, span] = pair[which, 1, :, span]
            return carry

        lax.fori_loop(0, width // LANES, step, 0)

    def back_copy(d, part):
        span = slice(0, MIDDLE) if part == 0 else slice(MIDDLE, BAND)
        return pltpu.make_async_remote_copy(
            src_ref=result.at[d, :, span], dst_ref=back.at[d, :, span],
            send_sem=s2.at[part, d], recv_sem=r2.at[part, d],
            device_id=level_id(TEAM - d), device_id_type=MESH,
        )

    def cache_copy(e, part, landing):
        peer = lax.rem(work + e, TEAM)
        low, high = (0, FIRST) if part == 0 else (FIRST, BAND)
        return pltpu.make_async_remote_copy(
            src_ref=kv_ref.at[:, :, band_cols(peer, low, high - low)],
            dst_ref=keep.at[landing, :, :, low:high],
            send_sem=s3.at[part, e], recv_sem=r3.at[part, e],
            device_id={"tok": level * TEAM + peer, "head": half}, device_id_type=MESH,
        )

    def fresh_copy(e, landing):
        peer = lax.rem(mine + e, team)
        return pltpu.make_async_remote_copy(
            src_ref=qkv_ref.at[1:3, :, band_cols(peer)],
            dst_ref=fresh.at[:, team_rows(landing, rows), :],
            send_sem=s4.at[e], recv_sem=r4.at[e],
            device_id=team_at(peer, level), device_id_type=MESH,
        )

    def final_copy(e, landing):
        peer = lax.rem(mine + e, team)
        return pltpu.make_async_remote_copy(
            src_ref=final.at[team_rows(peer, rows), :],
            dst_ref=out_ref.at[:, band_cols(landing)],
            send_sem=s5.at[e], recv_sem=r5.at[e],
            device_id=team_at(peer, level), device_id_type=MESH,
        )

    barrier = pltpu.get_barrier_semaphore()
    for e in range(1, team):
        pl.semaphore_signal(barrier, inc=1, device_id=team_at(lax.rem(mine + e, team), level), device_id_type=MESH)
    for d in range(1, TEAM):
        pl.semaphore_signal(barrier, inc=1, device_id=level_id(d), device_id_type=MESH)
    bring = pltpu.make_async_copy(cache_ref.at[0], cache, sl.at[3])
    bring.start()
    own_query = pltpu.make_async_copy(
        qkv_ref.at[0, :, band_cols(mine)], pool_ref.at[team_rows(mine, rows), :], sl.at[4]
    )
    own_query.start()
    own_fresh = pltpu.make_async_copy(
        qkv_ref.at[1:3, :, band_cols(mine)], fresh.at[:, team_rows(mine, rows), :], sl.at[1]
    )
    own_fresh.start()
    own_pair = pltpu.make_async_copy(qkv_ref.at[1:3, :, half_cols(half)], pair.at[0], sl.at[2])
    own_pair.start()
    pl.semaphore_wait(barrier, team - 1 + TEAM - 1)
    for part in range(2):
        for e in range(1, team):
            query_copy(e, part, mine).start()
    bring.wait()

    def split(c, carry):
        span = pl.ds(pl.multiple_of(c * LANES, LANES), LANES)
        kv_ref[0, :, span] = cache[:, 0, span]
        kv_ref[1, :, span] = cache[:, 1, span]
        return carry

    lax.fori_loop(0, width // LANES, split, 0)
    for part in range(2):
        for e in range(1, TEAM):
            cache_copy(e, part, work).start()
    own_cache = pltpu.make_async_copy(kv_ref.at[:, :, band_cols(work)], keep.at[work], sl.at[0])
    own_cache.start()
    own_query.wait()

    def flat(ref, z):
        block = ref[z]
        return jnp.concatenate([block[i:i + 1] for i in range(TEAM)], axis=1)

    down = lax.broadcasted_iota(jnp.int32, (cap, TEAM * toks), 0)
    code = flat(code_ref, level)

    def send(d, part):
        low, high = (0, FIRST) if part == 0 else (FIRST, BAND)
        goal = lax.rem(level + d, TEAM)
        pick = jnp.where(down == code - goal * CODE, 1.0, 0.0).astype(jnp.bfloat16)
        packed = dot_nn(pick, pool_ref[:, low:high]).astype(jnp.bfloat16)
        if d:
            outgo[d, :, low:high] = packed
            forth_copy(d, part).start()
        else:
            income[0, :, low:high] = packed

    for part in range(2):
        for e in range(1, team):
            query_copy(e, part, lax.rem(mine + team - e, team)).wait_recv()
        for d in (2, 3, 1):
            send(d, part)
    swap.start()
    for part in range(2):
        send(0, part)
    for d in range(TEAM):
        origin = lax.rem(level + TEAM - d, TEAM)
        hit = down == flat(code_ref, origin) - level * CODE
        seats = flat(slot_ref, origin).astype(jnp.float32)
        found = jnp.sum(jnp.where(hit, seats, 0.0), axis=1, keepdims=True)
        cols[d] = jnp.broadcast_to(found, (cap, LANES))
    stats[...] = jnp.zeros_like(stats)
    own_pair.wait()
    weave(0, half)
    own_cache.wait()

    def prefix(part):
        heads = range(2) if part == 0 else range(2, PER)

        def run(d, carry):
            which = cols[d][:, :1]
            lanes = lane_iota((cap, LANES))
            noted = stats[d]
            mixed = {}
            for j in heads:
                low, high = window(j)
                asked = masked_window(income[d, :, low:high], j)
                scores = None
                for s in range(TEAM):
                    part_scores = dot_nt(asked, keep[s, 0, :, low:high])
                    scores = part_scores if s == 0 else jnp.where(which == s, part_scores, scores)
                scores = scores * scale
                top = jnp.max(scores, axis=1, keepdims=True)
                raised = jnp.exp(scores - top)
                total = jnp.sum(raised, axis=1, keepdims=True)
                out = None
                for s in range(TEAM):
                    weights = jnp.where(which == s, raised, 0.0).astype(jnp.bfloat16)
                    term = dot_nn(weights, keep[s, 1, :, low:high])
                    out = term if s == 0 else out + term
                mixed[j] = out / total
                noted = jnp.where(lanes == j, top, noted)
                noted = jnp.where(lanes == PER + j, total, noted)

            def cut(j, tile):
                return mixed[j][:, tile * LANES - window(j)[0]:][:, :LANES]

            tiles = range(4) if part == 0 else range(3, BAND // LANES)
            for tile in tiles:
                first, last = owners_of(tile)
                span = slice(tile * LANES, (tile + 1) * LANES)
                if tile != 3:
                    values = by_tile(tile, lambda j: cut(j, tile)).astype(jnp.bfloat16)
                elif part == 0:
                    values = cut(first, tile).astype(jnp.bfloat16)
                else:
                    edge = last * HD - tile * LANES
                    values = jnp.where(
                        lanes < edge, result[d, :, span].astype(jnp.float32), cut(last, tile)
                    ).astype(jnp.bfloat16)
                result[d, :, span] = values
            stats[d] = noted
            if part == 1:
                folded = noted[:high_rows]
                for k in range(1, groups):
                    folded = folded + pltpu.roll(noted[k * high_rows:(k + 1) * high_rows], k * STAT, 1)
                note_out[d] = folded
            return carry

        lax.fori_loop(0, TEAM, run, 0)

    for part in range(2):
        for d in range(1, TEAM):
            forth_copy(d, part).wait_recv()
        for e in range(1, TEAM):
            cache_copy(e, part, lax.rem(work + TEAM - e, TEAM)).wait_recv()
        if part == 1:
            for e in range(1, team):
                fresh_copy(e, mine).start()
        prefix(part)
        for d in (2, 3, 1):
            back_copy(d, part).start()
        if part == 1:
            for d in range(1, TEAM):
                note_copy(d).start()
        else:
            swap.wait_recv()
            weave(1, 1 - half)
    back[0] = result[0]
    note_in[0] = note_out[0]
    own_fresh.wait()
    for e in range(1, team):
        fresh_copy(e, lax.rem(mine + team - e, team)).wait_recv()

    eye = lax.broadcasted_iota(jnp.int32, (toks, toks), 0) == lane_iota((toks, toks))
    causal = lane_iota((toks, toks)) <= lax.broadcasted_iota(jnp.int32, (toks, toks), 0)
    lanes = lane_iota((toks, LANES))

    def column(row):
        return jnp.sum(jnp.where(eye, row, 0.0), axis=1, keepdims=True)

    def suffix(i, carry):
        span = pl.ds(pl.multiple_of(i * toks, toks), toks)
        asks = req_ref[level, pl.ds(i, 1), :].astype(jnp.float32)
        allowed = (column(asks) == asks) & causal
        noted = jnp.zeros((toks, LANES), jnp.float32)
        outs = []
        for j in range(PER):
            low, high = window(j)
            scores = dot_nt(masked_window(pool_ref[span, low:high], j), fresh[0, span, low:high]) * scale
            scores = jnp.where(allowed, scores, -jnp.inf)
            peak = jnp.max(scores, axis=1, keepdims=True)
            raised = jnp.exp(scores - peak)
            total = jnp.sum(raised, axis=1, keepdims=True)
            outs.append(dot_nn(raised.astype(jnp.bfloat16), fresh[1, span, low:high]))
            noted = jnp.where(lanes == j, peak, noted)
            noted = jnp.where(lanes == PER + j, total, noted)
        for tile in range(BAND // LANES):
            mixed[span, tile * LANES:(tile + 1) * LANES] = by_tile(
                tile, lambda j: outs[j][:, tile * LANES - window(j)[0]:][:, :LANES]
            )
        local[span, :] = noted
        return carry

    lax.fori_loop(0, TEAM, suffix, 0)
    for part in range(2):
        for d in range(1, TEAM):
            back_copy(d, part).wait_recv()
    for d in range(1, TEAM):
        note_copy(d).wait_recv()
    for d in range(TEAM):
        block = note_in[d]
        turned = [block] + [pltpu.roll(block, LANES - k * STAT, 1) for k in range(1, groups)]
        full = jnp.where(lane_iota((cap, LANES)) < STAT, jnp.concatenate(turned, axis=0), 0.0)
        high = full.astype(jnp.bfloat16).astype(jnp.float32)
        rest = full - high
        mid = rest.astype(jnp.bfloat16).astype(jnp.float32)
        notes[d] = (high + pltpu.roll(mid, STAT, 1) + pltpu.roll(rest - mid, 2 * STAT, 1)).astype(jnp.bfloat16)

    def finish(turn, carry):
        k = lax.rem(turn + 1, TEAM)
        i = lax.rem(work + k, TEAM)
        span = pl.ds(pl.multiple_of(i * toks, toks), toks)
        codes = code_ref[level, pl.ds(i, 1), :]
        goal = lax.div(codes, CODE)
        seat = lax.rem(goal - level + TEAM, TEAM) * cap + (codes - goal * CODE)
        seat = column(seat.astype(jnp.float32)).astype(jnp.int32)
        pick = jnp.where(lane_iota((toks, TEAM * cap)) == seat, 1.0, 0.0).astype(jnp.bfloat16)
        packed = dot_nn(pick, notes[...].reshape(TEAM * cap, LANES))
        prior = (packed + pltpu.roll(packed, LANES - STAT, 1)) + pltpu.roll(packed, LANES - 2 * STAT, 1)
        ready = dot_nn(pick, back[...].reshape(TEAM * cap, BAND))
        noted = local[span, :]
        top = jnp.maximum(prior, noted)
        first = pltpu.roll(prior, LANES - PER, 1) * jnp.exp(prior - top)
        second = jnp.exp(noted - top)
        below = first + second * pltpu.roll(noted, LANES - PER, 1)
        wp = first / below
        ws = second / below
        for tile in range(BAND // LANES):
            at = slice(tile * LANES, (tile + 1) * LANES)
            values = (
                by_tile(tile, lambda j: wp[:, j:j + 1]) * ready[:, at]
                + by_tile(tile, lambda j: ws[:, j:j + 1]) * mixed[span, at]
            )
            final[span, at] = values.astype(jnp.bfloat16)

        @pl.when(k > 0)
        def _():
            final_copy(k, mine).start()

        final_copy(k + TEAM, mine).start()
        return carry

    lax.fori_loop(0, TEAM, finish, 0)
    out_ref[:, band_cols(mine)] = final[team_rows(mine, rows), :]
    for e in range(1, team):
        final_copy(e, lax.rem(mine + team - e, team)).wait_recv()
    for d in range(1, TEAM):
        note_copy(d).wait_send()
        for part in range(2):
            forth_copy(d, part).wait_send()
            back_copy(d, part).wait_send()
    for e in range(1, TEAM):
        for part in range(2):
            cache_copy(e, part, work).wait_send()
    swap.wait_send()
    for part in range(2):
        for e in range(1, team):
            query_copy(e, part, mine).wait_send()
    for e in range(1, team):
        fresh_copy(e, mine).wait_send()
        final_copy(e, mine).wait_send()


REQUESTS = 8


def pooled_device(qkv, prefix_cache, suffix_lengths, request_groups, prefix_owner):
    n_head = lax.axis_size("head")
    n_tok = lax.axis_size("tok")
    here = qkv.shape[0]
    width = qkv.shape[2] // n_head
    toks = here * n_head
    scale = 1.0 / math.sqrt(HD)
    past = prefix_cache.shape[1]
    planes = jnp.transpose(qkv, (1, 0, 2))
    meta = jnp.pad(jnp.concatenate([suffix_lengths, request_groups], 0), ((0, 6), (0, LANES - suffix_lengths.shape[1])))
    vmem = pl.BlockSpec(memory_space=pltpu.VMEM)
    smem = pl.BlockSpec(memory_space=pltpu.SMEM)
    hbm = pl.BlockSpec(memory_space=pl.ANY)
    dma = pltpu.SemaphoreType.DMA
    table = jax.ShapeDtypeStruct((TEAM, TEAM, LANES), jnp.int32)

    slot, code, request, peak = pl.pallas_call(
        tables_kernel,
        out_shape=[table, table, table, jax.ShapeDtypeStruct((8, LANES), jnp.int32)],
        in_specs=[vmem, smem],
        out_specs=[vmem] * 4,
        scratch_shapes=[pltpu.VMEM((n_tok, 8, LANES), jnp.int32), dma((n_tok,)), dma((n_tok,))],
        compiler_params=pltpu.CompilerParams(
            collective_id=0, has_side_effects=True, vmem_limit_bytes=8 * 1024 * 1024
        ),
        name="tables",
    )(meta, prefix_owner)

    def pooled(cap, number):
        def call(slot, code, request, planes, cache):
            return pl.pallas_call(
                functools.partial(pool_kernel, scale, cap),
                out_shape=[
                    jax.ShapeDtypeStruct((here, n_head * width), jnp.bfloat16),
                    jax.ShapeDtypeStruct((toks, 2, width), jnp.bfloat16),
                ],
                in_specs=[vmem, vmem, vmem, hbm, hbm],
                out_specs=[vmem] * 2,
                scratch_shapes=[
                    pltpu.VMEM((TEAM * toks, BAND), jnp.bfloat16),
                    pltpu.VMEM((past, 2, width), jnp.bfloat16),
                    pltpu.VMEM((2, past, width), jnp.bfloat16),
                    pltpu.VMEM((TEAM * toks, BAND), jnp.float32),
                    pltpu.VMEM((TEAM * toks, LANES), jnp.float32),
                    pltpu.VMEM((TEAM, cap, BAND), jnp.bfloat16),
                    pltpu.VMEM((TEAM, cap, BAND), jnp.bfloat16),
                    pltpu.VMEM((TEAM, cap, BAND), jnp.bfloat16),
                    pltpu.VMEM((TEAM, cap, BAND), jnp.bfloat16),
                    pltpu.VMEM((TEAM, cap, LANES), jnp.float32),
                    pltpu.VMEM((TEAM, cap, LANES), jnp.float32),
                    pltpu.VMEM((TEAM, 2, past, BAND), jnp.bfloat16),
                    pltpu.VMEM((2, TEAM * toks, BAND), jnp.bfloat16),
                    pltpu.VMEM((TEAM * toks, BAND), jnp.bfloat16),
                    pltpu.VMEM((TEAM, cap // fold(cap), LANES), jnp.float32),
                    pltpu.VMEM((TEAM, cap // fold(cap), LANES), jnp.float32),
                    pltpu.VMEM((TEAM, cap, LANES), jnp.bfloat16),
                    pltpu.VMEM((2, 2, here, width), jnp.bfloat16),
                    dma((2, TEAM)), dma((2, TEAM)), dma((2, TEAM)), dma((2, TEAM)),
                    dma((2, TEAM)), dma((2, TEAM)), dma((2 * TEAM,)), dma((2 * TEAM,)),
                    dma((2 * TEAM,)), dma((2 * TEAM,)), dma((TEAM,)), dma((TEAM,)),
                    dma((1,)), dma((1,)), dma((2, 2 * TEAM)), dma((2, 2 * TEAM)), dma((5,)),
                ],
                compiler_params=pltpu.CompilerParams(
                    collective_id=number, has_side_effects=True, vmem_limit_bytes=52 * 1024 * 1024
                ),
                name="pooled",
            )(slot, code, request, planes, cache)

        return call

    most = peak[0, 0]
    index = sum((most > cap).astype(jnp.int32) for cap in CAPS[:-1])
    return lax.switch(
        index, [pooled(cap, 1 + i) for i, cap in enumerate(CAPS)], slot, code, request, planes, prefix_cache
    )


def solution(mesh):
    in_specs = (
        P(("tok", "head"), None, None),
        P("tok", None, None, "head"),
        P("tok", None),
        P("tok", None),
        P(),
    )
    out_specs = (P(("tok", "head"), None), P("tok", None, "head"))
    pooled = mesh.shape["tok"] == TEAM * TEAM and BAND * TEAM * mesh.shape["head"] == FEATURES
    body = pooled_device if pooled else generic_device
    return jax.shard_map(
        body, mesh=mesh, in_specs=in_specs, out_specs=out_specs, check_vma=False
    )
```

```python
import functools
import math

import jax
import jax.numpy as jnp
from jax import lax
from jax.experimental import pallas as pl
from jax.experimental.pallas import tpu as pltpu
from jax.sharding import PartitionSpec as P

HD = 224
LANES = 128
BAND = math.lcm(HD, LANES)
PER = BAND // HD
LSPLIT = 16
PIECE = 2 * LSPLIT


def window(j):
    low = j * HD // LANES * LANES
    high = -(-(j + 1) * HD // LANES) * LANES
    return low, high


def owners_of(tile):
    first = tile * LANES // HD
    last = ((tile + 1) * LANES - 1) // HD
    return first, last


def lane_iota(shape):
    return lax.broadcasted_iota(jnp.int32, shape, len(shape) - 1)


def by_tile(tile, pick):
    first, last = owners_of(tile)
    left = pick(first)
    if first == last:
        return left
    right = pick(last)
    edge = last * HD - tile * LANES
    return jnp.where(lane_iota((right.shape[0], LANES)) < edge, left, right)


def masked_query(query, j):
    low, high = window(j)
    cols = lane_iota((query.shape[0], high - low)) + low
    keep = (cols >= j * HD) & (cols < (j + 1) * HD)
    return jnp.where(keep, query[:, low:high], jnp.zeros((), query.dtype))


def dot_nt(a, b):
    return lax.dot_general(a, b, (((1,), (1,)), ((), ())), preferred_element_type=jnp.float32)


def dot_nn(a, b):
    return lax.dot_general(a, b, (((1,), (0,)), ((), ())), preferred_element_type=jnp.float32)


def spread_kernel(target_ref, query_ref, out_ref):
    rows = out_ref.shape[0]
    toks = target_ref.shape[1]
    place = lax.broadcasted_iota(jnp.int32, (rows, toks), 0)
    pick = jnp.where(place == target_ref[...], 1.0, 0.0).astype(jnp.bfloat16)
    out_ref[...] = dot_nn(pick, query_ref[...]).astype(jnp.bfloat16)


def attend(query, keys, values, allowed, scale, normalise, put, stats_ref, band=None):
    band = pl.program_id(0) if band is None else band
    rows = query.shape[0]
    lanes = lane_iota((rows, LANES))

    if isinstance(band, int):
        stats = jnp.zeros_like(stats_ref) if band == 0 else stats_ref[...]
    else:

        @pl.when(band == 0)
        def _():
            stats_ref[...] = jnp.zeros_like(stats_ref)

        stats = stats_ref[...]
    mixed = []
    for j in range(PER):
        low, high = window(j)
        scores = dot_nt(masked_query(query, j), keys[:, low:high]) * scale
        if allowed is not None:
            scores = jnp.where(allowed, scores, -jnp.inf)
        peak = jnp.max(scores, axis=1, keepdims=True)
        raised = jnp.exp(scores - peak)
        total = jnp.sum(raised, axis=1, keepdims=True)
        out = dot_nn(raised.astype(jnp.bfloat16), values[:, low:high])
        if normalise:
            out = out / total
        mixed.append(out)
        head = band * PER + j
        stats = jnp.where(lanes == head, peak, stats)
        stats = jnp.where(lanes == head + LSPLIT, total, stats)
    stats_ref[...] = stats
    for tile in range(BAND // LANES):
        put(tile, by_tile(tile, lambda j: mixed[j][:, tile * LANES - window(j)[0]:][:, :LANES]))


def prefix_kernel(scale, query_ref, key_ref, value_ref, out_ref, stats_ref):
    band = pl.program_id(0)
    bands = pl.num_programs(0)
    width = out_ref.shape[1] - LANES

    def put(tile, cols):
        at = pl.multiple_of(band * BAND + tile * LANES, LANES)
        out_ref[:, pl.ds(at, LANES)] = cols.astype(out_ref.dtype)

    attend(query_ref[...], key_ref[...], value_ref[...], None, scale, True, put, stats_ref)

    @pl.when(band == bands - 1)
    def _():
        full = stats_ref[...]
        high = full.astype(jnp.bfloat16).astype(jnp.float32)
        rest = full - high
        mid = rest.astype(jnp.bfloat16).astype(jnp.float32)
        low = rest - mid
        packed = high + pltpu.roll(mid, PIECE, 1) + pltpu.roll(low, 2 * PIECE, 1)
        out_ref[:, width:] = packed.astype(out_ref.dtype)


def suffix_kernel(scale, reqc_ref, reqr_ref, query_ref, key_ref, value_ref, out_ref, stats_ref):
    toks = query_ref.shape[0]
    shape = (toks, toks)
    allowed = (reqc_ref[...] == reqr_ref[...]) & (
        lax.broadcasted_iota(jnp.int32, shape, 1) <= lax.broadcasted_iota(jnp.int32, shape, 0)
    )

    def put(tile, cols):
        out_ref[:, tile * LANES:(tile + 1) * LANES] = cols

    keys = key_ref[...].reshape(toks, BAND)
    values = value_ref[...].reshape(toks, BAND)
    attend(query_ref[...], keys, values, allowed, scale, False, put, stats_ref)


def merge_kernel(target_ref, back_ref, pstats_ref, mixed_ref, sstats_ref, out_ref):
    band = pl.program_id(0)
    rows = back_ref.shape[0]
    toks = target_ref.shape[0]
    place = lane_iota((toks, rows))
    pick = jnp.where(place == target_ref[...], 1.0, 0.0).astype(jnp.bfloat16)
    packed = dot_nn(pick, pstats_ref[...])
    prefix = (packed + pltpu.roll(packed, LANES - PIECE, 1)) + pltpu.roll(
        packed, LANES - 2 * PIECE, 1
    )
    suffix = sstats_ref[...]
    top = jnp.maximum(prefix, suffix)
    first = pltpu.roll(prefix, LANES - LSPLIT, 1) * jnp.exp(prefix - top)
    second = jnp.exp(suffix - top)
    below = first + second * pltpu.roll(suffix, LANES - LSPLIT, 1)
    wp = first / below
    ws = second / below
    lanes = lane_iota((toks, LANES))

    def column(weights, j):
        return jnp.sum(jnp.where(lanes == band * PER + j, weights, 0.0), axis=1, keepdims=True)

    cp = [column(wp, j) for j in range(PER)]
    cs = [column(ws, j) for j in range(PER)]
    for tile in range(BAND // LANES):
        cols = slice(tile * LANES, (tile + 1) * LANES)
        back = dot_nn(pick, back_ref[:, cols])
        merged = by_tile(tile, lambda j: cp[j]) * back + by_tile(tile, lambda j: cs[j]) * mixed_ref[:, cols]
        out_ref[:, cols] = merged.astype(out_ref.dtype)


def whole_block(array):
    return pl.BlockSpec(array.shape, lambda g: (0,) * array.ndim)


def band_block(rows, off=0):
    return pl.BlockSpec((rows, BAND), lambda g: (0, g + off))


def cost(flops, moved):
    return pl.CostEstimate(flops=flops, bytes_accessed=moved, transcendentals=0)


def room():
    return pltpu.CompilerParams(vmem_limit_bytes=48 * 1024 * 1024)


def exchange(x, axis):
    return lax.all_to_all(x, axis, split_axis=0, concat_axis=0, tiled=True)


def shift_exchange(x, axis):
    n = lax.axis_size(axis)
    me = lax.axis_index(axis)
    parts = [lax.dynamic_index_in_dim(x, me, 0, keepdims=False)]
    for d in range(1, n):
        ring = [(i, (i + d) % n) for i in range(n)]
        sent = lax.dynamic_index_in_dim(x, lax.rem(me + d, n), 0, keepdims=False)
        parts.append(lax.ppermute(sent, axis, ring))
    out = []
    for source in range(n):
        picked = parts[0]
        for d in range(1, n):
            picked = jnp.where(lax.rem(me + n - source, n) == d, parts[d], picked)
        out.append(picked)
    return jnp.stack(out)


def generic_device(qkv, prefix_cache, suffix_lengths, request_groups, prefix_owner):
    n_head = lax.axis_size("head")
    n_tok = lax.axis_size("tok")
    here = qkv.shape[0]
    width = qkv.shape[2] // n_head
    toks = here * n_head
    scale = 1.0 / math.sqrt(HD)
    bands = width // BAND
    parts = 1
    each = bands // parts
    cols = each * BAND
    capacity = 3 * toks // n_tok
    rows = n_tok * capacity
    planes = jnp.transpose(qkv, (1, 0, 2)).reshape(3, here, n_head, width)
    queries = [
        exchange(
            jnp.stack([qkv[:, 0, h * width:(h + 1) * width] for h in range(n_head)]), "head"
        ).reshape(toks, cols)
        for p in range(parts)
    ]
    kv_send = jnp.transpose(planes[1:], (2, 0, 1, 3))

    lengths = suffix_lengths[0]
    groups = request_groups[0]
    requests = lengths.shape[0]
    ends = jnp.sum(jnp.where(jnp.arange(requests)[:, None] <= jnp.arange(requests)[None, :], lengths[:, None], 0), axis=0)
    starts = ends - lengths
    slots = jnp.sum(jnp.where(groups[:, None] == jnp.arange(n_tok)[None, :], prefix_owner[None, :], 0), axis=1)
    position = jnp.arange(toks, dtype=jnp.int32)
    request = jnp.sum((position[:, None] >= ends[None, :]).astype(jnp.int32), axis=1)
    base = slots * capacity - starts
    inside = request[:, None] == jnp.arange(requests, dtype=jnp.int32)[None, :]
    target = (position + jnp.sum(jnp.where(inside, base[None, :], 0), axis=1)).astype(jnp.int32)
    target_row = target[None, :]
    target_col = target[:, None]
    reqc, reqr = request[:, None], request[None, :]

    prefix_len = prefix_cache.shape[1]
    queries[0], cache_keys, cache_values = lax.optimization_barrier(
        (queries[0], prefix_cache[0, :, 0], prefix_cache[0, :, 1])
    )
    received = []
    for p in range(parts):
        outgoing = pl.pallas_call(
            spread_kernel,
            grid=(each,),
            out_shape=jax.ShapeDtypeStruct((rows, cols), jnp.bfloat16),
            in_specs=[whole_block(target_row), band_block(toks)],
            out_specs=band_block(rows),
            cost_estimate=cost(2 * rows * toks * cols, 2 * (rows + toks) * cols),
            compiler_params=room(),
            name="spread",
        )(target_row, queries[p])
        if p == 0:
            outgoing, kv_send = lax.optimization_barrier((outgoing, kv_send))
        received.append(exchange(outgoing.reshape(n_tok, capacity, cols), "tok").reshape(rows, cols))
    kv = shift_exchange(kv_send, "head")

    back = []
    for p in range(parts):
        mixed = pl.pallas_call(
            functools.partial(prefix_kernel, scale),
            grid=(each,),
            out_shape=jax.ShapeDtypeStruct((rows, cols + LANES), jnp.bfloat16),
            in_specs=[band_block(rows), band_block(prefix_len, p * each), band_block(prefix_len, p * each)],
            out_specs=pl.BlockSpec((rows, cols + LANES), lambda g: (0, 0)),
            scratch_shapes=[pltpu.VMEM((rows, LANES), jnp.float32)],
            cost_estimate=cost(4 * rows * prefix_len * cols, 4 * (rows + prefix_len) * cols),
            compiler_params=room(),
            name="prefix",
        )(received[p], cache_keys, cache_values)
        back.append(exchange(mixed.reshape(n_tok, capacity, cols + LANES), "tok").reshape(rows, cols + LANES))

    finals = []
    for p in range(parts):
        key_spec = pl.BlockSpec((n_head, None, here, BAND), lambda g, p=p: (0, 0, 0, g + p * each))
        value_spec = pl.BlockSpec((n_head, None, here, BAND), lambda g, p=p: (0, 1, 0, g + p * each))
        mixed_s, stats_s = pl.pallas_call(
            functools.partial(suffix_kernel, scale),
            grid=(each,),
            out_shape=[
                jax.ShapeDtypeStruct((toks, cols), jnp.float32),
                jax.ShapeDtypeStruct((toks, LANES), jnp.float32),
            ],
            in_specs=[whole_block(reqc), whole_block(reqr), band_block(toks), key_spec, value_spec],
            out_specs=[band_block(toks), pl.BlockSpec((toks, LANES), lambda g: (0, 0))],
            cost_estimate=cost(4 * toks * toks * cols, 10 * toks * cols),
            compiler_params=room(),
            name="suffix",
        )(reqc, reqr, queries[p], kv, kv)
        merged = pl.pallas_call(
            merge_kernel,
            grid=(each,),
            out_shape=jax.ShapeDtypeStruct((toks, cols), jnp.bfloat16),
            in_specs=[
                whole_block(target_col),
                band_block(rows),
                pl.BlockSpec((rows, LANES), lambda g: (0, cols // LANES)),
                band_block(toks),
                whole_block(stats_s),
            ],
            out_specs=band_block(toks),
            cost_estimate=cost(2 * rows * toks * cols, 2 * (rows + 3 * toks) * cols),
            compiler_params=room(),
            name="merge",
        )(target_col, back[p], back[p], mixed_s, stats_s)
        finals.append(exchange(merged.reshape(n_head, here, cols), "head"))
    attended = jnp.transpose(jnp.stack(finals, axis=2), (1, 0, 2, 3)).reshape(here, n_head * width)
    suffix_cache = jnp.transpose(kv, (0, 2, 1, 3)).reshape(toks, 2, width)
    return (attended, suffix_cache)


TEAM = 4
FEATURES = 7168
CODE = 1024
FAR = (176, 192, 208, 240)
NEAR = 256
MOST = 384
FIRST = 512
MIDDLE = 384
STAT = 8
MESH = pl.DeviceIdType.MESH


def place():
    tok = lax.axis_index("tok")
    half = lax.axis_index("head")
    return lax.div(tok, TEAM), lax.rem(tok, TEAM), half


def team_at(member, level):
    return {"tok": level * TEAM + lax.rem(member, TEAM), "head": lax.div(member, TEAM)}


def team_rows(member, rows):
    at = (lax.rem(member, TEAM) * 2 + lax.div(member, TEAM)) * rows
    return pl.ds(pl.multiple_of(at, 16), rows)


def band_cols(member, low=0, wide=BAND):
    return pl.ds(pl.multiple_of(member * BAND + low, LANES), wide)


def layout(sizes):
    starts = [sum(sizes[:d]) for d in range(TEAM)]
    total = sum(sizes)
    return starts, total, -(-total // (16 * TEAM)) * 16


def note_layout(sizes):
    high = [-(-size // LANES) * STAT for size in sizes]
    return [sum(high[:d]) for d in range(TEAM)], high


def masked_window(query, j):
    low, high = window(j)
    cols = lane_iota((query.shape[0], high - low)) + low
    keep = (cols >= j * HD) & (cols < (j + 1) * HD)
    return jnp.where(keep, query, jnp.zeros((), query.dtype))


def tables_kernel(meta_ref, owner_ref, slot_ref, code_ref, req_ref, peak_ref, table, sm, rm):
    tok = lax.axis_index("tok")
    n = lax.axis_size("tok")

    def meta_copy(d, landing):
        return pltpu.make_async_remote_copy(
            src_ref=meta_ref,
            dst_ref=table.at[landing],
            send_sem=sm.at[d],
            recv_sem=rm.at[d],
            device_id={"tok": lax.rem(tok + d, n), "head": lax.axis_index("head")},
            device_id_type=MESH,
        )

    def each(body):
        def step(d, carry):
            body(d)
            return carry

        lax.fori_loop(1, n, step, 0)

    barrier = pltpu.get_barrier_semaphore()
    each(
        lambda d: pl.semaphore_signal(
            barrier, inc=1, device_id={"tok": lax.rem(tok + d, n), "head": lax.axis_index("head")},
            device_id_type=MESH,
        )
    )
    pl.semaphore_wait(barrier, n - 1)
    each(lambda d: meta_copy(d, tok).start())
    table[tok] = meta_ref[...]
    each(lambda d: meta_copy(d, lax.rem(tok + n - d, n)).wait_recv())

    lengths = table[:, 0, :]
    groups = table[:, 1, :]
    slots = jnp.zeros_like(groups)
    for g in range(owner_ref.shape[0]):
        slots = jnp.where(groups == g, owner_ref[g], slots)
    spot = lane_iota((n, LANES))
    slot = jnp.zeros((n, LANES), jnp.int32)
    request = jnp.zeros((n, LANES), jnp.int32)
    end = jnp.zeros((n, 1), jnp.int32)
    for r in range(REQUESTS):
        start = end
        end = start + lengths[:, r:r + 1]
        inside = (spot >= start) & (spot < end)
        slot = jnp.where(inside, slots[:, r:r + 1], slot)
        request = jnp.where(inside, r, request)
    goal = lax.div(slot, TEAM)
    marks = [jnp.where(goal == z, 1.0, 0.0) for z in range(TEAM)]
    hot = jnp.concatenate(marks, axis=0).astype(jnp.bfloat16)
    down = lax.broadcasted_iota(jnp.int32, (LANES, LANES), 0)
    upto = jnp.where(down <= lane_iota((LANES, LANES)), 1.0, 0.0).astype(jnp.bfloat16)
    running = dot_nn(hot, upto)
    totals = dot_nn(hot, jnp.ones((LANES, LANES), jnp.bfloat16))
    m = TEAM * n
    a = lax.broadcasted_iota(jnp.int32, (m, m), 0)
    b = lax.broadcasted_iota(jnp.int32, (m, m), 1)
    earlier = (lax.div(a, TEAM) == lax.div(b, TEAM)) & (b < a)
    before = dot_nn(jnp.where(earlier, 1.0, 0.0).astype(jnp.bfloat16), totals.astype(jnp.bfloat16))
    count = (running + before).astype(jnp.int32)
    code = jnp.zeros((n, LANES), jnp.int32)
    for z in range(TEAM):
        code = jnp.where(goal == z, z * CODE + count[z * n:(z + 1) * n] - 1, code)
    slot = slot - goal * TEAM
    for z in range(TEAM):
        part = slice(z * TEAM, (z + 1) * TEAM)
        slot_ref[z] = slot[part]
        code_ref[z] = code[part]
        req_ref[z] = request[part]
    aim = lax.div(lax.broadcasted_iota(jnp.int32, (m, LANES), 0), n)
    source = lax.div(lax.rem(lax.broadcasted_iota(jnp.int32, (m, LANES), 0), n), TEAM)
    far = lax.div(aim, 2) != lax.div(source, 2)
    need = jnp.where(far, count, jnp.where(count > NEAR, MOST, 0))
    most = jnp.max(jnp.max(need, axis=0, keepdims=True), axis=1, keepdims=True)
    peak_ref[...] = jnp.broadcast_to(most, peak_ref.shape)

    each(lambda d: meta_copy(d, tok).wait_send())


def pool_kernel(
    scale, sizes, slot_ref, code_ref, req_ref, qkv_ref, cache_ref, out_ref, pair_ref,
    pool_ref, cache, kv_ref, mixed, local, outgo, income, result, back, stats, cols, keep, fresh, final,
    note_out, note_in, notes, picks, pair,
    s1, r1, s2, r2, s3, r3, s4, r4, s5, r5, s6, r6, s7, r7, s8, r8, sl,
):
    level, work, half = place()
    team = 2 * TEAM
    mine = half * TEAM + work
    rows = qkv_ref.shape[1]
    toks = 2 * rows
    width = kv_ref.shape[2]
    starts, total_rows, block = layout(sizes)
    note_starts, note_sizes = note_layout(sizes)
    partners = (
        level, level + 1 - 2 * lax.rem(level, 2), lax.rem(level + 2, TEAM), TEAM - 1 - level,
    )
    order = (2, 3, 1)
    inner = ((0, FIRST), (FIRST, BAND))
    outer = ((0, MIDDLE), (MIDDLE, BAND))

    def rows_of(d):
        return slice(starts[d], starts[d] + sizes[d])

    def note_rows(d):
        return slice(note_starts[d], note_starts[d] + note_sizes[d])

    def level_id(d):
        return {"tok": partners[d] * TEAM + work, "head": half}

    def query_copy(e, part, landing):
        peer = lax.rem(mine + e, team)
        low, high = inner[part]
        return pltpu.make_async_remote_copy(
            src_ref=qkv_ref.at[0, :, band_cols(peer, low, high - low)],
            dst_ref=pool_ref.at[team_rows(landing, rows), low:high],
            send_sem=s8.at[part, e], recv_sem=r8.at[part, e],
            device_id=team_at(peer, level), device_id_type=MESH,
        )

    def forth_copy(d, part):
        span = slice(*inner[part])
        return pltpu.make_async_remote_copy(
            src_ref=outgo.at[rows_of(d), span], dst_ref=income.at[rows_of(d), span],
            send_sem=s1.at[part, d], recv_sem=r1.at[part, d],
            device_id=level_id(d), device_id_type=MESH,
        )

    def back_copy(d, part):
        span = slice(*outer[part])
        return pltpu.make_async_remote_copy(
            src_ref=result.at[rows_of(d), span], dst_ref=back.at[rows_of(d), span],
            send_sem=s2.at[part, d], recv_sem=r2.at[part, d],
            device_id=level_id(d), device_id_type=MESH,
        )

    def note_copy(d, part):
        return pltpu.make_async_remote_copy(
            src_ref=note_out.at[part, note_rows(d), :], dst_ref=note_in.at[part, note_rows(d), :],
            send_sem=s6.at[part, d], recv_sem=r6.at[part, d],
            device_id=level_id(d), device_id_type=MESH,
        )

    def cache_copy(e, part, landing):
        peer = lax.rem(work + e, TEAM)
        low, high = inner[part]
        return pltpu.make_async_remote_copy(
            src_ref=kv_ref.at[:, :, band_cols(peer, low, high - low)],
            dst_ref=keep.at[landing, :, :, low:high],
            send_sem=s3.at[part, e], recv_sem=r3.at[part, e],
            device_id={"tok": level * TEAM + peer, "head": half}, device_id_type=MESH,
        )

    def fresh_copy(e, part, landing):
        peer = lax.rem(mine + e, team)
        low, high = inner[part]
        return pltpu.make_async_remote_copy(
            src_ref=qkv_ref.at[1:3, :, band_cols(peer, low, high - low)],
            dst_ref=fresh.at[:, team_rows(landing, rows), low:high],
            send_sem=s4.at[part, e], recv_sem=r4.at[part, e],
            device_id=team_at(peer, level), device_id_type=MESH,
        )

    def final_copy(e, part, landing):
        peer = lax.rem(mine + e, team)
        low, high = outer[part]
        return pltpu.make_async_remote_copy(
            src_ref=final.at[team_rows(peer, rows), low:high],
            dst_ref=out_ref.at[:, band_cols(landing, low, high - low)],
            send_sem=s5.at[part, e], recv_sem=r5.at[part, e],
            device_id=team_at(peer, level), device_id_type=MESH,
        )

    def half_cols(which):
        return pl.ds(pl.multiple_of(which * width, LANES), width)

    swap = pltpu.make_async_remote_copy(
        src_ref=qkv_ref.at[1:3, :, half_cols(1 - half)], dst_ref=pair.at[1],
        send_sem=s7.at[0], recv_sem=r7.at[0],
        device_id={"tok": level * TEAM + work, "head": 1 - half}, device_id_type=MESH,
    )

    def weave(which, owner):
        where = pl.ds(pl.multiple_of(owner * rows, 16), rows)

        def step(c, carry):
            span = pl.ds(pl.multiple_of(c * LANES, LANES), LANES)
            pair_ref[where, 0, span] = pair[which, 0, :, span]
            pair_ref[where, 1, span] = pair[which, 1, :, span]
            return carry

        lax.fori_loop(0, width // LANES, step, 0)

    barrier = pltpu.get_barrier_semaphore()
    for e in range(1, team):
        pl.semaphore_signal(barrier, inc=1, device_id=team_at(lax.rem(mine + e, team), level), device_id_type=MESH)
    for d in range(1, TEAM):
        pl.semaphore_signal(barrier, inc=1, device_id=level_id(d), device_id_type=MESH)
    bring = pltpu.make_async_copy(cache_ref.at[0], cache, sl.at[3])
    bring.start()
    own_query = pltpu.make_async_copy(
        qkv_ref.at[0, :, band_cols(mine)], pool_ref.at[team_rows(mine, rows), :], sl.at[4]
    )
    own_query.start()
    own_fresh = pltpu.make_async_copy(
        qkv_ref.at[1:3, :, band_cols(mine)], fresh.at[:, team_rows(mine, rows), :], sl.at[1]
    )
    own_fresh.start()
    own_pair = pltpu.make_async_copy(qkv_ref.at[1:3, :, half_cols(half)], pair.at[0], sl.at[2])
    own_pair.start()
    pl.semaphore_wait(barrier, team - 1 + TEAM - 1)
    for part in range(2):
        for e in range(1, team):
            query_copy(e, part, mine).start()
    bring.wait()

    def split(c, carry):
        span = pl.ds(pl.multiple_of(c * LANES, LANES), LANES)
        kv_ref[0, :, span] = cache[:, 0, span]
        kv_ref[1, :, span] = cache[:, 1, span]
        return carry

    lax.fori_loop(0, width // LANES, split, 0)
    for part in range(2):
        for e in range(1, TEAM):
            cache_copy(e, part, work).start()
    own_cache = pltpu.make_async_copy(kv_ref.at[:, :, band_cols(work)], keep.at[work], sl.at[0])
    own_cache.start()
    own_query.wait()

    def flat(ref, z):
        entry = ref[z]
        return jnp.concatenate([entry[i:i + 1] for i in range(TEAM)], axis=1)

    code = flat(code_ref, level)

    def send(d, part):
        low, high = inner[part]
        down = lax.broadcasted_iota(jnp.int32, (sizes[d], TEAM * toks), 0)
        pick = jnp.where(down == code - partners[d] * CODE, 1.0, 0.0).astype(jnp.bfloat16)
        packed = dot_nn(pick, pool_ref[:, low:high]).astype(jnp.bfloat16)
        if d:
            outgo[rows_of(d), low:high] = packed
            forth_copy(d, part).start()
        else:
            income[rows_of(d), low:high] = packed

    for part in range(2):
        for e in range(1, team):
            query_copy(e, part, lax.rem(mine + team - e, team)).wait_recv()
        for d in order:
            send(d, part)
    swap.start()
    for part in range(2):
        send(0, part)
    for d in range(TEAM):
        down = lax.broadcasted_iota(jnp.int32, (sizes[d], TEAM * toks), 0)
        hit = down == flat(code_ref, partners[d]) - level * CODE
        seats = flat(slot_ref, partners[d]).astype(jnp.float32)
        found = jnp.sum(jnp.where(hit, seats, 0.0), axis=1, keepdims=True)
        cols[rows_of(d), :] = jnp.broadcast_to(found, (sizes[d], LANES))
    spare = TEAM * block - total_rows
    if spare:
        income[total_rows:TEAM * block, :] = jnp.zeros((spare, BAND), jnp.bfloat16)
        cols[total_rows:TEAM * block, :] = jnp.zeros((spare, LANES), jnp.float32)
    stats[...] = jnp.zeros_like(stats)
    own_pair.wait()
    weave(0, half)
    own_cache.wait()

    def heads_of(part):
        return range(2) if part == 0 else range(2, PER)

    def assemble(part, outs, old, keep_tile):
        for tile in range(4) if part == 0 else range(3, BAND // LANES):
            first, last = owners_of(tile)

            def cut(j):
                return outs[j][:, tile * LANES - window(j)[0]:][:, :LANES]

            if tile != 3:
                values = by_tile(tile, cut)
            elif part == 0:
                values = cut(first)
            else:
                before = old(tile)
                values = jnp.where(lane_iota(before.shape) < last * HD - tile * LANES, before, cut(last))
            keep_tile(tile, values)

    def prefix(part):
        def run(b, carry):
            span = pl.ds(pl.multiple_of(b * block, 16), block)
            which = cols[span, :][:, :1]
            lanes = lane_iota((block, LANES))
            noted = stats[span, :]
            outs = {}
            for j in heads_of(part):
                low, high = window(j)
                asked = masked_window(income[span, low:high], j)
                scores = None
                for s in range(TEAM):
                    some = dot_nt(asked, keep[s, 0, :, low:high])
                    scores = some if s == 0 else jnp.where(which == s, some, scores)
                scores = scores * scale
                top = jnp.max(scores, axis=1, keepdims=True)
                raised = jnp.exp(scores - top)
                total = jnp.sum(raised, axis=1, keepdims=True)
                out = None
                for s in range(TEAM):
                    weights = jnp.where(which == s, raised, 0.0).astype(jnp.bfloat16)
                    term = dot_nn(weights, keep[s, 1, :, low:high])
                    out = term if s == 0 else out + term
                outs[j] = out / total
                noted = jnp.where(lanes == j, top, noted)
                noted = jnp.where(lanes == PER + j, total, noted)

            def put(tile, values):
                result[span, tile * LANES:(tile + 1) * LANES] = values.astype(jnp.bfloat16)

            def old(tile):
                return result[span, tile * LANES:(tile + 1) * LANES].astype(jnp.float32)

            assemble(part, outs, old, put)
            stats[span, :] = noted
            return carry

        lax.fori_loop(0, TEAM, run, 0)
        for d in order:
            back_copy(d, part).start()
        for d in range(TEAM):
            high = note_sizes[d]
            folded = None
            for k in range(LANES // STAT):
                piece = stats[starts[d] + k * high:starts[d] + (k + 1) * high, :]
                folded = piece if k == 0 else folded + pltpu.roll(piece, k * STAT, 1)
            note_out[part, note_rows(d), :] = folded
            if d:
                note_copy(d, part).start()

    for part in range(2):
        for d in order:
            forth_copy(d, part).wait_recv()
        for e in range(1, TEAM):
            cache_copy(e, part, lax.rem(work + TEAM - e, TEAM)).wait_recv()
        if part == 1:
            for late in range(2):
                for e in range(1, team):
                    fresh_copy(e, late, mine).start()
        prefix(part)
        if part == 0:
            swap.wait_recv()
            weave(1, 1 - half)
    back[rows_of(0), :] = result[rows_of(0), :]
    note_in[:, note_rows(0), :] = note_out[:, note_rows(0), :]
    own_fresh.wait()

    eye = lax.broadcasted_iota(jnp.int32, (toks, toks), 0) == lane_iota((toks, toks))
    causal = lane_iota((toks, toks)) <= lax.broadcasted_iota(jnp.int32, (toks, toks), 0)
    lanes = lane_iota((toks, LANES))

    def column(row):
        return jnp.sum(jnp.where(eye, row, 0.0), axis=1, keepdims=True)

    def choose(i, carry):
        span = pl.ds(pl.multiple_of(i * toks, toks), toks)
        codes = code_ref[level, pl.ds(i, 1), :]
        goal = lax.div(codes, CODE)
        seat = codes - goal * CODE
        for d in range(1, TEAM):
            seat = jnp.where(goal == partners[d], seat + starts[d], seat)
        seat = column(seat.astype(jnp.float32)).astype(jnp.int32)
        picks[span, :] = jnp.where(lane_iota((toks, total_rows)) == seat, 1.0, 0.0).astype(jnp.bfloat16)
        local[span, :] = jnp.zeros((toks, LANES), jnp.float32)
        return carry

    lax.fori_loop(0, TEAM, choose, 0)

    def suffix(part):
        def run(i, carry):
            span = pl.ds(pl.multiple_of(i * toks, toks), toks)
            asks = req_ref[level, pl.ds(i, 1), :].astype(jnp.float32)
            allowed = (column(asks) == asks) & causal
            noted = local[span, :]
            outs = {}
            for j in heads_of(part):
                low, high = window(j)
                scores = dot_nt(masked_window(pool_ref[span, low:high], j), fresh[0, span, low:high]) * scale
                scores = jnp.where(allowed, scores, -jnp.inf)
                peak = jnp.max(scores, axis=1, keepdims=True)
                raised = jnp.exp(scores - peak)
                total = jnp.sum(raised, axis=1, keepdims=True)
                outs[j] = dot_nn(raised.astype(jnp.bfloat16), fresh[1, span, low:high])
                noted = jnp.where(lanes == j, peak, noted)
                noted = jnp.where(lanes == PER + j, total, noted)

            def put(tile, values):
                mixed[span, tile * LANES:(tile + 1) * LANES] = values

            def old(tile):
                return mixed[span, tile * LANES:(tile + 1) * LANES]

            assemble(part, outs, old, put)
            local[span, :] = noted
            return carry

        lax.fori_loop(0, TEAM, run, 0)

    def unfold(part):
        for d in range(TEAM):
            piece = note_in[part, note_rows(d), :]
            turned = [piece] + [pltpu.roll(piece, LANES - k * STAT, 1) for k in range(1, LANES // STAT)]
            full = jnp.concatenate(turned, axis=0)[:sizes[d]]
            full = jnp.where(lane_iota((sizes[d], LANES)) < STAT, full, 0.0)
            high = full.astype(jnp.bfloat16).astype(jnp.float32)
            rest = full - high
            mid = rest.astype(jnp.bfloat16).astype(jnp.float32)
            packed = high + pltpu.roll(mid, STAT, 1) + pltpu.roll(rest - mid, 2 * STAT, 1)
            notes[rows_of(d), :] = packed.astype(jnp.bfloat16)

    def finish(part):
        low, high = outer[part]

        def run(turn, carry):
            k = lax.rem(turn + 1, TEAM)
            span = pl.ds(pl.multiple_of(lax.rem(work + k, TEAM) * toks, toks), toks)
            pick = picks[span, :]
            packed = dot_nn(pick, notes[...])
            prior = (packed + pltpu.roll(packed, LANES - STAT, 1)) + pltpu.roll(packed, LANES - 2 * STAT, 1)
            ready = dot_nn(pick, back[:, low:high])
            noted = local[span, :]
            top = jnp.maximum(prior, noted)
            first = pltpu.roll(prior, LANES - PER, 1) * jnp.exp(prior - top)
            second = jnp.exp(noted - top)
            below = first + second * pltpu.roll(noted, LANES - PER, 1)
            wp = first / below
            ws = second / below
            for tile in range(low // LANES, high // LANES):
                at = slice(tile * LANES, (tile + 1) * LANES)
                values = (
                    by_tile(tile, lambda j: wp[:, j:j + 1]) * ready[:, tile * LANES - low:][:, :LANES]
                    + by_tile(tile, lambda j: ws[:, j:j + 1]) * mixed[span, at]
                )
                final[span, at] = values.astype(jnp.bfloat16)

            @pl.when(k > 0)
            def _():
                final_copy(k, part, mine).start()

            final_copy(k + TEAM, part, mine).start()
            return carry

        lax.fori_loop(0, TEAM, run, 0)

    for part in range(2):
        for e in range(1, team):
            fresh_copy(e, part, lax.rem(mine + team - e, team)).wait_recv()
        suffix(part)
        for d in order:
            back_copy(d, part).wait_recv()
            note_copy(d, part).wait_recv()
        unfold(part)
        finish(part)
    out_ref[:, band_cols(mine)] = final[team_rows(mine, rows), :]
    for part in range(2):
        for e in range(1, team):
            final_copy(e, part, lax.rem(mine + team - e, team)).wait_recv()
    swap.wait_send()
    for part in range(2):
        for d in range(1, TEAM):
            note_copy(d, part).wait_send()
            forth_copy(d, part).wait_send()
            back_copy(d, part).wait_send()
        for e in range(1, TEAM):
            cache_copy(e, part, work).wait_send()
        for e in range(1, team):
            query_copy(e, part, mine).wait_send()
            fresh_copy(e, part, mine).wait_send()
            final_copy(e, part, mine).wait_send()


REQUESTS = 8


def pooled_device(qkv, prefix_cache, suffix_lengths, request_groups, prefix_owner):
    n_head = lax.axis_size("head")
    n_tok = lax.axis_size("tok")
    here = qkv.shape[0]
    width = qkv.shape[2] // n_head
    toks = here * n_head
    scale = 1.0 / math.sqrt(HD)
    past = prefix_cache.shape[1]
    planes = jnp.transpose(qkv, (1, 0, 2))
    meta = jnp.pad(jnp.concatenate([suffix_lengths, request_groups], 0), ((0, 6), (0, LANES - suffix_lengths.shape[1])))
    vmem = pl.BlockSpec(memory_space=pltpu.VMEM)
    smem = pl.BlockSpec(memory_space=pltpu.SMEM)
    hbm = pl.BlockSpec(memory_space=pl.ANY)
    dma = pltpu.SemaphoreType.DMA
    table = jax.ShapeDtypeStruct((TEAM, TEAM, LANES), jnp.int32)

    slot, code, request, peak = pl.pallas_call(
        tables_kernel,
        out_shape=[table, table, table, jax.ShapeDtypeStruct((8, LANES), jnp.int32)],
        in_specs=[vmem, smem],
        out_specs=[vmem] * 4,
        scratch_shapes=[pltpu.VMEM((n_tok, 8, LANES), jnp.int32), dma((n_tok,)), dma((n_tok,))],
        compiler_params=pltpu.CompilerParams(
            collective_id=0, has_side_effects=True, vmem_limit_bytes=8 * 1024 * 1024
        ),
        name="tables",
    )(meta, prefix_owner)

    def pooled(sizes, number):
        total, block = layout(sizes)[1:]
        marks = sum(note_layout(sizes)[1])
        bf16, f32 = jnp.bfloat16, jnp.float32
        two, team = (2, TEAM), (2, 2 * TEAM)

        def call(slot, code, request, planes, cache):
            return pl.pallas_call(
                functools.partial(pool_kernel, scale, sizes),
                out_shape=[
                    jax.ShapeDtypeStruct((here, n_head * width), bf16),
                    jax.ShapeDtypeStruct((toks, 2, width), bf16),
                ],
                in_specs=[vmem, vmem, vmem, hbm, hbm],
                out_specs=[vmem] * 2,
                scratch_shapes=[
                    pltpu.VMEM((TEAM * toks, BAND), bf16),
                    pltpu.VMEM((past, 2, width), bf16),
                    pltpu.VMEM((2, past, width), bf16),
                    pltpu.VMEM((TEAM * toks, BAND), f32),
                    pltpu.VMEM((TEAM * toks, LANES), f32),
                    pltpu.VMEM((total, BAND), bf16),
                    pltpu.VMEM((TEAM * block, BAND), bf16),
                    pltpu.VMEM((TEAM * block, BAND), bf16),
                    pltpu.VMEM((total, BAND), bf16),
                    pltpu.VMEM((TEAM * block + LANES, LANES), f32),
                    pltpu.VMEM((TEAM * block, LANES), f32),
                    pltpu.VMEM((TEAM, 2, past, BAND), bf16),
                    pltpu.VMEM((2, TEAM * toks, BAND), bf16),
                    pltpu.VMEM((TEAM * toks, BAND), bf16),
                    pltpu.VMEM((2, marks, LANES), f32),
                    pltpu.VMEM((2, marks, LANES), f32),
                    pltpu.VMEM((total, LANES), bf16),
                    pltpu.VMEM((TEAM * toks, total), bf16),
                    pltpu.VMEM((2, 2, here, width), bf16),
                    dma(two), dma(two), dma(two), dma(two), dma(two), dma(two),
                    dma(team), dma(team), dma(team), dma(team), dma(two), dma(two),
                    dma((1,)), dma((1,)), dma(team), dma(team), dma((5,)),
                ],
                compiler_params=pltpu.CompilerParams(
                    collective_id=number, has_side_effects=True, vmem_limit_bytes=52 * 1024 * 1024
                ),
                name="pooled",
            )(slot, code, request, planes, cache)

        return call

    most = peak[0, 0]
    index = sum((most > size).astype(jnp.int32) for size in FAR)
    choices = [(NEAR, NEAR, size, size) for size in FAR] + [(MOST,) * TEAM]
    return lax.switch(
        index, [pooled(sizes, 1 + i) for i, sizes in enumerate(choices)],
        slot, code, request, planes, prefix_cache,
    )


def solution(mesh):
    in_specs = (
        P(("tok", "head"), None, None),
        P("tok", None, None, "head"),
        P("tok", None),
        P("tok", None),
        P(),
    )
    out_specs = (P(("tok", "head"), None), P("tok", None, "head"))
    pooled = mesh.shape["tok"] == TEAM * TEAM and BAND * TEAM * mesh.shape["head"] == FEATURES
    body = pooled_device if pooled else generic_device
    return jax.shard_map(
        body, mesh=mesh, in_specs=in_specs, out_specs=out_specs, check_vma=False
    )
```

```python
import functools
import math

import jax
import jax.numpy as jnp
from jax import lax
from jax.experimental import pallas as pl
from jax.experimental.pallas import tpu as pltpu
from jax.sharding import PartitionSpec as P

HD = 224
LANES = 128
BAND = math.lcm(HD, LANES)
PER = BAND // HD
LSPLIT = 16
PIECE = 2 * LSPLIT


def window(j):
    low = j * HD // LANES * LANES
    high = -(-(j + 1) * HD // LANES) * LANES
    return low, high


def owners_of(tile):
    first = tile * LANES // HD
    last = ((tile + 1) * LANES - 1) // HD
    return first, last


def lane_iota(shape):
    return lax.broadcasted_iota(jnp.int32, shape, len(shape) - 1)


def by_tile(tile, pick):
    first, last = owners_of(tile)
    left = pick(first)
    if first == last:
        return left
    right = pick(last)
    edge = last * HD - tile * LANES
    return jnp.where(lane_iota((right.shape[0], LANES)) < edge, left, right)


def masked_query(query, j):
    low, high = window(j)
    cols = lane_iota((query.shape[0], high - low)) + low
    keep = (cols >= j * HD) & (cols < (j + 1) * HD)
    return jnp.where(keep, query[:, low:high], jnp.zeros((), query.dtype))


def dot_nt(a, b):
    return lax.dot_general(a, b, (((1,), (1,)), ((), ())), preferred_element_type=jnp.float32)


def dot_nn(a, b):
    return lax.dot_general(a, b, (((1,), (0,)), ((), ())), preferred_element_type=jnp.float32)


def spread_kernel(target_ref, query_ref, out_ref):
    rows = out_ref.shape[0]
    toks = target_ref.shape[1]
    place = lax.broadcasted_iota(jnp.int32, (rows, toks), 0)
    pick = jnp.where(place == target_ref[...], 1.0, 0.0).astype(jnp.bfloat16)
    out_ref[...] = dot_nn(pick, query_ref[...]).astype(jnp.bfloat16)


def attend(query, keys, values, allowed, scale, normalise, put, stats_ref, band=None):
    band = pl.program_id(0) if band is None else band
    rows = query.shape[0]
    lanes = lane_iota((rows, LANES))

    if isinstance(band, int):
        stats = jnp.zeros_like(stats_ref) if band == 0 else stats_ref[...]
    else:

        @pl.when(band == 0)
        def _():
            stats_ref[...] = jnp.zeros_like(stats_ref)

        stats = stats_ref[...]
    mixed = []
    for j in range(PER):
        low, high = window(j)
        scores = dot_nt(masked_query(query, j), keys[:, low:high]) * scale
        if allowed is not None:
            scores = jnp.where(allowed, scores, -jnp.inf)
        peak = jnp.max(scores, axis=1, keepdims=True)
        raised = jnp.exp(scores - peak)
        total = jnp.sum(raised, axis=1, keepdims=True)
        out = dot_nn(raised.astype(jnp.bfloat16), values[:, low:high])
        if normalise:
            out = out / total
        mixed.append(out)
        head = band * PER + j
        stats = jnp.where(lanes == head, peak, stats)
        stats = jnp.where(lanes == head + LSPLIT, total, stats)
    stats_ref[...] = stats
    for tile in range(BAND // LANES):
        put(tile, by_tile(tile, lambda j: mixed[j][:, tile * LANES - window(j)[0]:][:, :LANES]))


def prefix_kernel(scale, query_ref, key_ref, value_ref, out_ref, stats_ref):
    band = pl.program_id(0)
    bands = pl.num_programs(0)
    width = out_ref.shape[1] - LANES

    def put(tile, cols):
        at = pl.multiple_of(band * BAND + tile * LANES, LANES)
        out_ref[:, pl.ds(at, LANES)] = cols.astype(out_ref.dtype)

    attend(query_ref[...], key_ref[...], value_ref[...], None, scale, True, put, stats_ref)

    @pl.when(band == bands - 1)
    def _():
        full = stats_ref[...]
        high = full.astype(jnp.bfloat16).astype(jnp.float32)
        rest = full - high
        mid = rest.astype(jnp.bfloat16).astype(jnp.float32)
        low = rest - mid
        packed = high + pltpu.roll(mid, PIECE, 1) + pltpu.roll(low, 2 * PIECE, 1)
        out_ref[:, width:] = packed.astype(out_ref.dtype)


def suffix_kernel(scale, reqc_ref, reqr_ref, query_ref, key_ref, value_ref, out_ref, stats_ref):
    toks = query_ref.shape[0]
    shape = (toks, toks)
    allowed = (reqc_ref[...] == reqr_ref[...]) & (
        lax.broadcasted_iota(jnp.int32, shape, 1) <= lax.broadcasted_iota(jnp.int32, shape, 0)
    )

    def put(tile, cols):
        out_ref[:, tile * LANES:(tile + 1) * LANES] = cols

    keys = key_ref[...].reshape(toks, BAND)
    values = value_ref[...].reshape(toks, BAND)
    attend(query_ref[...], keys, values, allowed, scale, False, put, stats_ref)


def merge_kernel(target_ref, back_ref, pstats_ref, mixed_ref, sstats_ref, out_ref):
    band = pl.program_id(0)
    rows = back_ref.shape[0]
    toks = target_ref.shape[0]
    place = lane_iota((toks, rows))
    pick = jnp.where(place == target_ref[...], 1.0, 0.0).astype(jnp.bfloat16)
    packed = dot_nn(pick, pstats_ref[...])
    prefix = (packed + pltpu.roll(packed, LANES - PIECE, 1)) + pltpu.roll(
        packed, LANES - 2 * PIECE, 1
    )
    suffix = sstats_ref[...]
    top = jnp.maximum(prefix, suffix)
    first = pltpu.roll(prefix, LANES - LSPLIT, 1) * jnp.exp(prefix - top)
    second = jnp.exp(suffix - top)
    below = first + second * pltpu.roll(suffix, LANES - LSPLIT, 1)
    wp = first / below
    ws = second / below
    lanes = lane_iota((toks, LANES))

    def column(weights, j):
        return jnp.sum(jnp.where(lanes == band * PER + j, weights, 0.0), axis=1, keepdims=True)

    cp = [column(wp, j) for j in range(PER)]
    cs = [column(ws, j) for j in range(PER)]
    for tile in range(BAND // LANES):
        cols = slice(tile * LANES, (tile + 1) * LANES)
        back = dot_nn(pick, back_ref[:, cols])
        merged = by_tile(tile, lambda j: cp[j]) * back + by_tile(tile, lambda j: cs[j]) * mixed_ref[:, cols]
        out_ref[:, cols] = merged.astype(out_ref.dtype)


def whole_block(array):
    return pl.BlockSpec(array.shape, lambda g: (0,) * array.ndim)


def band_block(rows, off=0):
    return pl.BlockSpec((rows, BAND), lambda g: (0, g + off))


def cost(flops, moved):
    return pl.CostEstimate(flops=flops, bytes_accessed=moved, transcendentals=0)


def room():
    return pltpu.CompilerParams(vmem_limit_bytes=48 * 1024 * 1024)


def exchange(x, axis):
    return lax.all_to_all(x, axis, split_axis=0, concat_axis=0, tiled=True)


def shift_exchange(x, axis):
    n = lax.axis_size(axis)
    me = lax.axis_index(axis)
    parts = [lax.dynamic_index_in_dim(x, me, 0, keepdims=False)]
    for d in range(1, n):
        ring = [(i, (i + d) % n) for i in range(n)]
        sent = lax.dynamic_index_in_dim(x, lax.rem(me + d, n), 0, keepdims=False)
        parts.append(lax.ppermute(sent, axis, ring))
    out = []
    for source in range(n):
        picked = parts[0]
        for d in range(1, n):
            picked = jnp.where(lax.rem(me + n - source, n) == d, parts[d], picked)
        out.append(picked)
    return jnp.stack(out)


def generic_device(qkv, prefix_cache, suffix_lengths, request_groups, prefix_owner):
    n_head = lax.axis_size("head")
    n_tok = lax.axis_size("tok")
    here = qkv.shape[0]
    width = qkv.shape[2] // n_head
    toks = here * n_head
    scale = 1.0 / math.sqrt(HD)
    bands = width // BAND
    parts = 1
    each = bands // parts
    cols = each * BAND
    capacity = 3 * toks // n_tok
    rows = n_tok * capacity
    planes = jnp.transpose(qkv, (1, 0, 2)).reshape(3, here, n_head, width)
    queries = [
        exchange(
            jnp.stack([qkv[:, 0, h * width:(h + 1) * width] for h in range(n_head)]), "head"
        ).reshape(toks, cols)
        for p in range(parts)
    ]
    kv_send = jnp.transpose(planes[1:], (2, 0, 1, 3))

    lengths = suffix_lengths[0]
    groups = request_groups[0]
    requests = lengths.shape[0]
    ends = jnp.sum(jnp.where(jnp.arange(requests)[:, None] <= jnp.arange(requests)[None, :], lengths[:, None], 0), axis=0)
    starts = ends - lengths
    slots = jnp.sum(jnp.where(groups[:, None] == jnp.arange(n_tok)[None, :], prefix_owner[None, :], 0), axis=1)
    position = jnp.arange(toks, dtype=jnp.int32)
    request = jnp.sum((position[:, None] >= ends[None, :]).astype(jnp.int32), axis=1)
    base = slots * capacity - starts
    inside = request[:, None] == jnp.arange(requests, dtype=jnp.int32)[None, :]
    target = (position + jnp.sum(jnp.where(inside, base[None, :], 0), axis=1)).astype(jnp.int32)
    target_row = target[None, :]
    target_col = target[:, None]
    reqc, reqr = request[:, None], request[None, :]

    prefix_len = prefix_cache.shape[1]
    queries[0], cache_keys, cache_values = lax.optimization_barrier(
        (queries[0], prefix_cache[0, :, 0], prefix_cache[0, :, 1])
    )
    received = []
    for p in range(parts):
        outgoing = pl.pallas_call(
            spread_kernel,
            grid=(each,),
            out_shape=jax.ShapeDtypeStruct((rows, cols), jnp.bfloat16),
            in_specs=[whole_block(target_row), band_block(toks)],
            out_specs=band_block(rows),
            cost_estimate=cost(2 * rows * toks * cols, 2 * (rows + toks) * cols),
            compiler_params=room(),
            name="spread",
        )(target_row, queries[p])
        if p == 0:
            outgoing, kv_send = lax.optimization_barrier((outgoing, kv_send))
        received.append(exchange(outgoing.reshape(n_tok, capacity, cols), "tok").reshape(rows, cols))
    kv = shift_exchange(kv_send, "head")

    back = []
    for p in range(parts):
        mixed = pl.pallas_call(
            functools.partial(prefix_kernel, scale),
            grid=(each,),
            out_shape=jax.ShapeDtypeStruct((rows, cols + LANES), jnp.bfloat16),
            in_specs=[band_block(rows), band_block(prefix_len, p * each), band_block(prefix_len, p * each)],
            out_specs=pl.BlockSpec((rows, cols + LANES), lambda g: (0, 0)),
            scratch_shapes=[pltpu.VMEM((rows, LANES), jnp.float32)],
            cost_estimate=cost(4 * rows * prefix_len * cols, 4 * (rows + prefix_len) * cols),
            compiler_params=room(),
            name="prefix",
        )(received[p], cache_keys, cache_values)
        back.append(exchange(mixed.reshape(n_tok, capacity, cols + LANES), "tok").reshape(rows, cols + LANES))

    finals = []
    for p in range(parts):
        key_spec = pl.BlockSpec((n_head, None, here, BAND), lambda g, p=p: (0, 0, 0, g + p * each))
        value_spec = pl.BlockSpec((n_head, None, here, BAND), lambda g, p=p: (0, 1, 0, g + p * each))
        mixed_s, stats_s = pl.pallas_call(
            functools.partial(suffix_kernel, scale),
            grid=(each,),
            out_shape=[
                jax.ShapeDtypeStruct((toks, cols), jnp.float32),
                jax.ShapeDtypeStruct((toks, LANES), jnp.float32),
            ],
            in_specs=[whole_block(reqc), whole_block(reqr), band_block(toks), key_spec, value_spec],
            out_specs=[band_block(toks), pl.BlockSpec((toks, LANES), lambda g: (0, 0))],
            cost_estimate=cost(4 * toks * toks * cols, 10 * toks * cols),
            compiler_params=room(),
            name="suffix",
        )(reqc, reqr, queries[p], kv, kv)
        merged = pl.pallas_call(
            merge_kernel,
            grid=(each,),
            out_shape=jax.ShapeDtypeStruct((toks, cols), jnp.bfloat16),
            in_specs=[
                whole_block(target_col),
                band_block(rows),
                pl.BlockSpec((rows, LANES), lambda g: (0, cols // LANES)),
                band_block(toks),
                whole_block(stats_s),
            ],
            out_specs=band_block(toks),
            cost_estimate=cost(2 * rows * toks * cols, 2 * (rows + 3 * toks) * cols),
            compiler_params=room(),
            name="merge",
        )(target_col, back[p], back[p], mixed_s, stats_s)
        finals.append(exchange(merged.reshape(n_head, here, cols), "head"))
    attended = jnp.transpose(jnp.stack(finals, axis=2), (1, 0, 2, 3)).reshape(here, n_head * width)
    suffix_cache = jnp.transpose(kv, (0, 2, 1, 3)).reshape(toks, 2, width)
    return (attended, suffix_cache)


TEAM = 4
FEATURES = 7168
CODE = 1024
FAR = (192, 208, 224, 240)
NEAR = 256
MOST = 384
FIRST = 512
MIDDLE = 384
STAT = 8
MESH = pl.DeviceIdType.MESH


def place():
    tok = lax.axis_index("tok")
    half = lax.axis_index("head")
    return lax.div(tok, TEAM), lax.rem(tok, TEAM), half


def team_at(member, level):
    return {"tok": level * TEAM + lax.rem(member, TEAM), "head": lax.div(member, TEAM)}


def team_rows(member, rows):
    at = (lax.rem(member, TEAM) * 2 + lax.div(member, TEAM)) * rows
    return pl.ds(pl.multiple_of(at, 16), rows)


def band_cols(member, low=0, wide=BAND):
    return pl.ds(pl.multiple_of(member * BAND + low, LANES), wide)


def layout(sizes):
    starts = [sum(sizes[:d]) for d in range(TEAM)]
    total = sum(sizes)
    return starts, total, -(-total // (16 * TEAM)) * 16


def note_layout(sizes):
    high = [-(-size // LANES) * STAT for size in sizes]
    return [sum(high[:d]) for d in range(TEAM)], high


def masked_window(query, j):
    low, high = window(j)
    cols = lane_iota((query.shape[0], high - low)) + low
    keep = (cols >= j * HD) & (cols < (j + 1) * HD)
    return jnp.where(keep, query, jnp.zeros((), query.dtype))


def tables_kernel(
    far_sizes, lengths_ref, groups_ref, owner_ref, qkv_ref, cache_ref,
    pool_ref, kv_ref, slot_ref, code_ref, req_ref, peak_ref,
    meta, table, cache, sm, rm, sq, rq, sl,
):
    level, work, half = place()
    tok = level * TEAM + work
    team = 2 * TEAM
    mine = half * TEAM + work
    n = lax.axis_size("tok")
    rows = qkv_ref.shape[1]
    width = kv_ref.shape[2]

    def tok_peer(d):
        return {"tok": lax.rem(tok + d, n), "head": half}

    def meta_copy(d, landing):
        return pltpu.make_async_remote_copy(
            src_ref=meta, dst_ref=table.at[landing], send_sem=sm.at[d], recv_sem=rm.at[d],
            device_id=tok_peer(d), device_id_type=MESH,
        )

    def query_copy(e, landing):
        peer = lax.rem(mine + e, team)
        return pltpu.make_async_remote_copy(
            src_ref=qkv_ref.at[0, :, band_cols(peer, 0, FIRST)],
            dst_ref=pool_ref.at[team_rows(landing, rows), :],
            send_sem=sq.at[e], recv_sem=rq.at[e],
            device_id=team_at(peer, level), device_id_type=MESH,
        )

    def each(body, count):
        def step(d, carry):
            body(d)
            return carry

        lax.fori_loop(1, count, step, 0)

    barrier = pltpu.get_barrier_semaphore()
    each(lambda d: pl.semaphore_signal(barrier, inc=1, device_id=tok_peer(d), device_id_type=MESH), n)
    for w in range(TEAM):
        pl.semaphore_signal(
            barrier, inc=1, device_id={"tok": level * TEAM + w, "head": 1 - half}, device_id_type=MESH
        )
    bring = pltpu.make_async_copy(cache_ref.at[0], cache, sl.at[0])
    bring.start()
    own = pltpu.make_async_copy(
        qkv_ref.at[0, :, band_cols(mine, 0, FIRST)], pool_ref.at[team_rows(mine, rows), :], sl.at[1]
    )
    own.start()
    count = lengths_ref.shape[1]
    meta[...] = jnp.zeros_like(meta)
    meta[0:1, 0:count] = lengths_ref[...]
    meta[1:2, 0:count] = groups_ref[...]
    pl.semaphore_wait(barrier, n - 1 + TEAM)
    each(lambda d: meta_copy(d, tok).start(), n)
    each(lambda e: query_copy(e, mine).start(), team)
    table[tok] = meta[...]
    bring.wait()
    past = kv_ref.shape[1]
    aim = lax.broadcasted_iota(jnp.int32, (past, 2 * past), 1)
    source = 2 * lax.broadcasted_iota(jnp.int32, (past, 2 * past), 0)
    even = jnp.where(aim == source, 1.0, 0.0).astype(jnp.bfloat16)
    odd = jnp.where(aim == source + 1, 1.0, 0.0).astype(jnp.bfloat16)

    def split(c, carry):
        span = pl.ds(pl.multiple_of(c * 2 * LANES, LANES), 2 * LANES)
        both = cache[:, :, span].reshape(2 * past, 2 * LANES)
        kv_ref[0, :, span] = dot_nn(even, both).astype(jnp.bfloat16)
        kv_ref[1, :, span] = dot_nn(odd, both).astype(jnp.bfloat16)
        return carry

    lax.fori_loop(0, width // (2 * LANES), split, 0)
    each(lambda d: meta_copy(d, lax.rem(tok + n - d, n)).wait_recv(), n)

    lengths = table[:, 0, :]
    groups = table[:, 1, :]
    slots = jnp.zeros_like(groups)
    owners = owner_ref[...]
    for g in range(owners.shape[1]):
        slots = jnp.where(groups == g, owners[:, g:g + 1], slots)
    spot = lane_iota((n, LANES))
    slot = jnp.zeros((n, LANES), jnp.int32)
    request = jnp.zeros((n, LANES), jnp.int32)
    end = jnp.zeros((n, 1), jnp.int32)
    for r in range(REQUESTS):
        start = end
        end = start + lengths[:, r:r + 1]
        inside = (spot >= start) & (spot < end)
        slot = jnp.where(inside, slots[:, r:r + 1], slot)
        request = jnp.where(inside, r, request)
    goal = lax.div(slot, TEAM)
    marks = [jnp.where(goal == z, 1.0, 0.0) for z in range(TEAM)]
    hot = jnp.concatenate(marks, axis=0).astype(jnp.bfloat16)
    down = lax.broadcasted_iota(jnp.int32, (LANES, LANES), 0)
    upto = jnp.where(down <= lane_iota((LANES, LANES)), 1.0, 0.0).astype(jnp.bfloat16)
    running = dot_nn(hot, upto)
    totals = dot_nn(hot, jnp.ones((LANES, LANES), jnp.bfloat16))
    m = TEAM * n
    a = lax.broadcasted_iota(jnp.int32, (m, m), 0)
    b = lax.broadcasted_iota(jnp.int32, (m, m), 1)
    earlier = (lax.div(a, TEAM) == lax.div(b, TEAM)) & (b < a)
    before = dot_nn(jnp.where(earlier, 1.0, 0.0).astype(jnp.bfloat16), totals.astype(jnp.bfloat16))
    count = (running + before).astype(jnp.int32)
    code = jnp.zeros((n, LANES), jnp.int32)
    for z in range(TEAM):
        code = jnp.where(goal == z, z * CODE + count[z * n:(z + 1) * n] - 1, code)
    slot = slot - goal * TEAM
    for z in range(TEAM):
        part = slice(z * TEAM, (z + 1) * TEAM)
        slot_ref[z] = slot[part]
        code_ref[z] = code[part]
        req_ref[z] = request[part]
    aim = lax.div(lax.broadcasted_iota(jnp.int32, (m, LANES), 0), n)
    source = lax.div(lax.rem(lax.broadcasted_iota(jnp.int32, (m, LANES), 0), n), TEAM)
    far = lax.div(aim, 2) != lax.div(source, 2)
    need = jnp.where(far, count, jnp.where(count > NEAR, MOST, 0))
    most = jnp.max(need)
    choice = jnp.int32(0)
    for size in far_sizes:
        choice = choice + (most > size).astype(jnp.int32)
    peak_ref[0, 0] = choice

    own.wait()
    each(lambda e: query_copy(e, lax.rem(mine + team - e, team)).wait_recv(), team)
    each(lambda d: meta_copy(d, tok).wait_send(), n)
    each(lambda e: query_copy(e, mine).wait_send(), team)


def pool_kernel(
    scale, sizes, early_ref, kv_ref, slot_ref, code_ref, req_ref, qkv_ref, out_ref, pair_ref,
    pool_ref, mixed, local, outgo, income, result, back, stats, cols, keep, fresh, final,
    note_out, note_in, notes, picks, pair,
    s1, r1, s2, r2, s3, r3, s4, r4, s5, r5, s6, r6, s7, r7, s8, r8, sl,
):
    level, work, half = place()
    team = 2 * TEAM
    mine = half * TEAM + work
    rows = qkv_ref.shape[1]
    toks = 2 * rows
    width = kv_ref.shape[2]
    starts, total_rows, block = layout(sizes)
    note_starts, note_sizes = note_layout(sizes)
    partners = (
        level, level + 1 - 2 * lax.rem(level, 2), lax.rem(level + 2, TEAM), TEAM - 1 - level,
    )
    order = (2, 3, 1)
    inner = ((0, FIRST), (FIRST, BAND))
    outer = ((0, MIDDLE), (MIDDLE, BAND))

    def rows_of(d):
        return slice(starts[d], starts[d] + sizes[d])

    def note_rows(d):
        return slice(note_starts[d], note_starts[d] + note_sizes[d])

    def level_id(d):
        return {"tok": partners[d] * TEAM + work, "head": half}

    def query_copy(e, landing):
        peer = lax.rem(mine + e, team)
        return pltpu.make_async_remote_copy(
            src_ref=qkv_ref.at[0, :, band_cols(peer, FIRST, BAND - FIRST)],
            dst_ref=pool_ref.at[team_rows(landing, rows), FIRST:BAND],
            send_sem=s8.at[e], recv_sem=r8.at[e],
            device_id=team_at(peer, level), device_id_type=MESH,
        )

    def forth_copy(d, part):
        span = slice(*inner[part])
        return pltpu.make_async_remote_copy(
            src_ref=outgo.at[rows_of(d), span], dst_ref=income.at[rows_of(d), span],
            send_sem=s1.at[part, d], recv_sem=r1.at[part, d],
            device_id=level_id(d), device_id_type=MESH,
        )

    def back_copy(d, part):
        span = slice(*outer[part])
        return pltpu.make_async_remote_copy(
            src_ref=result.at[rows_of(d), span], dst_ref=back.at[rows_of(d), span],
            send_sem=s2.at[part, d], recv_sem=r2.at[part, d],
            device_id=level_id(d), device_id_type=MESH,
        )

    def note_copy(d, part):
        return pltpu.make_async_remote_copy(
            src_ref=note_out.at[part, note_rows(d), :], dst_ref=note_in.at[part, note_rows(d), :],
            send_sem=s6.at[part, d], recv_sem=r6.at[part, d],
            device_id=level_id(d), device_id_type=MESH,
        )

    def cache_copy(e, part, landing):
        peer = lax.rem(work + e, TEAM)
        low, high = inner[part]
        return pltpu.make_async_remote_copy(
            src_ref=kv_ref.at[:, :, band_cols(peer, low, high - low)],
            dst_ref=keep.at[landing, :, :, low:high],
            send_sem=s3.at[part, e], recv_sem=r3.at[part, e],
            device_id={"tok": level * TEAM + peer, "head": half}, device_id_type=MESH,
        )

    def fresh_copy(e, part, landing):
        peer = lax.rem(mine + e, team)
        low, high = inner[part]
        return pltpu.make_async_remote_copy(
            src_ref=qkv_ref.at[1:3, :, band_cols(peer, low, high - low)],
            dst_ref=fresh.at[:, team_rows(landing, rows), low:high],
            send_sem=s4.at[part, e], recv_sem=r4.at[part, e],
            device_id=team_at(peer, level), device_id_type=MESH,
        )

    def final_copy(e, part, landing):
        peer = lax.rem(mine + e, team)
        low, high = outer[part]
        return pltpu.make_async_remote_copy(
            src_ref=final.at[team_rows(peer, rows), low:high],
            dst_ref=out_ref.at[:, band_cols(landing, low, high - low)],
            send_sem=s5.at[part, e], recv_sem=r5.at[part, e],
            device_id=team_at(peer, level), device_id_type=MESH,
        )

    def half_cols(which):
        return pl.ds(pl.multiple_of(which * width, LANES), width)

    swap = pltpu.make_async_remote_copy(
        src_ref=qkv_ref.at[1:3, :, half_cols(1 - half)], dst_ref=pair.at[1],
        send_sem=s7.at[0], recv_sem=r7.at[0],
        device_id={"tok": level * TEAM + work, "head": 1 - half}, device_id_type=MESH,
    )

    def weave(which, owner):
        where = pl.ds(pl.multiple_of(owner * rows, 16), rows)

        def step(c, carry):
            span = pl.ds(pl.multiple_of(c * LANES, LANES), LANES)
            pair_ref[where, 0, span] = pair[which, 0, :, span]
            pair_ref[where, 1, span] = pair[which, 1, :, span]
            return carry

        lax.fori_loop(0, width // LANES, step, 0)

    barrier = pltpu.get_barrier_semaphore()
    for e in range(1, team):
        pl.semaphore_signal(barrier, inc=1, device_id=team_at(lax.rem(mine + e, team), level), device_id_type=MESH)
    for d in range(1, TEAM):
        pl.semaphore_signal(barrier, inc=1, device_id=level_id(d), device_id_type=MESH)
    own_query = pltpu.make_async_copy(
        qkv_ref.at[0, :, band_cols(mine, FIRST, BAND - FIRST)],
        pool_ref.at[team_rows(mine, rows), FIRST:BAND], sl.at[4],
    )
    own_query.start()
    early = pltpu.make_async_copy(early_ref, pool_ref.at[:, 0:FIRST], sl.at[3])
    early.start()
    own_fresh = pltpu.make_async_copy(
        qkv_ref.at[1:3, :, band_cols(mine)], fresh.at[:, team_rows(mine, rows), :], sl.at[1]
    )
    own_fresh.start()
    own_pair = pltpu.make_async_copy(qkv_ref.at[1:3, :, half_cols(half)], pair.at[0], sl.at[2])
    own_pair.start()
    own_cache = pltpu.make_async_copy(kv_ref.at[:, :, band_cols(work)], keep.at[work], sl.at[0])
    own_cache.start()

    def flat(ref, z):
        entry = ref[z]
        return jnp.concatenate([entry[i:i + 1] for i in range(TEAM)], axis=1)

    code = flat(code_ref, level)

    def packed(d, part):
        source = early_ref[...] if part == 0 else pool_ref[:, FIRST:BAND]
        down = lax.broadcasted_iota(jnp.int32, (sizes[d], TEAM * toks), 0)
        pick = jnp.where(down == code - partners[d] * CODE, 1.0, 0.0).astype(jnp.bfloat16)
        return dot_nn(pick, source).astype(jnp.bfloat16)

    for d in order:
        outgo[rows_of(d), 0:FIRST] = packed(d, 0)
    pl.semaphore_wait(barrier, team - 1 + TEAM - 1)
    for d in order:
        forth_copy(d, 0).start()
    for e in range(1, team):
        query_copy(e, mine).start()
    for part in range(2):
        for e in range(1, TEAM):
            cache_copy(e, part, work).start()
    for late in range(2):
        for e in range(1, team):
            fresh_copy(e, late, mine).start()
    swap.start()
    own_query.wait()
    early.wait()
    for e in range(1, team):
        query_copy(e, lax.rem(mine + team - e, team)).wait_recv()
    for d in order:
        outgo[rows_of(d), FIRST:BAND] = packed(d, 1)
        forth_copy(d, 1).start()
    for part in range(2):
        income[rows_of(0), slice(*inner[part])] = packed(0, part)
    for d in range(TEAM):
        down = lax.broadcasted_iota(jnp.int32, (sizes[d], TEAM * toks), 0)
        hit = down == flat(code_ref, partners[d]) - level * CODE
        seats = flat(slot_ref, partners[d]).astype(jnp.float32)
        found = jnp.sum(jnp.where(hit, seats, 0.0), axis=1, keepdims=True)
        cols[rows_of(d), :] = jnp.broadcast_to(found, (sizes[d], LANES))
    spare = TEAM * block - total_rows
    if spare:
        income[total_rows:TEAM * block, :] = jnp.zeros((spare, BAND), jnp.bfloat16)
        cols[total_rows:TEAM * block, :] = jnp.zeros((spare, LANES), jnp.float32)
    stats[...] = jnp.zeros_like(stats)
    own_pair.wait()
    weave(0, half)
    own_cache.wait()

    def heads_of(part):
        return range(2) if part == 0 else range(2, PER)

    def assemble(part, outs, old, keep_tile):
        for tile in range(4) if part == 0 else range(3, BAND // LANES):
            first, last = owners_of(tile)

            def cut(j):
                return outs[j][:, tile * LANES - window(j)[0]:][:, :LANES]

            if tile != 3:
                values = by_tile(tile, cut)
            elif part == 0:
                values = cut(first)
            else:
                before = old(tile)
                values = jnp.where(lane_iota(before.shape) < last * HD - tile * LANES, before, cut(last))
            keep_tile(tile, values)

    def prefix(part):
        def run(b, carry):
            span = pl.ds(pl.multiple_of(b * block, 16), block)
            which = cols[span, :][:, :1]
            lanes = lane_iota((block, LANES))
            noted = stats[span, :]
            outs = {}
            for j in heads_of(part):
                low, high = window(j)
                asked = masked_window(income[span, low:high], j)
                scores = None
                for s in range(TEAM):
                    some = dot_nt(asked, keep[s, 0, :, low:high])
                    scores = some if s == 0 else jnp.where(which == s, some, scores)
                scores = scores * scale
                top = jnp.max(scores, axis=1, keepdims=True)
                raised = jnp.exp(scores - top)
                total = jnp.sum(raised, axis=1, keepdims=True)
                out = None
                for s in range(TEAM):
                    weights = jnp.where(which == s, raised, 0.0).astype(jnp.bfloat16)
                    term = dot_nn(weights, keep[s, 1, :, low:high])
                    out = term if s == 0 else out + term
                outs[j] = out / total
                noted = jnp.where(lanes == j, top, noted)
                noted = jnp.where(lanes == PER + j, total, noted)

            def put(tile, values):
                result[span, tile * LANES:(tile + 1) * LANES] = values.astype(jnp.bfloat16)

            def old(tile):
                return result[span, tile * LANES:(tile + 1) * LANES].astype(jnp.float32)

            assemble(part, outs, old, put)
            stats[span, :] = noted
            return carry

        lax.fori_loop(0, TEAM, run, 0)
        for d in order:
            back_copy(d, part).start()
        for d in range(TEAM):
            high = note_sizes[d]
            folded = None
            for k in range(LANES // STAT):
                piece = stats[starts[d] + k * high:starts[d] + (k + 1) * high, :]
                folded = piece if k == 0 else folded + pltpu.roll(piece, k * STAT, 1)
            note_out[part, note_rows(d), :] = folded
            if d:
                note_copy(d, part).start()

    for part in range(2):
        for d in order:
            forth_copy(d, part).wait_recv()
        for e in range(1, TEAM):
            cache_copy(e, part, lax.rem(work + TEAM - e, TEAM)).wait_recv()
        prefix(part)
        if part == 0:
            swap.wait_recv()
            weave(1, 1 - half)
    back[rows_of(0), :] = result[rows_of(0), :]
    note_in[:, note_rows(0), :] = note_out[:, note_rows(0), :]
    own_fresh.wait()

    eye = lax.broadcasted_iota(jnp.int32, (toks, toks), 0) == lane_iota((toks, toks))
    causal = lane_iota((toks, toks)) <= lax.broadcasted_iota(jnp.int32, (toks, toks), 0)
    lanes = lane_iota((toks, LANES))

    def column(row):
        return jnp.sum(jnp.where(eye, row, 0.0), axis=1, keepdims=True)

    def choose(i, carry):
        span = pl.ds(pl.multiple_of(i * toks, toks), toks)
        codes = code_ref[level, pl.ds(i, 1), :]
        goal = lax.div(codes, CODE)
        seat = codes - goal * CODE
        for d in range(1, TEAM):
            seat = jnp.where(goal == partners[d], seat + starts[d], seat)
        seat = column(seat.astype(jnp.float32)).astype(jnp.int32)
        picks[span, :] = jnp.where(lane_iota((toks, total_rows)) == seat, 1.0, 0.0).astype(jnp.bfloat16)
        local[span, :] = jnp.zeros((toks, LANES), jnp.float32)
        return carry

    lax.fori_loop(0, TEAM, choose, 0)

    def suffix(part):
        def run(i, carry):
            span = pl.ds(pl.multiple_of(i * toks, toks), toks)
            asks = req_ref[level, pl.ds(i, 1), :].astype(jnp.float32)
            allowed = (column(asks) == asks) & causal
            noted = local[span, :]
            outs = {}
            for j in heads_of(part):
                low, high = window(j)
                scores = dot_nt(masked_window(pool_ref[span, low:high], j), fresh[0, span, low:high]) * scale
                scores = jnp.where(allowed, scores, -jnp.inf)
                peak = jnp.max(scores, axis=1, keepdims=True)
                raised = jnp.exp(scores - peak)
                total = jnp.sum(raised, axis=1, keepdims=True)
                outs[j] = dot_nn(raised.astype(jnp.bfloat16), fresh[1, span, low:high])
                noted = jnp.where(lanes == j, peak, noted)
                noted = jnp.where(lanes == PER + j, total, noted)

            def put(tile, values):
                mixed[span, tile * LANES:(tile + 1) * LANES] = values

            def old(tile):
                return mixed[span, tile * LANES:(tile + 1) * LANES]

            assemble(part, outs, old, put)
            local[span, :] = noted
            return carry

        lax.fori_loop(0, TEAM, run, 0)

    def unfold(part):
        for d in range(TEAM):
            piece = note_in[part, note_rows(d), :]
            turned = [piece] + [pltpu.roll(piece, LANES - k * STAT, 1) for k in range(1, LANES // STAT)]
            full = jnp.concatenate(turned, axis=0)[:sizes[d]]
            full = jnp.where(lane_iota((sizes[d], LANES)) < STAT, full, 0.0)
            high = full.astype(jnp.bfloat16).astype(jnp.float32)
            rest = full - high
            mid = rest.astype(jnp.bfloat16).astype(jnp.float32)
            packed = high + pltpu.roll(mid, STAT, 1) + pltpu.roll(rest - mid, 2 * STAT, 1)
            notes[rows_of(d), :] = packed.astype(jnp.bfloat16)

    def finish(part):
        low, high = outer[part]

        def run(turn, carry):
            k = lax.rem(turn + 1, TEAM)
            span = pl.ds(pl.multiple_of(lax.rem(work + k, TEAM) * toks, toks), toks)
            pick = picks[span, :]
            packed = dot_nn(pick, notes[...])
            prior = (packed + pltpu.roll(packed, LANES - STAT, 1)) + pltpu.roll(packed, LANES - 2 * STAT, 1)
            ready = dot_nn(pick, back[:, low:high])
            noted = local[span, :]
            top = jnp.maximum(prior, noted)
            first = pltpu.roll(prior, LANES - PER, 1) * jnp.exp(prior - top)
            second = jnp.exp(noted - top)
            below = first + second * pltpu.roll(noted, LANES - PER, 1)
            wp = first / below
            ws = second / below
            for tile in range(low // LANES, high // LANES):
                at = slice(tile * LANES, (tile + 1) * LANES)
                values = (
                    by_tile(tile, lambda j: wp[:, j:j + 1]) * ready[:, tile * LANES - low:][:, :LANES]
                    + by_tile(tile, lambda j: ws[:, j:j + 1]) * mixed[span, at]
                )
                final[span, at] = values.astype(jnp.bfloat16)

            @pl.when(k > 0)
            def _():
                final_copy(k, part, mine).start()

            final_copy(k + TEAM, part, mine).start()
            return carry

        lax.fori_loop(0, TEAM, run, 0)

    for part in range(2):
        for e in range(1, team):
            fresh_copy(e, part, lax.rem(mine + team - e, team)).wait_recv()
        suffix(part)
        for d in order:
            back_copy(d, part).wait_recv()
            note_copy(d, part).wait_recv()
        unfold(part)
        finish(part)
    out_ref[:, band_cols(mine)] = final[team_rows(mine, rows), :]
    for part in range(2):
        for e in range(1, team):
            final_copy(e, part, lax.rem(mine + team - e, team)).wait_recv()
    swap.wait_send()
    for e in range(1, team):
        query_copy(e, mine).wait_send()
    for part in range(2):
        for d in range(1, TEAM):
            note_copy(d, part).wait_send()
            forth_copy(d, part).wait_send()
            back_copy(d, part).wait_send()
        for e in range(1, TEAM):
            cache_copy(e, part, work).wait_send()
        for e in range(1, team):
            fresh_copy(e, part, mine).wait_send()
            final_copy(e, part, mine).wait_send()


REQUESTS = 8


def pooled_device(qkv, prefix_cache, suffix_lengths, request_groups, prefix_owner):
    n_head = lax.axis_size("head")
    n_tok = lax.axis_size("tok")
    here = qkv.shape[0]
    width = qkv.shape[2] // n_head
    toks = here * n_head
    scale = 1.0 / math.sqrt(HD)
    past = prefix_cache.shape[1]
    planes = jnp.transpose(qkv, (1, 0, 2))
    vmem = pl.BlockSpec(memory_space=pltpu.VMEM)
    smem = pl.BlockSpec(memory_space=pltpu.SMEM)
    hbm = pl.BlockSpec(memory_space=pltpu.HBM)
    free = pl.BlockSpec(memory_space=pl.ANY)
    dma = pltpu.SemaphoreType.DMA
    table = jax.ShapeDtypeStruct((TEAM, TEAM, LANES), jnp.int32)

    early, kv, slot, code, request, peak = pl.pallas_call(
        functools.partial(tables_kernel, FAR),
        out_shape=[
            jax.ShapeDtypeStruct((TEAM * toks, FIRST), jnp.bfloat16),
            jax.ShapeDtypeStruct((2, past, width), jnp.bfloat16),
            table, table, table, jax.ShapeDtypeStruct((1, 1), jnp.int32),
        ],
        in_specs=[vmem, vmem, vmem, hbm, hbm],
        out_specs=[vmem] * 5 + [smem],
        scratch_shapes=[
            pltpu.VMEM((8, LANES), jnp.int32),
            pltpu.VMEM((n_tok, 8, LANES), jnp.int32),
            pltpu.VMEM((past, 2, width), jnp.bfloat16),
            dma((n_tok,)), dma((n_tok,)), dma((2 * TEAM,)), dma((2 * TEAM,)), dma((2,)),
        ],
        compiler_params=pltpu.CompilerParams(
            collective_id=0, has_side_effects=True, vmem_limit_bytes=56 * 1024 * 1024
        ),
        name="tables",
    )(suffix_lengths, request_groups, prefix_owner[None], planes, prefix_cache)

    def pooled(sizes, number):
        total, block = layout(sizes)[1:]
        marks = sum(note_layout(sizes)[1])
        bf16, f32 = jnp.bfloat16, jnp.float32
        two, team = (2, TEAM), (2, 2 * TEAM)

        def call(early, kv, slot, code, request, planes):
            return pl.pallas_call(
                functools.partial(pool_kernel, scale, sizes),
                out_shape=[
                    jax.ShapeDtypeStruct((here, n_head * width), bf16),
                    jax.ShapeDtypeStruct((toks, 2, width), bf16),
                ],
                in_specs=[vmem, free, vmem, vmem, vmem, hbm],
                out_specs=[vmem] * 2,
                scratch_shapes=[
                    pltpu.VMEM((TEAM * toks, BAND), bf16),
                    pltpu.VMEM((TEAM * toks, BAND), f32),
                    pltpu.VMEM((TEAM * toks, LANES), f32),
                    pltpu.VMEM((total, BAND), bf16),
                    pltpu.VMEM((TEAM * block, BAND), bf16),
                    pltpu.VMEM((TEAM * block, BAND), bf16),
                    pltpu.VMEM((total, BAND), bf16),
                    pltpu.VMEM((TEAM * block + LANES, LANES), f32),
                    pltpu.VMEM((TEAM * block, LANES), f32),
                    pltpu.VMEM((TEAM, 2, past, BAND), bf16),
                    pltpu.VMEM((2, TEAM * toks, BAND), bf16),
                    pltpu.VMEM((TEAM * toks, BAND), bf16),
                    pltpu.VMEM((2, marks, LANES), f32),
                    pltpu.VMEM((2, marks, LANES), f32),
                    pltpu.VMEM((total, LANES), bf16),
                    pltpu.VMEM((TEAM * toks, total), bf16),
                    pltpu.VMEM((2, 2, here, width), bf16),
                    dma(two), dma(two), dma(two), dma(two), dma(two), dma(two),
                    dma(team), dma(team), dma(team), dma(team), dma(two), dma(two),
                    dma((1,)), dma((1,)), dma((2 * TEAM,)), dma((2 * TEAM,)), dma((5,)),
                ],
                compiler_params=pltpu.CompilerParams(
                    collective_id=number, has_side_effects=True, vmem_limit_bytes=52 * 1024 * 1024
                ),
                name="pooled",
            )(early, kv, slot, code, request, planes)

        return call

    choices = [(NEAR, NEAR, size, size) for size in FAR] + [(MOST,) * TEAM]
    return lax.switch(
        peak[0, 0], [pooled(sizes, 1 + i) for i, sizes in enumerate(choices)],
        early, kv, slot, code, request, planes,
    )


def solution(mesh):
    in_specs = (
        P(("tok", "head"), None, None),
        P("tok", None, None, "head"),
        P("tok", None),
        P("tok", None),
        P(),
    )
    out_specs = (P(("tok", "head"), None), P("tok", None, "head"))
    pooled = mesh.shape["tok"] == TEAM * TEAM and BAND * TEAM * mesh.shape["head"] == FEATURES
    body = pooled_device if pooled else generic_device
    return jax.shard_map(
        body, mesh=mesh, in_specs=in_specs, out_specs=out_specs, check_vma=False
    )
```

```python
import functools
import math

import jax
import jax.numpy as jnp
from jax import lax
from jax.experimental import pallas as pl
from jax.experimental.pallas import tpu as pltpu
from jax.sharding import PartitionSpec as P

HD = 224
LANES = 128
BAND = math.lcm(HD, LANES)
PER = BAND // HD
LSPLIT = 16
PIECE = 2 * LSPLIT


def window(j):
    low = j * HD // LANES * LANES
    high = -(-(j + 1) * HD // LANES) * LANES
    return low, high


def owners_of(tile):
    first = tile * LANES // HD
    last = ((tile + 1) * LANES - 1) // HD
    return first, last


def lane_iota(shape):
    return lax.broadcasted_iota(jnp.int32, shape, len(shape) - 1)


def by_tile(tile, pick):
    first, last = owners_of(tile)
    left = pick(first)
    if first == last:
        return left
    right = pick(last)
    edge = last * HD - tile * LANES
    return jnp.where(lane_iota((right.shape[0], LANES)) < edge, left, right)


def masked_query(query, j):
    low, high = window(j)
    cols = lane_iota((query.shape[0], high - low)) + low
    keep = (cols >= j * HD) & (cols < (j + 1) * HD)
    return jnp.where(keep, query[:, low:high], jnp.zeros((), query.dtype))


def dot_nt(a, b):
    return lax.dot_general(a, b, (((1,), (1,)), ((), ())), preferred_element_type=jnp.float32)


def dot_nn(a, b):
    return lax.dot_general(a, b, (((1,), (0,)), ((), ())), preferred_element_type=jnp.float32)


def spread_kernel(target_ref, query_ref, out_ref):
    rows = out_ref.shape[0]
    toks = target_ref.shape[1]
    place = lax.broadcasted_iota(jnp.int32, (rows, toks), 0)
    pick = jnp.where(place == target_ref[...], 1.0, 0.0).astype(jnp.bfloat16)
    out_ref[...] = dot_nn(pick, query_ref[...]).astype(jnp.bfloat16)


def attend(query, keys, values, allowed, scale, normalise, put, stats_ref, band=None):
    band = pl.program_id(0) if band is None else band
    rows = query.shape[0]
    lanes = lane_iota((rows, LANES))

    if isinstance(band, int):
        stats = jnp.zeros_like(stats_ref) if band == 0 else stats_ref[...]
    else:

        @pl.when(band == 0)
        def _():
            stats_ref[...] = jnp.zeros_like(stats_ref)

        stats = stats_ref[...]
    mixed = []
    for j in range(PER):
        low, high = window(j)
        scores = dot_nt(masked_query(query, j), keys[:, low:high]) * scale
        if allowed is not None:
            scores = jnp.where(allowed, scores, -jnp.inf)
        peak = jnp.max(scores, axis=1, keepdims=True)
        raised = jnp.exp(scores - peak)
        total = jnp.sum(raised, axis=1, keepdims=True)
        out = dot_nn(raised.astype(jnp.bfloat16), values[:, low:high])
        if normalise:
            out = out / total
        mixed.append(out)
        head = band * PER + j
        stats = jnp.where(lanes == head, peak, stats)
        stats = jnp.where(lanes == head + LSPLIT, total, stats)
    stats_ref[...] = stats
    for tile in range(BAND // LANES):
        put(tile, by_tile(tile, lambda j: mixed[j][:, tile * LANES - window(j)[0]:][:, :LANES]))


def prefix_kernel(scale, query_ref, key_ref, value_ref, out_ref, stats_ref):
    band = pl.program_id(0)
    bands = pl.num_programs(0)
    width = out_ref.shape[1] - LANES

    def put(tile, cols):
        at = pl.multiple_of(band * BAND + tile * LANES, LANES)
        out_ref[:, pl.ds(at, LANES)] = cols.astype(out_ref.dtype)

    attend(query_ref[...], key_ref[...], value_ref[...], None, scale, True, put, stats_ref)

    @pl.when(band == bands - 1)
    def _():
        full = stats_ref[...]
        high = full.astype(jnp.bfloat16).astype(jnp.float32)
        rest = full - high
        mid = rest.astype(jnp.bfloat16).astype(jnp.float32)
        low = rest - mid
        packed = high + pltpu.roll(mid, PIECE, 1) + pltpu.roll(low, 2 * PIECE, 1)
        out_ref[:, width:] = packed.astype(out_ref.dtype)


def suffix_kernel(scale, reqc_ref, reqr_ref, query_ref, key_ref, value_ref, out_ref, stats_ref):
    toks = query_ref.shape[0]
    shape = (toks, toks)
    allowed = (reqc_ref[...] == reqr_ref[...]) & (
        lax.broadcasted_iota(jnp.int32, shape, 1) <= lax.broadcasted_iota(jnp.int32, shape, 0)
    )

    def put(tile, cols):
        out_ref[:, tile * LANES:(tile + 1) * LANES] = cols

    keys = key_ref[...].reshape(toks, BAND)
    values = value_ref[...].reshape(toks, BAND)
    attend(query_ref[...], keys, values, allowed, scale, False, put, stats_ref)


def merge_kernel(target_ref, back_ref, pstats_ref, mixed_ref, sstats_ref, out_ref):
    band = pl.program_id(0)
    rows = back_ref.shape[0]
    toks = target_ref.shape[0]
    place = lane_iota((toks, rows))
    pick = jnp.where(place == target_ref[...], 1.0, 0.0).astype(jnp.bfloat16)
    packed = dot_nn(pick, pstats_ref[...])
    prefix = (packed + pltpu.roll(packed, LANES - PIECE, 1)) + pltpu.roll(
        packed, LANES - 2 * PIECE, 1
    )
    suffix = sstats_ref[...]
    top = jnp.maximum(prefix, suffix)
    first = pltpu.roll(prefix, LANES - LSPLIT, 1) * jnp.exp(prefix - top)
    second = jnp.exp(suffix - top)
    below = first + second * pltpu.roll(suffix, LANES - LSPLIT, 1)
    wp = first / below
    ws = second / below
    lanes = lane_iota((toks, LANES))

    def column(weights, j):
        return jnp.sum(jnp.where(lanes == band * PER + j, weights, 0.0), axis=1, keepdims=True)

    cp = [column(wp, j) for j in range(PER)]
    cs = [column(ws, j) for j in range(PER)]
    for tile in range(BAND // LANES):
        cols = slice(tile * LANES, (tile + 1) * LANES)
        back = dot_nn(pick, back_ref[:, cols])
        merged = by_tile(tile, lambda j: cp[j]) * back + by_tile(tile, lambda j: cs[j]) * mixed_ref[:, cols]
        out_ref[:, cols] = merged.astype(out_ref.dtype)


def whole_block(array):
    return pl.BlockSpec(array.shape, lambda g: (0,) * array.ndim)


def band_block(rows, off=0):
    return pl.BlockSpec((rows, BAND), lambda g: (0, g + off))


def cost(flops, moved):
    return pl.CostEstimate(flops=flops, bytes_accessed=moved, transcendentals=0)


def room():
    return pltpu.CompilerParams(vmem_limit_bytes=48 * 1024 * 1024)


def exchange(x, axis):
    return lax.all_to_all(x, axis, split_axis=0, concat_axis=0, tiled=True)


def shift_exchange(x, axis):
    n = lax.axis_size(axis)
    me = lax.axis_index(axis)
    parts = [lax.dynamic_index_in_dim(x, me, 0, keepdims=False)]
    for d in range(1, n):
        ring = [(i, (i + d) % n) for i in range(n)]
        sent = lax.dynamic_index_in_dim(x, lax.rem(me + d, n), 0, keepdims=False)
        parts.append(lax.ppermute(sent, axis, ring))
    out = []
    for source in range(n):
        picked = parts[0]
        for d in range(1, n):
            picked = jnp.where(lax.rem(me + n - source, n) == d, parts[d], picked)
        out.append(picked)
    return jnp.stack(out)


def generic_device(qkv, prefix_cache, suffix_lengths, request_groups, prefix_owner):
    n_head = lax.axis_size("head")
    n_tok = lax.axis_size("tok")
    here = qkv.shape[0]
    width = qkv.shape[2] // n_head
    toks = here * n_head
    scale = 1.0 / math.sqrt(HD)
    bands = width // BAND
    parts = 1
    each = bands // parts
    cols = each * BAND
    capacity = 3 * toks // n_tok
    rows = n_tok * capacity
    planes = jnp.transpose(qkv, (1, 0, 2)).reshape(3, here, n_head, width)
    queries = [
        exchange(
            jnp.stack([qkv[:, 0, h * width:(h + 1) * width] for h in range(n_head)]), "head"
        ).reshape(toks, cols)
        for p in range(parts)
    ]
    kv_send = jnp.transpose(planes[1:], (2, 0, 1, 3))

    lengths = suffix_lengths[0]
    groups = request_groups[0]
    requests = lengths.shape[0]
    ends = jnp.sum(jnp.where(jnp.arange(requests)[:, None] <= jnp.arange(requests)[None, :], lengths[:, None], 0), axis=0)
    starts = ends - lengths
    slots = jnp.sum(jnp.where(groups[:, None] == jnp.arange(n_tok)[None, :], prefix_owner[None, :], 0), axis=1)
    position = jnp.arange(toks, dtype=jnp.int32)
    request = jnp.sum((position[:, None] >= ends[None, :]).astype(jnp.int32), axis=1)
    base = slots * capacity - starts
    inside = request[:, None] == jnp.arange(requests, dtype=jnp.int32)[None, :]
    target = (position + jnp.sum(jnp.where(inside, base[None, :], 0), axis=1)).astype(jnp.int32)
    target_row = target[None, :]
    target_col = target[:, None]
    reqc, reqr = request[:, None], request[None, :]

    prefix_len = prefix_cache.shape[1]
    queries[0], cache_keys, cache_values = lax.optimization_barrier(
        (queries[0], prefix_cache[0, :, 0], prefix_cache[0, :, 1])
    )
    received = []
    for p in range(parts):
        outgoing = pl.pallas_call(
            spread_kernel,
            grid=(each,),
            out_shape=jax.ShapeDtypeStruct((rows, cols), jnp.bfloat16),
            in_specs=[whole_block(target_row), band_block(toks)],
            out_specs=band_block(rows),
            cost_estimate=cost(2 * rows * toks * cols, 2 * (rows + toks) * cols),
            compiler_params=room(),
            name="spread",
        )(target_row, queries[p])
        if p == 0:
            outgoing, kv_send = lax.optimization_barrier((outgoing, kv_send))
        received.append(exchange(outgoing.reshape(n_tok, capacity, cols), "tok").reshape(rows, cols))
    kv = shift_exchange(kv_send, "head")

    back = []
    for p in range(parts):
        mixed = pl.pallas_call(
            functools.partial(prefix_kernel, scale),
            grid=(each,),
            out_shape=jax.ShapeDtypeStruct((rows, cols + LANES), jnp.bfloat16),
            in_specs=[band_block(rows), band_block(prefix_len, p * each), band_block(prefix_len, p * each)],
            out_specs=pl.BlockSpec((rows, cols + LANES), lambda g: (0, 0)),
            scratch_shapes=[pltpu.VMEM((rows, LANES), jnp.float32)],
            cost_estimate=cost(4 * rows * prefix_len * cols, 4 * (rows + prefix_len) * cols),
            compiler_params=room(),
            name="prefix",
        )(received[p], cache_keys, cache_values)
        back.append(exchange(mixed.reshape(n_tok, capacity, cols + LANES), "tok").reshape(rows, cols + LANES))

    finals = []
    for p in range(parts):
        key_spec = pl.BlockSpec((n_head, None, here, BAND), lambda g, p=p: (0, 0, 0, g + p * each))
        value_spec = pl.BlockSpec((n_head, None, here, BAND), lambda g, p=p: (0, 1, 0, g + p * each))
        mixed_s, stats_s = pl.pallas_call(
            functools.partial(suffix_kernel, scale),
            grid=(each,),
            out_shape=[
                jax.ShapeDtypeStruct((toks, cols), jnp.float32),
                jax.ShapeDtypeStruct((toks, LANES), jnp.float32),
            ],
            in_specs=[whole_block(reqc), whole_block(reqr), band_block(toks), key_spec, value_spec],
            out_specs=[band_block(toks), pl.BlockSpec((toks, LANES), lambda g: (0, 0))],
            cost_estimate=cost(4 * toks * toks * cols, 10 * toks * cols),
            compiler_params=room(),
            name="suffix",
        )(reqc, reqr, queries[p], kv, kv)
        merged = pl.pallas_call(
            merge_kernel,
            grid=(each,),
            out_shape=jax.ShapeDtypeStruct((toks, cols), jnp.bfloat16),
            in_specs=[
                whole_block(target_col),
                band_block(rows),
                pl.BlockSpec((rows, LANES), lambda g: (0, cols // LANES)),
                band_block(toks),
                whole_block(stats_s),
            ],
            out_specs=band_block(toks),
            cost_estimate=cost(2 * rows * toks * cols, 2 * (rows + 3 * toks) * cols),
            compiler_params=room(),
            name="merge",
        )(target_col, back[p], back[p], mixed_s, stats_s)
        finals.append(exchange(merged.reshape(n_head, here, cols), "head"))
    attended = jnp.transpose(jnp.stack(finals, axis=2), (1, 0, 2, 3)).reshape(here, n_head * width)
    suffix_cache = jnp.transpose(kv, (0, 2, 1, 3)).reshape(toks, 2, width)
    return (attended, suffix_cache)


TEAM = 4
FEATURES = 7168
CODE = 1024
FAR = (192, 208, 224, 240)
NEAR = 256
MOST = 384
INNER = ((0, 512), (512, 768), (768, 896))
OUTER = ((0, 384), (384, 640), (640, 896))
TURNS = ((0, 1), (2,), (3,))
PARTS = len(TURNS)
FIRST = INNER[0][1]
STAT = 8
MESH = pl.DeviceIdType.MESH


def place():
    tok = lax.axis_index("tok")
    half = lax.axis_index("head")
    return lax.div(tok, TEAM), lax.rem(tok, TEAM), half


def team_at(member, level):
    return {"tok": level * TEAM + lax.rem(member, TEAM), "head": lax.div(member, TEAM)}


def team_rows(member, rows):
    at = (lax.rem(member, TEAM) * 2 + lax.div(member, TEAM)) * rows
    return pl.ds(pl.multiple_of(at, 16), rows)


def band_cols(member, low=0, wide=BAND):
    return pl.ds(pl.multiple_of(member * BAND + low, LANES), wide)


def layout(sizes):
    starts = [sum(sizes[:d]) for d in range(TEAM)]
    total = sum(sizes)
    return starts, total, -(-total // (16 * TEAM)) * 16


def note_layout(sizes):
    high = [-(-size // LANES) * STAT for size in sizes]
    return [sum(high[:d]) for d in range(TEAM)], high


def masked_window(query, j):
    low, high = window(j)
    cols = lane_iota((query.shape[0], high - low)) + low
    keep = (cols >= j * HD) & (cols < (j + 1) * HD)
    return jnp.where(keep, query, jnp.zeros((), query.dtype))


def tables_kernel(
    far_sizes, lengths_ref, groups_ref, owner_ref, qkv_ref, cache_ref,
    pool_ref, kv_ref, slot_ref, code_ref, req_ref, peak_ref,
    meta, table, cache, sm, rm, sq, rq, sl,
):
    level, work, half = place()
    tok = level * TEAM + work
    team = 2 * TEAM
    mine = half * TEAM + work
    n = lax.axis_size("tok")
    rows = qkv_ref.shape[1]
    width = kv_ref.shape[2]

    def tok_peer(d):
        return {"tok": lax.rem(tok + d, n), "head": half}

    def meta_copy(d, landing):
        return pltpu.make_async_remote_copy(
            src_ref=meta, dst_ref=table.at[landing], send_sem=sm.at[d], recv_sem=rm.at[d],
            device_id=tok_peer(d), device_id_type=MESH,
        )

    def query_copy(e, landing):
        peer = lax.rem(mine + e, team)
        return pltpu.make_async_remote_copy(
            src_ref=qkv_ref.at[0, :, band_cols(peer, 0, FIRST)],
            dst_ref=pool_ref.at[team_rows(landing, rows), :],
            send_sem=sq.at[e], recv_sem=rq.at[e],
            device_id=team_at(peer, level), device_id_type=MESH,
        )

    def each(body, count):
        def step(d, carry):
            body(d)
            return carry

        lax.fori_loop(1, count, step, 0)

    barrier = pltpu.get_barrier_semaphore()
    each(lambda d: pl.semaphore_signal(barrier, inc=1, device_id=tok_peer(d), device_id_type=MESH), n)
    for w in range(TEAM):
        pl.semaphore_signal(
            barrier, inc=1, device_id={"tok": level * TEAM + w, "head": 1 - half}, device_id_type=MESH
        )
    bring = pltpu.make_async_copy(cache_ref.at[0], cache, sl.at[0])
    bring.start()
    own = pltpu.make_async_copy(
        qkv_ref.at[0, :, band_cols(mine, 0, FIRST)], pool_ref.at[team_rows(mine, rows), :], sl.at[1]
    )
    own.start()
    count = lengths_ref.shape[1]
    meta[...] = jnp.zeros_like(meta)
    meta[0:1, 0:count] = lengths_ref[...]
    meta[1:2, 0:count] = groups_ref[...]
    pl.semaphore_wait(barrier, n - 1 + TEAM)
    each(lambda d: meta_copy(d, tok).start(), n)
    each(lambda e: query_copy(e, mine).start(), team)
    table[tok] = meta[...]
    bring.wait()
    past = kv_ref.shape[1]
    aim = lax.broadcasted_iota(jnp.int32, (past, 2 * past), 1)
    source = 2 * lax.broadcasted_iota(jnp.int32, (past, 2 * past), 0)
    even = jnp.where(aim == source, 1.0, 0.0).astype(jnp.bfloat16)
    odd = jnp.where(aim == source + 1, 1.0, 0.0).astype(jnp.bfloat16)

    def split(c, carry):
        span = pl.ds(pl.multiple_of(c * 2 * LANES, LANES), 2 * LANES)
        both = cache[:, :, span].reshape(2 * past, 2 * LANES)
        kv_ref[0, :, span] = dot_nn(even, both).astype(jnp.bfloat16)
        kv_ref[1, :, span] = dot_nn(odd, both).astype(jnp.bfloat16)
        return carry

    lax.fori_loop(0, width // (2 * LANES), split, 0)
    each(lambda d: meta_copy(d, lax.rem(tok + n - d, n)).wait_recv(), n)

    lengths = table[:, 0, :]
    groups = table[:, 1, :]
    slots = jnp.zeros_like(groups)
    owners = owner_ref[...]
    for g in range(owners.shape[1]):
        slots = jnp.where(groups == g, owners[:, g:g + 1], slots)
    spot = lane_iota((n, LANES))
    slot = jnp.zeros((n, LANES), jnp.int32)
    request = jnp.zeros((n, LANES), jnp.int32)
    end = jnp.zeros((n, 1), jnp.int32)
    for r in range(REQUESTS):
        start = end
        end = start + lengths[:, r:r + 1]
        inside = (spot >= start) & (spot < end)
        slot = jnp.where(inside, slots[:, r:r + 1], slot)
        request = jnp.where(inside, r, request)
    goal = lax.div(slot, TEAM)
    marks = [jnp.where(goal == z, 1.0, 0.0) for z in range(TEAM)]
    hot = jnp.concatenate(marks, axis=0).astype(jnp.bfloat16)
    down = lax.broadcasted_iota(jnp.int32, (LANES, LANES), 0)
    upto = jnp.where(down <= lane_iota((LANES, LANES)), 1.0, 0.0).astype(jnp.bfloat16)
    running = dot_nn(hot, upto)
    totals = dot_nn(hot, jnp.ones((LANES, LANES), jnp.bfloat16))
    m = TEAM * n
    a = lax.broadcasted_iota(jnp.int32, (m, m), 0)
    b = lax.broadcasted_iota(jnp.int32, (m, m), 1)
    earlier = (lax.div(a, TEAM) == lax.div(b, TEAM)) & (b < a)
    before = dot_nn(jnp.where(earlier, 1.0, 0.0).astype(jnp.bfloat16), totals.astype(jnp.bfloat16))
    count = (running + before).astype(jnp.int32)
    code = jnp.zeros((n, LANES), jnp.int32)
    for z in range(TEAM):
        code = jnp.where(goal == z, z * CODE + count[z * n:(z + 1) * n] - 1, code)
    slot = slot - goal * TEAM
    for z in range(TEAM):
        part = slice(z * TEAM, (z + 1) * TEAM)
        slot_ref[z] = slot[part]
        code_ref[z] = code[part]
        req_ref[z] = request[part]
    aim = lax.div(lax.broadcasted_iota(jnp.int32, (m, LANES), 0), n)
    source = lax.div(lax.rem(lax.broadcasted_iota(jnp.int32, (m, LANES), 0), n), TEAM)
    far = lax.div(aim, 2) != lax.div(source, 2)
    need = jnp.where(far, count, jnp.where(count > NEAR, MOST, 0))
    most = jnp.max(need)
    choice = jnp.int32(0)
    for size in far_sizes:
        choice = choice + (most > size).astype(jnp.int32)
    peak_ref[0, 0] = choice

    own.wait()
    each(lambda e: query_copy(e, lax.rem(mine + team - e, team)).wait_recv(), team)
    each(lambda d: meta_copy(d, tok).wait_send(), n)
    each(lambda e: query_copy(e, mine).wait_send(), team)


def pool_kernel(
    scale, sizes, early_ref, kv_ref, slot_ref, code_ref, req_ref, qkv_ref, out_ref, pair_ref,
    pool_ref, mixed, local, outgo, income, result, back, stats, cols, keep, fresh, final,
    note_out, note_in, notes, picks, pair,
    s1, r1, s2, r2, s3, r3, s4, r4, s5, r5, s6, r6, s7, r7, s8, r8, sl,
):
    level, work, half = place()
    team = 2 * TEAM
    mine = half * TEAM + work
    rows = qkv_ref.shape[1]
    toks = 2 * rows
    width = kv_ref.shape[2]
    starts, total_rows, block = layout(sizes)
    note_starts, note_sizes = note_layout(sizes)
    partners = (
        level, level + 1 - 2 * lax.rem(level, 2), lax.rem(level + 2, TEAM), TEAM - 1 - level,
    )
    order = (2, 3, 1)
    inner, outer = INNER, OUTER

    def rows_of(d):
        return slice(starts[d], starts[d] + sizes[d])

    def note_rows(d):
        return slice(note_starts[d], note_starts[d] + note_sizes[d])

    def level_id(d):
        return {"tok": partners[d] * TEAM + work, "head": half}

    def query_copy(e, landing):
        peer = lax.rem(mine + e, team)
        return pltpu.make_async_remote_copy(
            src_ref=qkv_ref.at[0, :, band_cols(peer, FIRST, BAND - FIRST)],
            dst_ref=pool_ref.at[team_rows(landing, rows), FIRST:BAND],
            send_sem=s8.at[e], recv_sem=r8.at[e],
            device_id=team_at(peer, level), device_id_type=MESH,
        )

    def forth_copy(d, part):
        span = slice(*inner[part])
        return pltpu.make_async_remote_copy(
            src_ref=outgo.at[rows_of(d), span], dst_ref=income.at[rows_of(d), span],
            send_sem=s1.at[part, d], recv_sem=r1.at[part, d],
            device_id=level_id(d), device_id_type=MESH,
        )

    def back_copy(d, part):
        span = slice(*outer[part])
        return pltpu.make_async_remote_copy(
            src_ref=result.at[rows_of(d), span], dst_ref=back.at[rows_of(d), span],
            send_sem=s2.at[part, d], recv_sem=r2.at[part, d],
            device_id=level_id(d), device_id_type=MESH,
        )

    def note_copy(d, part):
        return pltpu.make_async_remote_copy(
            src_ref=note_out.at[part, note_rows(d), :], dst_ref=note_in.at[part, note_rows(d), :],
            send_sem=s6.at[part, d], recv_sem=r6.at[part, d],
            device_id=level_id(d), device_id_type=MESH,
        )

    def cache_copy(e, part, landing):
        peer = lax.rem(work + e, TEAM)
        low, high = inner[part]
        return pltpu.make_async_remote_copy(
            src_ref=kv_ref.at[:, :, band_cols(peer, low, high - low)],
            dst_ref=keep.at[landing, :, :, low:high],
            send_sem=s3.at[part, e], recv_sem=r3.at[part, e],
            device_id={"tok": level * TEAM + peer, "head": half}, device_id_type=MESH,
        )

    def fresh_copy(e, part, landing):
        peer = lax.rem(mine + e, team)
        low, high = inner[part]
        return pltpu.make_async_remote_copy(
            src_ref=qkv_ref.at[1:3, :, band_cols(peer, low, high - low)],
            dst_ref=fresh.at[:, team_rows(landing, rows), low:high],
            send_sem=s4.at[part, e], recv_sem=r4.at[part, e],
            device_id=team_at(peer, level), device_id_type=MESH,
        )

    def final_copy(e, part, landing):
        peer = lax.rem(mine + e, team)
        low, high = outer[part]
        return pltpu.make_async_remote_copy(
            src_ref=final.at[team_rows(peer, rows), low:high],
            dst_ref=out_ref.at[:, band_cols(landing, low, high - low)],
            send_sem=s5.at[part, e], recv_sem=r5.at[part, e],
            device_id=team_at(peer, level), device_id_type=MESH,
        )

    def half_cols(which):
        return pl.ds(pl.multiple_of(which * width, LANES), width)

    swap = pltpu.make_async_remote_copy(
        src_ref=qkv_ref.at[1:3, :, half_cols(1 - half)], dst_ref=pair.at[1],
        send_sem=s7.at[0], recv_sem=r7.at[0],
        device_id={"tok": level * TEAM + work, "head": 1 - half}, device_id_type=MESH,
    )

    def weave(which, owner):
        where = pl.ds(pl.multiple_of(owner * rows, 16), rows)

        def step(c, carry):
            span = pl.ds(pl.multiple_of(c * LANES, LANES), LANES)
            pair_ref[where, 0, span] = pair[which, 0, :, span]
            pair_ref[where, 1, span] = pair[which, 1, :, span]
            return carry

        lax.fori_loop(0, width // LANES, step, 0)

    barrier = pltpu.get_barrier_semaphore()
    for e in range(1, team):
        pl.semaphore_signal(barrier, inc=1, device_id=team_at(lax.rem(mine + e, team), level), device_id_type=MESH)
    for d in range(1, TEAM):
        pl.semaphore_signal(barrier, inc=1, device_id=level_id(d), device_id_type=MESH)
    own_query = pltpu.make_async_copy(
        qkv_ref.at[0, :, band_cols(mine, FIRST, BAND - FIRST)],
        pool_ref.at[team_rows(mine, rows), FIRST:BAND], sl.at[4],
    )
    own_query.start()
    early = pltpu.make_async_copy(early_ref, pool_ref.at[:, 0:FIRST], sl.at[3])
    early.start()
    own_fresh = pltpu.make_async_copy(
        qkv_ref.at[1:3, :, band_cols(mine)], fresh.at[:, team_rows(mine, rows), :], sl.at[1]
    )
    own_fresh.start()
    own_pair = pltpu.make_async_copy(qkv_ref.at[1:3, :, half_cols(half)], pair.at[0], sl.at[2])
    own_pair.start()
    own_cache = pltpu.make_async_copy(kv_ref.at[:, :, band_cols(work)], keep.at[work], sl.at[0])
    own_cache.start()

    def flat(ref, z):
        entry = ref[z]
        return jnp.concatenate([entry[i:i + 1] for i in range(TEAM)], axis=1)

    code = flat(code_ref, level)

    def packed(d, part):
        source = early_ref[...] if part == 0 else pool_ref[:, FIRST:BAND]
        down = lax.broadcasted_iota(jnp.int32, (sizes[d], TEAM * toks), 0)
        pick = jnp.where(down == code - partners[d] * CODE, 1.0, 0.0).astype(jnp.bfloat16)
        return dot_nn(pick, source).astype(jnp.bfloat16)

    for d in order:
        outgo[rows_of(d), 0:FIRST] = packed(d, 0)
    pl.semaphore_wait(barrier, team - 1 + TEAM - 1)
    for d in order:
        forth_copy(d, 0).start()
    for e in range(1, team):
        query_copy(e, mine).start()
    for part in range(PARTS):
        for e in range(1, TEAM):
            cache_copy(e, part, work).start()
    for late in range(PARTS):
        for e in range(1, team):
            fresh_copy(e, late, mine).start()
    swap.start()
    own_query.wait()
    early.wait()
    for e in range(1, team):
        query_copy(e, lax.rem(mine + team - e, team)).wait_recv()
    for d in order:
        outgo[rows_of(d), FIRST:BAND] = packed(d, 1)
        forth_copy(d, 1).start()
    for part in range(2, PARTS):
        for d in order:
            forth_copy(d, part).start()
    income[rows_of(0), 0:FIRST] = packed(0, 0)
    income[rows_of(0), FIRST:BAND] = packed(0, 1)
    for d in range(TEAM):
        down = lax.broadcasted_iota(jnp.int32, (sizes[d], TEAM * toks), 0)
        hit = down == flat(code_ref, partners[d]) - level * CODE
        seats = flat(slot_ref, partners[d]).astype(jnp.float32)
        found = jnp.sum(jnp.where(hit, seats, 0.0), axis=1, keepdims=True)
        cols[rows_of(d), :] = jnp.broadcast_to(found, (sizes[d], LANES))
    spare = TEAM * block - total_rows
    if spare:
        income[total_rows:TEAM * block, :] = jnp.zeros((spare, BAND), jnp.bfloat16)
        cols[total_rows:TEAM * block, :] = jnp.zeros((spare, LANES), jnp.float32)
    stats[...] = jnp.zeros_like(stats)
    own_pair.wait()
    weave(0, half)
    own_cache.wait()

    def heads_of(part):
        return TURNS[part]

    def assemble(part, outs, old, keep_tile):
        stop = -(-(TURNS[part][-1] + 1) * HD // LANES)
        for tile in range(outer[part][0] // LANES, stop):
            owners = owners_of(tile)
            first, last = owners[0], owners[-1]

            def cut(j):
                return outs[j][:, tile * LANES - window(j)[0]:][:, :LANES]

            if last not in outs:
                values = cut(first)
            elif first in outs:
                values = by_tile(tile, cut)
            else:
                before = old(tile)
                values = jnp.where(lane_iota(before.shape) < last * HD - tile * LANES, before, cut(last))
            keep_tile(tile, values)

    def prefix(part):
        def run(b, carry):
            span = pl.ds(pl.multiple_of(b * block, 16), block)
            which = cols[span, :][:, :1]
            lanes = lane_iota((block, LANES))
            noted = stats[span, :]
            outs = {}
            for j in heads_of(part):
                low, high = window(j)
                asked = masked_window(income[span, low:high], j)
                scores = None
                for s in range(TEAM):
                    some = dot_nt(asked, keep[s, 0, :, low:high])
                    scores = some if s == 0 else jnp.where(which == s, some, scores)
                scores = scores * scale
                top = jnp.max(scores, axis=1, keepdims=True)
                raised = jnp.exp(scores - top)
                total = jnp.sum(raised, axis=1, keepdims=True)
                out = None
                for s in range(TEAM):
                    weights = jnp.where(which == s, raised, 0.0).astype(jnp.bfloat16)
                    term = dot_nn(weights, keep[s, 1, :, low:high])
                    out = term if s == 0 else out + term
                outs[j] = out / total
                noted = jnp.where(lanes == j, top, noted)
                noted = jnp.where(lanes == PER + j, total, noted)

            def put(tile, values):
                result[span, tile * LANES:(tile + 1) * LANES] = values.astype(jnp.bfloat16)

            def old(tile):
                return result[span, tile * LANES:(tile + 1) * LANES].astype(jnp.float32)

            assemble(part, outs, old, put)
            stats[span, :] = noted
            return carry

        lax.fori_loop(0, TEAM, run, 0)
        for d in order:
            back_copy(d, part).start()
        for d in range(TEAM):
            high = note_sizes[d]
            folded = None
            for k in range(LANES // STAT):
                piece = stats[starts[d] + k * high:starts[d] + (k + 1) * high, :]
                folded = piece if k == 0 else folded + pltpu.roll(piece, k * STAT, 1)
            note_out[part, note_rows(d), :] = folded
            if d:
                note_copy(d, part).start()

    for part in range(PARTS):
        for d in order:
            forth_copy(d, part).wait_recv()
        for e in range(1, TEAM):
            cache_copy(e, part, lax.rem(work + TEAM - e, TEAM)).wait_recv()
        prefix(part)
        if part == 0:
            swap.wait_recv()
            weave(1, 1 - half)
    back[rows_of(0), :] = result[rows_of(0), :]
    note_in[:, note_rows(0), :] = note_out[:, note_rows(0), :]
    own_fresh.wait()

    eye = lax.broadcasted_iota(jnp.int32, (toks, toks), 0) == lane_iota((toks, toks))
    causal = lane_iota((toks, toks)) <= lax.broadcasted_iota(jnp.int32, (toks, toks), 0)
    lanes = lane_iota((toks, LANES))

    def column(row):
        return jnp.sum(jnp.where(eye, row, 0.0), axis=1, keepdims=True)

    def choose(i, carry):
        span = pl.ds(pl.multiple_of(i * toks, toks), toks)
        codes = code_ref[level, pl.ds(i, 1), :]
        goal = lax.div(codes, CODE)
        seat = codes - goal * CODE
        for d in range(1, TEAM):
            seat = jnp.where(goal == partners[d], seat + starts[d], seat)
        seat = column(seat.astype(jnp.float32)).astype(jnp.int32)
        picks[span, :] = jnp.where(lane_iota((toks, total_rows)) == seat, 1.0, 0.0).astype(jnp.bfloat16)
        local[span, :] = jnp.zeros((toks, LANES), jnp.float32)
        return carry

    lax.fori_loop(0, TEAM, choose, 0)

    def suffix(part):
        def run(i, carry):
            span = pl.ds(pl.multiple_of(i * toks, toks), toks)
            asks = req_ref[level, pl.ds(i, 1), :].astype(jnp.float32)
            allowed = (column(asks) == asks) & causal
            noted = local[span, :]
            outs = {}
            for j in heads_of(part):
                low, high = window(j)
                scores = dot_nt(masked_window(pool_ref[span, low:high], j), fresh[0, span, low:high]) * scale
                scores = jnp.where(allowed, scores, -jnp.inf)
                peak = jnp.max(scores, axis=1, keepdims=True)
                raised = jnp.exp(scores - peak)
                total = jnp.sum(raised, axis=1, keepdims=True)
                outs[j] = dot_nn(raised.astype(jnp.bfloat16), fresh[1, span, low:high])
                noted = jnp.where(lanes == j, peak, noted)
                noted = jnp.where(lanes == PER + j, total, noted)

            def put(tile, values):
                mixed[span, tile * LANES:(tile + 1) * LANES] = values

            def old(tile):
                return mixed[span, tile * LANES:(tile + 1) * LANES]

            assemble(part, outs, old, put)
            local[span, :] = noted
            return carry

        lax.fori_loop(0, TEAM, run, 0)

    def unfold(part):
        for d in range(TEAM):
            piece = note_in[part, note_rows(d), :]
            turned = [piece] + [pltpu.roll(piece, LANES - k * STAT, 1) for k in range(1, LANES // STAT)]
            full = jnp.concatenate(turned, axis=0)[:sizes[d]]
            full = jnp.where(lane_iota((sizes[d], LANES)) < STAT, full, 0.0)
            high = full.astype(jnp.bfloat16).astype(jnp.float32)
            rest = full - high
            mid = rest.astype(jnp.bfloat16).astype(jnp.float32)
            packed = high + pltpu.roll(mid, STAT, 1) + pltpu.roll(rest - mid, 2 * STAT, 1)
            notes[rows_of(d), :] = packed.astype(jnp.bfloat16)

    def finish(part):
        low, high = outer[part]

        def run(turn, carry):
            k = lax.rem(turn + 1, TEAM)
            span = pl.ds(pl.multiple_of(lax.rem(work + k, TEAM) * toks, toks), toks)
            pick = picks[span, :]
            packed = dot_nn(pick, notes[...])
            prior = (packed + pltpu.roll(packed, LANES - STAT, 1)) + pltpu.roll(packed, LANES - 2 * STAT, 1)
            ready = dot_nn(pick, back[:, low:high])
            noted = local[span, :]
            top = jnp.maximum(prior, noted)
            first = pltpu.roll(prior, LANES - PER, 1) * jnp.exp(prior - top)
            second = jnp.exp(noted - top)
            below = first + second * pltpu.roll(noted, LANES - PER, 1)
            wp = first / below
            ws = second / below
            for tile in range(low // LANES, high // LANES):
                at = slice(tile * LANES, (tile + 1) * LANES)
                values = (
                    by_tile(tile, lambda j: wp[:, j:j + 1]) * ready[:, tile * LANES - low:][:, :LANES]
                    + by_tile(tile, lambda j: ws[:, j:j + 1]) * mixed[span, at]
                )
                final[span, at] = values.astype(jnp.bfloat16)

            @pl.when(k > 0)
            def _():
                final_copy(k, part, mine).start()

            final_copy(k + TEAM, part, mine).start()
            return carry

        lax.fori_loop(0, TEAM, run, 0)

    for part in range(PARTS):
        for e in range(1, team):
            fresh_copy(e, part, lax.rem(mine + team - e, team)).wait_recv()
        suffix(part)
        for d in order:
            back_copy(d, part).wait_recv()
            note_copy(d, part).wait_recv()
        unfold(part)
        finish(part)
    out_ref[:, band_cols(mine)] = final[team_rows(mine, rows), :]
    for part in range(PARTS):
        for e in range(1, team):
            final_copy(e, part, lax.rem(mine + team - e, team)).wait_recv()
    swap.wait_send()
    for e in range(1, team):
        query_copy(e, mine).wait_send()
    for part in range(PARTS):
        for d in range(1, TEAM):
            note_copy(d, part).wait_send()
            forth_copy(d, part).wait_send()
            back_copy(d, part).wait_send()
        for e in range(1, TEAM):
            cache_copy(e, part, work).wait_send()
        for e in range(1, team):
            fresh_copy(e, part, mine).wait_send()
            final_copy(e, part, mine).wait_send()


REQUESTS = 8


def pooled_device(qkv, prefix_cache, suffix_lengths, request_groups, prefix_owner):
    n_head = lax.axis_size("head")
    n_tok = lax.axis_size("tok")
    here = qkv.shape[0]
    width = qkv.shape[2] // n_head
    toks = here * n_head
    scale = 1.0 / math.sqrt(HD)
    past = prefix_cache.shape[1]
    planes = jnp.transpose(qkv, (1, 0, 2))
    vmem = pl.BlockSpec(memory_space=pltpu.VMEM)
    smem = pl.BlockSpec(memory_space=pltpu.SMEM)
    hbm = pl.BlockSpec(memory_space=pltpu.HBM)
    free = pl.BlockSpec(memory_space=pl.ANY)
    dma = pltpu.SemaphoreType.DMA
    table = jax.ShapeDtypeStruct((TEAM, TEAM, LANES), jnp.int32)

    early, kv, slot, code, request, peak = pl.pallas_call(
        functools.partial(tables_kernel, FAR),
        out_shape=[
            jax.ShapeDtypeStruct((TEAM * toks, FIRST), jnp.bfloat16),
            jax.ShapeDtypeStruct((2, past, width), jnp.bfloat16),
            table, table, table, jax.ShapeDtypeStruct((1, 1), jnp.int32),
        ],
        in_specs=[vmem, vmem, vmem, hbm, hbm],
        out_specs=[vmem] * 5 + [smem],
        scratch_shapes=[
            pltpu.VMEM((8, LANES), jnp.int32),
            pltpu.VMEM((n_tok, 8, LANES), jnp.int32),
            pltpu.VMEM((past, 2, width), jnp.bfloat16),
            dma((n_tok,)), dma((n_tok,)), dma((2 * TEAM,)), dma((2 * TEAM,)), dma((2,)),
        ],
        compiler_params=pltpu.CompilerParams(
            collective_id=0, has_side_effects=True, vmem_limit_bytes=62 * 1024 * 1024
        ),
        name="tables",
    )(suffix_lengths, request_groups, prefix_owner[None], planes, prefix_cache)

    def pooled(sizes, number):
        total, block = layout(sizes)[1:]
        marks = sum(note_layout(sizes)[1])
        bf16, f32 = jnp.bfloat16, jnp.float32
        two, team = (PARTS, TEAM), (PARTS, 2 * TEAM)

        def call(early, kv, slot, code, request, planes):
            return pl.pallas_call(
                functools.partial(pool_kernel, scale, sizes),
                out_shape=[
                    jax.ShapeDtypeStruct((here, n_head * width), bf16),
                    jax.ShapeDtypeStruct((toks, 2, width), bf16),
                ],
                in_specs=[vmem, free, vmem, vmem, vmem, hbm],
                out_specs=[vmem] * 2,
                scratch_shapes=[
                    pltpu.VMEM((TEAM * toks, BAND), bf16),
                    pltpu.VMEM((TEAM * toks, BAND), f32),
                    pltpu.VMEM((TEAM * toks, LANES), f32),
                    pltpu.VMEM((total, BAND), bf16),
                    pltpu.VMEM((TEAM * block, BAND), bf16),
                    pltpu.VMEM((TEAM * block, BAND), bf16),
                    pltpu.VMEM((total, BAND), bf16),
                    pltpu.VMEM((TEAM * block + LANES, LANES), f32),
                    pltpu.VMEM((TEAM * block, LANES), f32),
                    pltpu.VMEM((TEAM, 2, past, BAND), bf16),
                    pltpu.VMEM((2, TEAM * toks, BAND), bf16),
                    pltpu.VMEM((TEAM * toks, BAND), bf16),
                    pltpu.VMEM((PARTS, marks, LANES), f32),
                    pltpu.VMEM((PARTS, marks, LANES), f32),
                    pltpu.VMEM((total, LANES), bf16),
                    pltpu.VMEM((TEAM * toks, total), bf16),
                    pltpu.VMEM((2, 2, here, width), bf16),
                    dma(two), dma(two), dma(two), dma(two), dma(two), dma(two),
                    dma(team), dma(team), dma(team), dma(team), dma(two), dma(two),
                    dma((1,)), dma((1,)), dma((2 * TEAM,)), dma((2 * TEAM,)), dma((5,)),
                ],
                compiler_params=pltpu.CompilerParams(
                    collective_id=number, has_side_effects=True, vmem_limit_bytes=52 * 1024 * 1024
                ),
                name="pooled",
            )(early, kv, slot, code, request, planes)

        return call

    choices = [(NEAR, NEAR, size, size) for size in FAR] + [(MOST,) * TEAM]
    return lax.switch(
        peak[0, 0], [pooled(sizes, 1 + i) for i, sizes in enumerate(choices)],
        early, kv, slot, code, request, planes,
    )


def solution(mesh):
    in_specs = (
        P(("tok", "head"), None, None),
        P("tok", None, None, "head"),
        P("tok", None),
        P("tok", None),
        P(),
    )
    out_specs = (P(("tok", "head"), None), P("tok", None, "head"))
    pooled = mesh.shape["tok"] == TEAM * TEAM and BAND * TEAM * mesh.shape["head"] == FEATURES
    body = pooled_device if pooled else generic_device
    return jax.shard_map(
        body, mesh=mesh, in_specs=in_specs, out_specs=out_specs, check_vma=False
    )
```

```python
import functools
import math

import jax
import jax.numpy as jnp
from jax import lax
from jax.experimental import pallas as pl
from jax.experimental.pallas import tpu as pltpu
from jax.sharding import PartitionSpec as P

HD = 224
LANES = 128
BAND = math.lcm(HD, LANES)
PER = BAND // HD
LSPLIT = 16
PIECE = 2 * LSPLIT


def window(j):
    low = j * HD // LANES * LANES
    high = -(-(j + 1) * HD // LANES) * LANES
    return low, high


def owners_of(tile):
    first = tile * LANES // HD
    last = ((tile + 1) * LANES - 1) // HD
    return first, last


def lane_iota(shape):
    return lax.broadcasted_iota(jnp.int32, shape, len(shape) - 1)


def by_tile(tile, pick):
    first, last = owners_of(tile)
    left = pick(first)
    if first == last:
        return left
    right = pick(last)
    edge = last * HD - tile * LANES
    return jnp.where(lane_iota((right.shape[0], LANES)) < edge, left, right)


def masked_query(query, j):
    low, high = window(j)
    cols = lane_iota((query.shape[0], high - low)) + low
    keep = (cols >= j * HD) & (cols < (j + 1) * HD)
    return jnp.where(keep, query[:, low:high], jnp.zeros((), query.dtype))


def dot_nt(a, b):
    return lax.dot_general(a, b, (((1,), (1,)), ((), ())), preferred_element_type=jnp.float32)


def dot_nn(a, b):
    return lax.dot_general(a, b, (((1,), (0,)), ((), ())), preferred_element_type=jnp.float32)


def spread_kernel(target_ref, query_ref, out_ref):
    rows = out_ref.shape[0]
    toks = target_ref.shape[1]
    place = lax.broadcasted_iota(jnp.int32, (rows, toks), 0)
    pick = jnp.where(place == target_ref[...], 1.0, 0.0).astype(jnp.bfloat16)
    out_ref[...] = dot_nn(pick, query_ref[...]).astype(jnp.bfloat16)


def attend(query, keys, values, allowed, scale, normalise, put, stats_ref, band=None):
    band = pl.program_id(0) if band is None else band
    rows = query.shape[0]
    lanes = lane_iota((rows, LANES))

    if isinstance(band, int):
        stats = jnp.zeros_like(stats_ref) if band == 0 else stats_ref[...]
    else:

        @pl.when(band == 0)
        def _():
            stats_ref[...] = jnp.zeros_like(stats_ref)

        stats = stats_ref[...]
    mixed = []
    for j in range(PER):
        low, high = window(j)
        scores = dot_nt(masked_query(query, j), keys[:, low:high]) * scale
        if allowed is not None:
            scores = jnp.where(allowed, scores, -jnp.inf)
        peak = jnp.max(scores, axis=1, keepdims=True)
        raised = jnp.exp(scores - peak)
        total = jnp.sum(raised, axis=1, keepdims=True)
        out = dot_nn(raised.astype(jnp.bfloat16), values[:, low:high])
        if normalise:
            out = out / total
        mixed.append(out)
        head = band * PER + j
        stats = jnp.where(lanes == head, peak, stats)
        stats = jnp.where(lanes == head + LSPLIT, total, stats)
    stats_ref[...] = stats
    for tile in range(BAND // LANES):
        put(tile, by_tile(tile, lambda j: mixed[j][:, tile * LANES - window(j)[0]:][:, :LANES]))


def prefix_kernel(scale, query_ref, key_ref, value_ref, out_ref, stats_ref):
    band = pl.program_id(0)
    bands = pl.num_programs(0)
    width = out_ref.shape[1] - LANES

    def put(tile, cols):
        at = pl.multiple_of(band * BAND + tile * LANES, LANES)
        out_ref[:, pl.ds(at, LANES)] = cols.astype(out_ref.dtype)

    attend(query_ref[...], key_ref[...], value_ref[...], None, scale, True, put, stats_ref)

    @pl.when(band == bands - 1)
    def _():
        full = stats_ref[...]
        high = full.astype(jnp.bfloat16).astype(jnp.float32)
        rest = full - high
        mid = rest.astype(jnp.bfloat16).astype(jnp.float32)
        low = rest - mid
        packed = high + pltpu.roll(mid, PIECE, 1) + pltpu.roll(low, 2 * PIECE, 1)
        out_ref[:, width:] = packed.astype(out_ref.dtype)


def suffix_kernel(scale, reqc_ref, reqr_ref, query_ref, key_ref, value_ref, out_ref, stats_ref):
    toks = query_ref.shape[0]
    shape = (toks, toks)
    allowed = (reqc_ref[...] == reqr_ref[...]) & (
        lax.broadcasted_iota(jnp.int32, shape, 1) <= lax.broadcasted_iota(jnp.int32, shape, 0)
    )

    def put(tile, cols):
        out_ref[:, tile * LANES:(tile + 1) * LANES] = cols

    keys = key_ref[...].reshape(toks, BAND)
    values = value_ref[...].reshape(toks, BAND)
    attend(query_ref[...], keys, values, allowed, scale, False, put, stats_ref)


def merge_kernel(target_ref, back_ref, pstats_ref, mixed_ref, sstats_ref, out_ref):
    band = pl.program_id(0)
    rows = back_ref.shape[0]
    toks = target_ref.shape[0]
    place = lane_iota((toks, rows))
    pick = jnp.where(place == target_ref[...], 1.0, 0.0).astype(jnp.bfloat16)
    packed = dot_nn(pick, pstats_ref[...])
    prefix = (packed + pltpu.roll(packed, LANES - PIECE, 1)) + pltpu.roll(
        packed, LANES - 2 * PIECE, 1
    )
    suffix = sstats_ref[...]
    top = jnp.maximum(prefix, suffix)
    first = pltpu.roll(prefix, LANES - LSPLIT, 1) * jnp.exp(prefix - top)
    second = jnp.exp(suffix - top)
    below = first + second * pltpu.roll(suffix, LANES - LSPLIT, 1)
    wp = first / below
    ws = second / below
    lanes = lane_iota((toks, LANES))

    def column(weights, j):
        return jnp.sum(jnp.where(lanes == band * PER + j, weights, 0.0), axis=1, keepdims=True)

    cp = [column(wp, j) for j in range(PER)]
    cs = [column(ws, j) for j in range(PER)]
    for tile in range(BAND // LANES):
        cols = slice(tile * LANES, (tile + 1) * LANES)
        back = dot_nn(pick, back_ref[:, cols])
        merged = by_tile(tile, lambda j: cp[j]) * back + by_tile(tile, lambda j: cs[j]) * mixed_ref[:, cols]
        out_ref[:, cols] = merged.astype(out_ref.dtype)


def whole_block(array):
    return pl.BlockSpec(array.shape, lambda g: (0,) * array.ndim)


def band_block(rows, off=0):
    return pl.BlockSpec((rows, BAND), lambda g: (0, g + off))


def cost(flops, moved):
    return pl.CostEstimate(flops=flops, bytes_accessed=moved, transcendentals=0)


def room():
    return pltpu.CompilerParams(vmem_limit_bytes=48 * 1024 * 1024)


def exchange(x, axis):
    return lax.all_to_all(x, axis, split_axis=0, concat_axis=0, tiled=True)


def shift_exchange(x, axis):
    n = lax.axis_size(axis)
    me = lax.axis_index(axis)
    parts = [lax.dynamic_index_in_dim(x, me, 0, keepdims=False)]
    for d in range(1, n):
        ring = [(i, (i + d) % n) for i in range(n)]
        sent = lax.dynamic_index_in_dim(x, lax.rem(me + d, n), 0, keepdims=False)
        parts.append(lax.ppermute(sent, axis, ring))
    out = []
    for source in range(n):
        picked = parts[0]
        for d in range(1, n):
            picked = jnp.where(lax.rem(me + n - source, n) == d, parts[d], picked)
        out.append(picked)
    return jnp.stack(out)


def generic_device(qkv, prefix_cache, suffix_lengths, request_groups, prefix_owner):
    n_head = lax.axis_size("head")
    n_tok = lax.axis_size("tok")
    here = qkv.shape[0]
    width = qkv.shape[2] // n_head
    toks = here * n_head
    scale = 1.0 / math.sqrt(HD)
    bands = width // BAND
    parts = 1
    each = bands // parts
    cols = each * BAND
    capacity = 3 * toks // n_tok
    rows = n_tok * capacity
    planes = jnp.transpose(qkv, (1, 0, 2)).reshape(3, here, n_head, width)
    queries = [
        exchange(
            jnp.stack([qkv[:, 0, h * width:(h + 1) * width] for h in range(n_head)]), "head"
        ).reshape(toks, cols)
        for p in range(parts)
    ]
    kv_send = jnp.transpose(planes[1:], (2, 0, 1, 3))

    lengths = suffix_lengths[0]
    groups = request_groups[0]
    requests = lengths.shape[0]
    ends = jnp.sum(jnp.where(jnp.arange(requests)[:, None] <= jnp.arange(requests)[None, :], lengths[:, None], 0), axis=0)
    starts = ends - lengths
    slots = jnp.sum(jnp.where(groups[:, None] == jnp.arange(n_tok)[None, :], prefix_owner[None, :], 0), axis=1)
    position = jnp.arange(toks, dtype=jnp.int32)
    request = jnp.sum((position[:, None] >= ends[None, :]).astype(jnp.int32), axis=1)
    base = slots * capacity - starts
    inside = request[:, None] == jnp.arange(requests, dtype=jnp.int32)[None, :]
    target = (position + jnp.sum(jnp.where(inside, base[None, :], 0), axis=1)).astype(jnp.int32)
    target_row = target[None, :]
    target_col = target[:, None]
    reqc, reqr = request[:, None], request[None, :]

    prefix_len = prefix_cache.shape[1]
    queries[0], cache_keys, cache_values = lax.optimization_barrier(
        (queries[0], prefix_cache[0, :, 0], prefix_cache[0, :, 1])
    )
    received = []
    for p in range(parts):
        outgoing = pl.pallas_call(
            spread_kernel,
            grid=(each,),
            out_shape=jax.ShapeDtypeStruct((rows, cols), jnp.bfloat16),
            in_specs=[whole_block(target_row), band_block(toks)],
            out_specs=band_block(rows),
            cost_estimate=cost(2 * rows * toks * cols, 2 * (rows + toks) * cols),
            compiler_params=room(),
            name="spread",
        )(target_row, queries[p])
        if p == 0:
            outgoing, kv_send = lax.optimization_barrier((outgoing, kv_send))
        received.append(exchange(outgoing.reshape(n_tok, capacity, cols), "tok").reshape(rows, cols))
    kv = shift_exchange(kv_send, "head")

    back = []
    for p in range(parts):
        mixed = pl.pallas_call(
            functools.partial(prefix_kernel, scale),
            grid=(each,),
            out_shape=jax.ShapeDtypeStruct((rows, cols + LANES), jnp.bfloat16),
            in_specs=[band_block(rows), band_block(prefix_len, p * each), band_block(prefix_len, p * each)],
            out_specs=pl.BlockSpec((rows, cols + LANES), lambda g: (0, 0)),
            scratch_shapes=[pltpu.VMEM((rows, LANES), jnp.float32)],
            cost_estimate=cost(4 * rows * prefix_len * cols, 4 * (rows + prefix_len) * cols),
            compiler_params=room(),
            name="prefix",
        )(received[p], cache_keys, cache_values)
        back.append(exchange(mixed.reshape(n_tok, capacity, cols + LANES), "tok").reshape(rows, cols + LANES))

    finals = []
    for p in range(parts):
        key_spec = pl.BlockSpec((n_head, None, here, BAND), lambda g, p=p: (0, 0, 0, g + p * each))
        value_spec = pl.BlockSpec((n_head, None, here, BAND), lambda g, p=p: (0, 1, 0, g + p * each))
        mixed_s, stats_s = pl.pallas_call(
            functools.partial(suffix_kernel, scale),
            grid=(each,),
            out_shape=[
                jax.ShapeDtypeStruct((toks, cols), jnp.float32),
                jax.ShapeDtypeStruct((toks, LANES), jnp.float32),
            ],
            in_specs=[whole_block(reqc), whole_block(reqr), band_block(toks), key_spec, value_spec],
            out_specs=[band_block(toks), pl.BlockSpec((toks, LANES), lambda g: (0, 0))],
            cost_estimate=cost(4 * toks * toks * cols, 10 * toks * cols),
            compiler_params=room(),
            name="suffix",
        )(reqc, reqr, queries[p], kv, kv)
        merged = pl.pallas_call(
            merge_kernel,
            grid=(each,),
            out_shape=jax.ShapeDtypeStruct((toks, cols), jnp.bfloat16),
            in_specs=[
                whole_block(target_col),
                band_block(rows),
                pl.BlockSpec((rows, LANES), lambda g: (0, cols // LANES)),
                band_block(toks),
                whole_block(stats_s),
            ],
            out_specs=band_block(toks),
            cost_estimate=cost(2 * rows * toks * cols, 2 * (rows + 3 * toks) * cols),
            compiler_params=room(),
            name="merge",
        )(target_col, back[p], back[p], mixed_s, stats_s)
        finals.append(exchange(merged.reshape(n_head, here, cols), "head"))
    attended = jnp.transpose(jnp.stack(finals, axis=2), (1, 0, 2, 3)).reshape(here, n_head * width)
    suffix_cache = jnp.transpose(kv, (0, 2, 1, 3)).reshape(toks, 2, width)
    return (attended, suffix_cache)


TEAM = 4
FEATURES = 7168
CODE = 1024
FAR = (192, 208, 240)
NEAR = 256
MOST = 384
INNER = ((0, 512), (512, 768), (768, 896))
OUTER = ((0, 384), (384, 640), (640, 896))
TURNS = ((0, 1), (2,), (3,))
PARTS = len(TURNS)
FIRST = INNER[0][1]
STAT = 8
MESH = pl.DeviceIdType.MESH


def place():
    tok = lax.axis_index("tok")
    half = lax.axis_index("head")
    return lax.div(tok, TEAM), lax.rem(tok, TEAM), half


def team_at(member, level):
    return {"tok": level * TEAM + lax.rem(member, TEAM), "head": lax.div(member, TEAM)}


def team_rows(member, rows):
    at = (lax.rem(member, TEAM) * 2 + lax.div(member, TEAM)) * rows
    return pl.ds(pl.multiple_of(at, 16), rows)


def band_cols(member, low=0, wide=BAND):
    return pl.ds(pl.multiple_of(member * BAND + low, LANES), wide)


def layout(sizes):
    starts = [sum(sizes[:d]) for d in range(TEAM)]
    total = sum(sizes)
    return starts, total, -(-total // (16 * TEAM)) * 16


def note_layout(sizes):
    high = [-(-size // LANES) * STAT for size in sizes]
    return [sum(high[:d]) for d in range(TEAM)], high


def masked_window(query, j):
    low, high = window(j)
    cols = lane_iota((query.shape[0], high - low)) + low
    keep = (cols >= j * HD) & (cols < (j + 1) * HD)
    return jnp.where(keep, query, jnp.zeros((), query.dtype))


def tables_kernel(
    far_sizes, lengths_ref, groups_ref, owner_ref, qkv_ref, cache_ref,
    pool_ref, kv_ref, slot_ref, code_ref, req_ref, peak_ref,
    meta, table, cache, sm, rm, sq, rq, sl,
):
    level, work, half = place()
    tok = level * TEAM + work
    team = 2 * TEAM
    mine = half * TEAM + work
    n = lax.axis_size("tok")
    rows = qkv_ref.shape[1]
    width = kv_ref.shape[2]

    def tok_peer(d):
        return {"tok": lax.rem(tok + d, n), "head": half}

    def meta_copy(d, landing):
        return pltpu.make_async_remote_copy(
            src_ref=meta, dst_ref=table.at[landing], send_sem=sm.at[d], recv_sem=rm.at[d],
            device_id=tok_peer(d), device_id_type=MESH,
        )

    def query_copy(e, landing):
        peer = lax.rem(mine + e, team)
        return pltpu.make_async_remote_copy(
            src_ref=qkv_ref.at[0, :, band_cols(peer, 0, FIRST)],
            dst_ref=pool_ref.at[team_rows(landing, rows), :],
            send_sem=sq.at[e], recv_sem=rq.at[e],
            device_id=team_at(peer, level), device_id_type=MESH,
        )

    def each(body, count):
        def step(d, carry):
            body(d)
            return carry

        lax.fori_loop(1, count, step, 0)

    barrier = pltpu.get_barrier_semaphore()
    each(lambda d: pl.semaphore_signal(barrier, inc=1, device_id=tok_peer(d), device_id_type=MESH), n)
    for w in range(TEAM):
        pl.semaphore_signal(
            barrier, inc=1, device_id={"tok": level * TEAM + w, "head": 1 - half}, device_id_type=MESH
        )
    bring = pltpu.make_async_copy(cache_ref.at[0], cache, sl.at[0])
    bring.start()
    own = pltpu.make_async_copy(
        qkv_ref.at[0, :, band_cols(mine, 0, FIRST)], pool_ref.at[team_rows(mine, rows), :], sl.at[1]
    )
    own.start()
    count = lengths_ref.shape[1]
    meta[...] = jnp.zeros_like(meta)
    meta[0:1, 0:count] = lengths_ref[...]
    meta[1:2, 0:count] = groups_ref[...]
    pl.semaphore_wait(barrier, n - 1 + TEAM)
    each(lambda d: meta_copy(d, tok).start(), n)
    each(lambda e: query_copy(e, mine).start(), team)
    table[tok] = meta[...]
    bring.wait()
    past = kv_ref.shape[1]
    aim = lax.broadcasted_iota(jnp.int32, (past, 2 * past), 1)
    source = 2 * lax.broadcasted_iota(jnp.int32, (past, 2 * past), 0)
    even = jnp.where(aim == source, 1.0, 0.0).astype(jnp.bfloat16)
    odd = jnp.where(aim == source + 1, 1.0, 0.0).astype(jnp.bfloat16)

    def split(c, carry):
        span = pl.ds(pl.multiple_of(c * 2 * LANES, LANES), 2 * LANES)
        both = cache[:, :, span].reshape(2 * past, 2 * LANES)
        kv_ref[0, :, span] = dot_nn(even, both).astype(jnp.bfloat16)
        kv_ref[1, :, span] = dot_nn(odd, both).astype(jnp.bfloat16)
        return carry

    lax.fori_loop(0, width // (2 * LANES), split, 0)
    each(lambda d: meta_copy(d, lax.rem(tok + n - d, n)).wait_recv(), n)

    lengths = table[:, 0, :]
    groups = table[:, 1, :]
    slots = jnp.zeros_like(groups)
    owners = owner_ref[...]
    for g in range(owners.shape[1]):
        slots = jnp.where(groups == g, owners[:, g:g + 1], slots)
    spot = lane_iota((n, LANES))
    slot = jnp.zeros((n, LANES), jnp.int32)
    request = jnp.zeros((n, LANES), jnp.int32)
    end = jnp.zeros((n, 1), jnp.int32)
    for r in range(REQUESTS):
        start = end
        end = start + lengths[:, r:r + 1]
        inside = (spot >= start) & (spot < end)
        slot = jnp.where(inside, slots[:, r:r + 1], slot)
        request = jnp.where(inside, r, request)
    goal = lax.div(slot, TEAM)
    marks = [jnp.where(goal == z, 1.0, 0.0) for z in range(TEAM)]
    hot = jnp.concatenate(marks, axis=0).astype(jnp.bfloat16)
    down = lax.broadcasted_iota(jnp.int32, (LANES, LANES), 0)
    upto = jnp.where(down <= lane_iota((LANES, LANES)), 1.0, 0.0).astype(jnp.bfloat16)
    running = dot_nn(hot, upto)
    totals = dot_nn(hot, jnp.ones((LANES, LANES), jnp.bfloat16))
    m = TEAM * n
    a = lax.broadcasted_iota(jnp.int32, (m, m), 0)
    b = lax.broadcasted_iota(jnp.int32, (m, m), 1)
    earlier = (lax.div(a, TEAM) == lax.div(b, TEAM)) & (b < a)
    before = dot_nn(jnp.where(earlier, 1.0, 0.0).astype(jnp.bfloat16), totals.astype(jnp.bfloat16))
    count = (running + before).astype(jnp.int32)
    code = jnp.zeros((n, LANES), jnp.int32)
    for z in range(TEAM):
        code = jnp.where(goal == z, z * CODE + count[z * n:(z + 1) * n] - 1, code)
    slot = slot - goal * TEAM
    for z in range(TEAM):
        part = slice(z * TEAM, (z + 1) * TEAM)
        slot_ref[z] = slot[part]
        code_ref[z] = code[part]
        req_ref[z] = request[part]
    aim = lax.div(lax.broadcasted_iota(jnp.int32, (m, LANES), 0), n)
    source = lax.div(lax.rem(lax.broadcasted_iota(jnp.int32, (m, LANES), 0), n), TEAM)
    far = lax.div(aim, 2) != lax.div(source, 2)
    need = jnp.where(far, count, jnp.where(count > NEAR, MOST, 0))
    most = jnp.max(need)
    choice = jnp.int32(0)
    for size in far_sizes:
        choice = choice + (most > size).astype(jnp.int32)
    peak_ref[0, 0] = choice

    own.wait()
    each(lambda e: query_copy(e, lax.rem(mine + team - e, team)).wait_recv(), team)
    each(lambda d: meta_copy(d, tok).wait_send(), n)
    each(lambda e: query_copy(e, mine).wait_send(), team)


def pool_kernel(
    scale, sizes, early_ref, kv_ref, slot_ref, code_ref, req_ref, qkv_ref, out_ref, pair_ref,
    pool_ref, mixed, local, outgo, income, result, back, stats, cols, keep, fresh, final,
    note_out, note_in, notes, picks, pair,
    s1, r1, s2, r2, s3, r3, s4, r4, s5, r5, s6, r6, s7, r7, s8, r8, sl,
):
    level, work, half = place()
    team = 2 * TEAM
    mine = half * TEAM + work
    rows = qkv_ref.shape[1]
    toks = 2 * rows
    width = kv_ref.shape[2]
    starts, total_rows, block = layout(sizes)
    note_starts, note_sizes = note_layout(sizes)
    partners = (
        level, level + 1 - 2 * lax.rem(level, 2), lax.rem(level + 2, TEAM), TEAM - 1 - level,
    )
    order = (2, 3, 1)
    inner, outer = INNER, OUTER

    def rows_of(d):
        return slice(starts[d], starts[d] + sizes[d])

    def note_rows(d):
        return slice(note_starts[d], note_starts[d] + note_sizes[d])

    def level_id(d):
        return {"tok": partners[d] * TEAM + work, "head": half}

    def query_copy(e, landing):
        peer = lax.rem(mine + e, team)
        return pltpu.make_async_remote_copy(
            src_ref=qkv_ref.at[0, :, band_cols(peer, FIRST, BAND - FIRST)],
            dst_ref=pool_ref.at[team_rows(landing, rows), FIRST:BAND],
            send_sem=s8.at[e], recv_sem=r8.at[e],
            device_id=team_at(peer, level), device_id_type=MESH,
        )

    def forth_copy(d, part):
        span = slice(*inner[part])
        return pltpu.make_async_remote_copy(
            src_ref=outgo.at[rows_of(d), span], dst_ref=income.at[rows_of(d), span],
            send_sem=s1.at[part, d], recv_sem=r1.at[part, d],
            device_id=level_id(d), device_id_type=MESH,
        )

    def back_copy(d, part):
        span = slice(*outer[part])
        return pltpu.make_async_remote_copy(
            src_ref=result.at[rows_of(d), span], dst_ref=back.at[rows_of(d), span],
            send_sem=s2.at[part, d], recv_sem=r2.at[part, d],
            device_id=level_id(d), device_id_type=MESH,
        )

    def note_copy(d, part):
        return pltpu.make_async_remote_copy(
            src_ref=note_out.at[part, note_rows(d), :], dst_ref=note_in.at[part, note_rows(d), :],
            send_sem=s6.at[part, d], recv_sem=r6.at[part, d],
            device_id=level_id(d), device_id_type=MESH,
        )

    def cache_copy(e, part, landing):
        peer = lax.rem(work + e, TEAM)
        low, high = inner[part]
        return pltpu.make_async_remote_copy(
            src_ref=kv_ref.at[:, :, band_cols(peer, low, high - low)],
            dst_ref=keep.at[landing, :, :, low:high],
            send_sem=s3.at[part, e], recv_sem=r3.at[part, e],
            device_id={"tok": level * TEAM + peer, "head": half}, device_id_type=MESH,
        )

    def fresh_copy(e, part, landing):
        peer = lax.rem(mine + e, team)
        low, high = inner[part]
        return pltpu.make_async_remote_copy(
            src_ref=qkv_ref.at[1:3, :, band_cols(peer, low, high - low)],
            dst_ref=fresh.at[:, team_rows(landing, rows), low:high],
            send_sem=s4.at[part, e], recv_sem=r4.at[part, e],
            device_id=team_at(peer, level), device_id_type=MESH,
        )

    def final_copy(e, part, landing):
        peer = lax.rem(mine + e, team)
        low, high = outer[part]
        return pltpu.make_async_remote_copy(
            src_ref=final.at[team_rows(peer, rows), low:high],
            dst_ref=out_ref.at[:, band_cols(landing, low, high - low)],
            send_sem=s5.at[part, e], recv_sem=r5.at[part, e],
            device_id=team_at(peer, level), device_id_type=MESH,
        )

    def half_cols(which):
        return pl.ds(pl.multiple_of(which * width, LANES), width)

    swap = pltpu.make_async_remote_copy(
        src_ref=qkv_ref.at[1:3, :, half_cols(1 - half)], dst_ref=pair.at[1],
        send_sem=s7.at[0], recv_sem=r7.at[0],
        device_id={"tok": level * TEAM + work, "head": 1 - half}, device_id_type=MESH,
    )

    def weave(which, owner):
        where = pl.ds(pl.multiple_of(owner * rows, 16), rows)

        def step(c, carry):
            span = pl.ds(pl.multiple_of(c * LANES, LANES), LANES)
            pair_ref[where, 0, span] = pair[which, 0, :, span]
            pair_ref[where, 1, span] = pair[which, 1, :, span]
            return carry

        lax.fori_loop(0, width // LANES, step, 0)

    barrier = pltpu.get_barrier_semaphore()
    for e in range(1, team):
        pl.semaphore_signal(barrier, inc=1, device_id=team_at(lax.rem(mine + e, team), level), device_id_type=MESH)
    for d in range(1, TEAM):
        pl.semaphore_signal(barrier, inc=1, device_id=level_id(d), device_id_type=MESH)
    own_query = pltpu.make_async_copy(
        qkv_ref.at[0, :, band_cols(mine, FIRST, BAND - FIRST)],
        pool_ref.at[team_rows(mine, rows), FIRST:BAND], sl.at[4],
    )
    own_query.start()
    early = pltpu.make_async_copy(early_ref, pool_ref.at[:, 0:FIRST], sl.at[3])
    early.start()
    own_fresh = pltpu.make_async_copy(
        qkv_ref.at[1:3, :, band_cols(mine)], fresh.at[:, team_rows(mine, rows), :], sl.at[1]
    )
    own_fresh.start()
    own_pair = pltpu.make_async_copy(qkv_ref.at[1:3, :, half_cols(half)], pair.at[0], sl.at[2])
    own_pair.start()
    own_cache = pltpu.make_async_copy(kv_ref.at[:, :, band_cols(work)], keep.at[work], sl.at[0])
    own_cache.start()

    def flat(ref, z):
        entry = ref[z]
        return jnp.concatenate([entry[i:i + 1] for i in range(TEAM)], axis=1)

    code = flat(code_ref, level)

    def packed(d, part):
        source = early_ref[...] if part == 0 else pool_ref[:, FIRST:BAND]
        down = lax.broadcasted_iota(jnp.int32, (sizes[d], TEAM * toks), 0)
        pick = jnp.where(down == code - partners[d] * CODE, 1.0, 0.0).astype(jnp.bfloat16)
        return dot_nn(pick, source).astype(jnp.bfloat16)

    for d in order:
        outgo[rows_of(d), 0:FIRST] = packed(d, 0)
    pl.semaphore_wait(barrier, team - 1 + TEAM - 1)
    for d in order:
        forth_copy(d, 0).start()
    for e in range(1, team):
        query_copy(e, mine).start()
    for part in range(PARTS):
        for e in range(1, TEAM):
            cache_copy(e, part, work).start()
    for late in range(PARTS):
        for e in range(1, team):
            fresh_copy(e, late, mine).start()
    swap.start()
    own_query.wait()
    early.wait()
    for e in range(1, team):
        query_copy(e, lax.rem(mine + team - e, team)).wait_recv()
    for d in order:
        outgo[rows_of(d), FIRST:BAND] = packed(d, 1)
        forth_copy(d, 1).start()
    for part in range(2, PARTS):
        for d in order:
            forth_copy(d, part).start()
    income[rows_of(0), 0:FIRST] = packed(0, 0)
    income[rows_of(0), FIRST:BAND] = packed(0, 1)
    for d in range(TEAM):
        down = lax.broadcasted_iota(jnp.int32, (sizes[d], TEAM * toks), 0)
        hit = down == flat(code_ref, partners[d]) - level * CODE
        seats = flat(slot_ref, partners[d]).astype(jnp.float32)
        found = jnp.sum(jnp.where(hit, seats, 0.0), axis=1, keepdims=True)
        cols[rows_of(d), :] = jnp.broadcast_to(found, (sizes[d], LANES))
    spare = TEAM * block - total_rows
    if spare:
        income[total_rows:TEAM * block, :] = jnp.zeros((spare, BAND), jnp.bfloat16)
        cols[total_rows:TEAM * block, :] = jnp.zeros((spare, LANES), jnp.float32)
    stats[...] = jnp.zeros_like(stats)
    own_pair.wait()
    weave(0, half)
    own_cache.wait()

    def heads_of(part):
        return TURNS[part]

    def assemble(part, outs, old, keep_tile):
        stop = -(-(TURNS[part][-1] + 1) * HD // LANES)
        for tile in range(outer[part][0] // LANES, stop):
            owners = owners_of(tile)
            first, last = owners[0], owners[-1]

            def cut(j):
                return outs[j][:, tile * LANES - window(j)[0]:][:, :LANES]

            if last not in outs:
                values = cut(first)
            elif first in outs:
                values = by_tile(tile, cut)
            else:
                before = old(tile)
                values = jnp.where(lane_iota(before.shape) < last * HD - tile * LANES, before, cut(last))
            keep_tile(tile, values)

    def prefix(part):
        def run(b, carry):
            span = pl.ds(pl.multiple_of(b * block, 16), block)
            which = cols[span, :][:, :1]
            lanes = lane_iota((block, LANES))
            noted = stats[span, :]
            outs = {}
            for j in heads_of(part):
                low, high = window(j)
                asked = masked_window(income[span, low:high], j)
                scores = None
                for s in range(TEAM):
                    some = dot_nt(asked, keep[s, 0, :, low:high])
                    scores = some if s == 0 else jnp.where(which == s, some, scores)
                scores = scores * scale
                top = jnp.max(scores, axis=1, keepdims=True)
                raised = jnp.exp(scores - top)
                total = jnp.sum(raised, axis=1, keepdims=True)
                out = None
                for s in range(TEAM):
                    weights = jnp.where(which == s, raised, 0.0).astype(jnp.bfloat16)
                    term = dot_nn(weights, keep[s, 1, :, low:high])
                    out = term if s == 0 else out + term
                outs[j] = out / total
                noted = jnp.where(lanes == j, top, noted)
                noted = jnp.where(lanes == PER + j, total, noted)

            def put(tile, values):
                result[span, tile * LANES:(tile + 1) * LANES] = values.astype(jnp.bfloat16)

            def old(tile):
                return result[span, tile * LANES:(tile + 1) * LANES].astype(jnp.float32)

            assemble(part, outs, old, put)
            stats[span, :] = noted
            return carry

        lax.fori_loop(0, TEAM, run, 0)
        for d in order:
            back_copy(d, part).start()
        for d in range(TEAM):
            high = note_sizes[d]
            folded = None
            for k in range(LANES // STAT):
                piece = stats[starts[d] + k * high:starts[d] + (k + 1) * high, :]
                folded = piece if k == 0 else folded + pltpu.roll(piece, k * STAT, 1)
            note_out[part, note_rows(d), :] = folded
            if d:
                note_copy(d, part).start()

    for part in range(PARTS):
        for d in order:
            forth_copy(d, part).wait_recv()
        for e in range(1, TEAM):
            cache_copy(e, part, lax.rem(work + TEAM - e, TEAM)).wait_recv()
        prefix(part)
        if part == 0:
            swap.wait_recv()
            weave(1, 1 - half)
    back[rows_of(0), :] = result[rows_of(0), :]
    note_in[:, note_rows(0), :] = note_out[:, note_rows(0), :]
    own_fresh.wait()

    eye = lax.broadcasted_iota(jnp.int32, (toks, toks), 0) == lane_iota((toks, toks))
    causal = lane_iota((toks, toks)) <= lax.broadcasted_iota(jnp.int32, (toks, toks), 0)
    lanes = lane_iota((toks, LANES))

    def column(row):
        return jnp.sum(jnp.where(eye, row, 0.0), axis=1, keepdims=True)

    def choose(i, carry):
        span = pl.ds(pl.multiple_of(i * toks, toks), toks)
        codes = code_ref[level, pl.ds(i, 1), :]
        goal = lax.div(codes, CODE)
        seat = codes - goal * CODE
        for d in range(1, TEAM):
            seat = jnp.where(goal == partners[d], seat + starts[d], seat)
        seat = column(seat.astype(jnp.float32)).astype(jnp.int32)
        picks[span, :] = jnp.where(lane_iota((toks, total_rows)) == seat, 1.0, 0.0).astype(jnp.bfloat16)
        local[span, :] = jnp.zeros((toks, LANES), jnp.float32)
        return carry

    lax.fori_loop(0, TEAM, choose, 0)

    def suffix(part):
        def run(i, carry):
            span = pl.ds(pl.multiple_of(i * toks, toks), toks)
            asks = req_ref[level, pl.ds(i, 1), :].astype(jnp.float32)
            allowed = (column(asks) == asks) & causal
            noted = local[span, :]
            outs = {}
            for j in heads_of(part):
                low, high = window(j)
                scores = dot_nt(masked_window(pool_ref[span, low:high], j), fresh[0, span, low:high]) * scale
                scores = jnp.where(allowed, scores, -jnp.inf)
                peak = jnp.max(scores, axis=1, keepdims=True)
                raised = jnp.exp(scores - peak)
                total = jnp.sum(raised, axis=1, keepdims=True)
                outs[j] = dot_nn(raised.astype(jnp.bfloat16), fresh[1, span, low:high])
                noted = jnp.where(lanes == j, peak, noted)
                noted = jnp.where(lanes == PER + j, total, noted)

            def put(tile, values):
                mixed[span, tile * LANES:(tile + 1) * LANES] = values

            def old(tile):
                return mixed[span, tile * LANES:(tile + 1) * LANES]

            assemble(part, outs, old, put)
            local[span, :] = noted
            return carry

        lax.fori_loop(0, TEAM, run, 0)

    def unfold(part):
        for d in range(TEAM):
            piece = note_in[part, note_rows(d), :]
            turned = [piece] + [pltpu.roll(piece, LANES - k * STAT, 1) for k in range(1, LANES // STAT)]
            full = jnp.concatenate(turned, axis=0)[:sizes[d]]
            full = jnp.where(lane_iota((sizes[d], LANES)) < STAT, full, 0.0)
            high = full.astype(jnp.bfloat16).astype(jnp.float32)
            rest = full - high
            mid = rest.astype(jnp.bfloat16).astype(jnp.float32)
            packed = high + pltpu.roll(mid, STAT, 1) + pltpu.roll(rest - mid, 2 * STAT, 1)
            notes[rows_of(d), :] = packed.astype(jnp.bfloat16)

    def finish(part):
        low, high = outer[part]

        def run(turn, carry):
            k = lax.rem(turn + 1, TEAM)
            span = pl.ds(pl.multiple_of(lax.rem(work + k, TEAM) * toks, toks), toks)
            pick = picks[span, :]
            packed = dot_nn(pick, notes[...])
            prior = (packed + pltpu.roll(packed, LANES - STAT, 1)) + pltpu.roll(packed, LANES - 2 * STAT, 1)
            ready = dot_nn(pick, back[:, low:high])
            noted = local[span, :]
            top = jnp.maximum(prior, noted)
            first = pltpu.roll(prior, LANES - PER, 1) * jnp.exp(prior - top)
            second = jnp.exp(noted - top)
            below = first + second * pltpu.roll(noted, LANES - PER, 1)
            wp = first / below
            ws = second / below
            for tile in range(low // LANES, high // LANES):
                at = slice(tile * LANES, (tile + 1) * LANES)
                values = (
                    by_tile(tile, lambda j: wp[:, j:j + 1]) * ready[:, tile * LANES - low:][:, :LANES]
                    + by_tile(tile, lambda j: ws[:, j:j + 1]) * mixed[span, at]
                )
                final[span, at] = values.astype(jnp.bfloat16)

            @pl.when(k > 0)
            def _():
                final_copy(k, part, mine).start()

            final_copy(k + TEAM, part, mine).start()
            return carry

        lax.fori_loop(0, TEAM, run, 0)

    for part in range(PARTS):
        for e in range(1, team):
            fresh_copy(e, part, lax.rem(mine + team - e, team)).wait_recv()
        suffix(part)
        for d in order:
            back_copy(d, part).wait_recv()
            note_copy(d, part).wait_recv()
        unfold(part)
        finish(part)
    out_ref[:, band_cols(mine)] = final[team_rows(mine, rows), :]
    for part in range(PARTS):
        for e in range(1, team):
            final_copy(e, part, lax.rem(mine + team - e, team)).wait_recv()
    swap.wait_send()
    for e in range(1, team):
        query_copy(e, mine).wait_send()
    for part in range(PARTS):
        for d in range(1, TEAM):
            note_copy(d, part).wait_send()
            forth_copy(d, part).wait_send()
            back_copy(d, part).wait_send()
        for e in range(1, TEAM):
            cache_copy(e, part, work).wait_send()
        for e in range(1, team):
            fresh_copy(e, part, mine).wait_send()
            final_copy(e, part, mine).wait_send()


REQUESTS = 8


def pooled_device(qkv, prefix_cache, suffix_lengths, request_groups, prefix_owner):
    n_head = lax.axis_size("head")
    n_tok = lax.axis_size("tok")
    here = qkv.shape[0]
    width = qkv.shape[2] // n_head
    toks = here * n_head
    scale = 1.0 / math.sqrt(HD)
    past = prefix_cache.shape[1]
    planes = jnp.transpose(qkv, (1, 0, 2))
    vmem = pl.BlockSpec(memory_space=pltpu.VMEM)
    smem = pl.BlockSpec(memory_space=pltpu.SMEM)
    hbm = pl.BlockSpec(memory_space=pltpu.HBM)
    free = pl.BlockSpec(memory_space=pl.ANY)
    dma = pltpu.SemaphoreType.DMA
    table = jax.ShapeDtypeStruct((TEAM, TEAM, LANES), jnp.int32)

    early, kv, slot, code, request, peak = pl.pallas_call(
        functools.partial(tables_kernel, FAR),
        out_shape=[
            jax.ShapeDtypeStruct((TEAM * toks, FIRST), jnp.bfloat16),
            jax.ShapeDtypeStruct((2, past, width), jnp.bfloat16),
            table, table, table, jax.ShapeDtypeStruct((1, 1), jnp.int32),
        ],
        in_specs=[vmem, vmem, vmem, hbm, hbm],
        out_specs=[vmem] * 5 + [smem],
        scratch_shapes=[
            pltpu.VMEM((8, LANES), jnp.int32),
            pltpu.VMEM((n_tok, 8, LANES), jnp.int32),
            pltpu.VMEM((past, 2, width), jnp.bfloat16),
            dma((n_tok,)), dma((n_tok,)), dma((2 * TEAM,)), dma((2 * TEAM,)), dma((2,)),
        ],
        compiler_params=pltpu.CompilerParams(
            collective_id=0, has_side_effects=True, vmem_limit_bytes=62 * 1024 * 1024
        ),
        name="tables",
    )(suffix_lengths, request_groups, prefix_owner[None], planes, prefix_cache)

    def pooled(sizes, number):
        total, block = layout(sizes)[1:]
        marks = sum(note_layout(sizes)[1])
        bf16, f32 = jnp.bfloat16, jnp.float32
        two, team = (PARTS, TEAM), (PARTS, 2 * TEAM)

        def call(early, kv, slot, code, request, planes):
            return pl.pallas_call(
                functools.partial(pool_kernel, scale, sizes),
                out_shape=[
                    jax.ShapeDtypeStruct((here, n_head * width), bf16),
                    jax.ShapeDtypeStruct((toks, 2, width), bf16),
                ],
                in_specs=[vmem, free, vmem, vmem, vmem, hbm],
                out_specs=[vmem] * 2,
                scratch_shapes=[
                    pltpu.VMEM((TEAM * toks, BAND), bf16),
                    pltpu.VMEM((TEAM * toks, BAND), f32),
                    pltpu.VMEM((TEAM * toks, LANES), f32),
                    pltpu.VMEM((total, BAND), bf16),
                    pltpu.VMEM((TEAM * block, BAND), bf16),
                    pltpu.VMEM((TEAM * block, BAND), bf16),
                    pltpu.VMEM((total, BAND), bf16),
                    pltpu.VMEM((TEAM * block + LANES, LANES), f32),
                    pltpu.VMEM((TEAM * block, LANES), f32),
                    pltpu.VMEM((TEAM, 2, past, BAND), bf16),
                    pltpu.VMEM((2, TEAM * toks, BAND), bf16),
                    pltpu.VMEM((TEAM * toks, BAND), bf16),
                    pltpu.VMEM((PARTS, marks, LANES), f32),
                    pltpu.VMEM((PARTS, marks, LANES), f32),
                    pltpu.VMEM((total, LANES), bf16),
                    pltpu.VMEM((TEAM * toks, total), bf16),
                    pltpu.VMEM((2, 2, here, width), bf16),
                    dma(two), dma(two), dma(two), dma(two), dma(two), dma(two),
                    dma(team), dma(team), dma(team), dma(team), dma(two), dma(two),
                    dma((1,)), dma((1,)), dma((2 * TEAM,)), dma((2 * TEAM,)), dma((5,)),
                ],
                compiler_params=pltpu.CompilerParams(
                    collective_id=number, has_side_effects=True, vmem_limit_bytes=52 * 1024 * 1024
                ),
                name="pooled",
            )(early, kv, slot, code, request, planes)

        return call

    choices = [(NEAR, NEAR, size, size) for size in FAR] + [(MOST,) * TEAM]
    return lax.switch(
        peak[0, 0], [pooled(sizes, 1 + i) for i, sizes in enumerate(choices)],
        early, kv, slot, code, request, planes,
    )


def solution(mesh):
    in_specs = (
        P(("tok", "head"), None, None),
        P("tok", None, None, "head"),
        P("tok", None),
        P("tok", None),
        P(),
    )
    out_specs = (P(("tok", "head"), None), P("tok", None, "head"))
    pooled = mesh.shape["tok"] == TEAM * TEAM and BAND * TEAM * mesh.shape["head"] == FEATURES
    body = pooled_device if pooled else generic_device
    return jax.shard_map(
        body, mesh=mesh, in_specs=in_specs, out_specs=out_specs, check_vma=False
    )
```

```python
import functools
import math

import jax
import jax.numpy as jnp
from jax import lax
from jax.experimental import pallas as pl
from jax.experimental.pallas import tpu as pltpu
from jax.sharding import PartitionSpec as P

HD = 224
LANES = 128
BAND = math.lcm(HD, LANES)
PER = BAND // HD
LSPLIT = 16
PIECE = 2 * LSPLIT


def window(j):
    low = j * HD // LANES * LANES
    high = -(-(j + 1) * HD // LANES) * LANES
    return low, high


def owners_of(tile):
    first = tile * LANES // HD
    last = ((tile + 1) * LANES - 1) // HD
    return first, last


def lane_iota(shape):
    return lax.broadcasted_iota(jnp.int32, shape, len(shape) - 1)


def by_tile(tile, pick):
    first, last = owners_of(tile)
    left = pick(first)
    if first == last:
        return left
    right = pick(last)
    edge = last * HD - tile * LANES
    return jnp.where(lane_iota((right.shape[0], LANES)) < edge, left, right)


def masked_query(query, j):
    low, high = window(j)
    cols = lane_iota((query.shape[0], high - low)) + low
    keep = (cols >= j * HD) & (cols < (j + 1) * HD)
    return jnp.where(keep, query[:, low:high], jnp.zeros((), query.dtype))


def dot_nt(a, b):
    return lax.dot_general(a, b, (((1,), (1,)), ((), ())), preferred_element_type=jnp.float32)


def dot_nn(a, b):
    return lax.dot_general(a, b, (((1,), (0,)), ((), ())), preferred_element_type=jnp.float32)


def spread_kernel(target_ref, query_ref, out_ref):
    rows = out_ref.shape[0]
    toks = target_ref.shape[1]
    place = lax.broadcasted_iota(jnp.int32, (rows, toks), 0)
    pick = jnp.where(place == target_ref[...], 1.0, 0.0).astype(jnp.bfloat16)
    out_ref[...] = dot_nn(pick, query_ref[...]).astype(jnp.bfloat16)


def attend(query, keys, values, allowed, scale, normalise, put, stats_ref, band=None):
    band = pl.program_id(0) if band is None else band
    rows = query.shape[0]
    lanes = lane_iota((rows, LANES))

    if isinstance(band, int):
        stats = jnp.zeros_like(stats_ref) if band == 0 else stats_ref[...]
    else:

        @pl.when(band == 0)
        def _():
            stats_ref[...] = jnp.zeros_like(stats_ref)

        stats = stats_ref[...]
    mixed = []
    for j in range(PER):
        low, high = window(j)
        scores = dot_nt(masked_query(query, j), keys[:, low:high]) * scale
        if allowed is not None:
            scores = jnp.where(allowed, scores, -jnp.inf)
        peak = jnp.max(scores, axis=1, keepdims=True)
        raised = jnp.exp(scores - peak)
        total = jnp.sum(raised, axis=1, keepdims=True)
        out = dot_nn(raised.astype(jnp.bfloat16), values[:, low:high])
        if normalise:
            out = out / total
        mixed.append(out)
        head = band * PER + j
        stats = jnp.where(lanes == head, peak, stats)
        stats = jnp.where(lanes == head + LSPLIT, total, stats)
    stats_ref[...] = stats
    for tile in range(BAND // LANES):
        put(tile, by_tile(tile, lambda j: mixed[j][:, tile * LANES - window(j)[0]:][:, :LANES]))


def prefix_kernel(scale, query_ref, key_ref, value_ref, out_ref, stats_ref):
    band = pl.program_id(0)
    bands = pl.num_programs(0)
    width = out_ref.shape[1] - LANES

    def put(tile, cols):
        at = pl.multiple_of(band * BAND + tile * LANES, LANES)
        out_ref[:, pl.ds(at, LANES)] = cols.astype(out_ref.dtype)

    attend(query_ref[...], key_ref[...], value_ref[...], None, scale, True, put, stats_ref)

    @pl.when(band == bands - 1)
    def _():
        full = stats_ref[...]
        high = full.astype(jnp.bfloat16).astype(jnp.float32)
        rest = full - high
        mid = rest.astype(jnp.bfloat16).astype(jnp.float32)
        low = rest - mid
        packed = high + pltpu.roll(mid, PIECE, 1) + pltpu.roll(low, 2 * PIECE, 1)
        out_ref[:, width:] = packed.astype(out_ref.dtype)


def suffix_kernel(scale, reqc_ref, reqr_ref, query_ref, key_ref, value_ref, out_ref, stats_ref):
    toks = query_ref.shape[0]
    shape = (toks, toks)
    allowed = (reqc_ref[...] == reqr_ref[...]) & (
        lax.broadcasted_iota(jnp.int32, shape, 1) <= lax.broadcasted_iota(jnp.int32, shape, 0)
    )

    def put(tile, cols):
        out_ref[:, tile * LANES:(tile + 1) * LANES] = cols

    keys = key_ref[...].reshape(toks, BAND)
    values = value_ref[...].reshape(toks, BAND)
    attend(query_ref[...], keys, values, allowed, scale, False, put, stats_ref)


def merge_kernel(target_ref, back_ref, pstats_ref, mixed_ref, sstats_ref, out_ref):
    band = pl.program_id(0)
    rows = back_ref.shape[0]
    toks = target_ref.shape[0]
    place = lane_iota((toks, rows))
    pick = jnp.where(place == target_ref[...], 1.0, 0.0).astype(jnp.bfloat16)
    packed = dot_nn(pick, pstats_ref[...])
    prefix = (packed + pltpu.roll(packed, LANES - PIECE, 1)) + pltpu.roll(
        packed, LANES - 2 * PIECE, 1
    )
    suffix = sstats_ref[...]
    top = jnp.maximum(prefix, suffix)
    first = pltpu.roll(prefix, LANES - LSPLIT, 1) * jnp.exp(prefix - top)
    second = jnp.exp(suffix - top)
    below = first + second * pltpu.roll(suffix, LANES - LSPLIT, 1)
    wp = first / below
    ws = second / below
    lanes = lane_iota((toks, LANES))

    def column(weights, j):
        return jnp.sum(jnp.where(lanes == band * PER + j, weights, 0.0), axis=1, keepdims=True)

    cp = [column(wp, j) for j in range(PER)]
    cs = [column(ws, j) for j in range(PER)]
    for tile in range(BAND // LANES):
        cols = slice(tile * LANES, (tile + 1) * LANES)
        back = dot_nn(pick, back_ref[:, cols])
        merged = by_tile(tile, lambda j: cp[j]) * back + by_tile(tile, lambda j: cs[j]) * mixed_ref[:, cols]
        out_ref[:, cols] = merged.astype(out_ref.dtype)


def whole_block(array):
    return pl.BlockSpec(array.shape, lambda g: (0,) * array.ndim)


def band_block(rows, off=0):
    return pl.BlockSpec((rows, BAND), lambda g: (0, g + off))


def cost(flops, moved):
    return pl.CostEstimate(flops=flops, bytes_accessed=moved, transcendentals=0)


def room():
    return pltpu.CompilerParams(vmem_limit_bytes=48 * 1024 * 1024)


def exchange(x, axis):
    return lax.all_to_all(x, axis, split_axis=0, concat_axis=0, tiled=True)


def shift_exchange(x, axis):
    n = lax.axis_size(axis)
    me = lax.axis_index(axis)
    parts = [lax.dynamic_index_in_dim(x, me, 0, keepdims=False)]
    for d in range(1, n):
        ring = [(i, (i + d) % n) for i in range(n)]
        sent = lax.dynamic_index_in_dim(x, lax.rem(me + d, n), 0, keepdims=False)
        parts.append(lax.ppermute(sent, axis, ring))
    out = []
    for source in range(n):
        picked = parts[0]
        for d in range(1, n):
            picked = jnp.where(lax.rem(me + n - source, n) == d, parts[d], picked)
        out.append(picked)
    return jnp.stack(out)


def generic_device(qkv, prefix_cache, suffix_lengths, request_groups, prefix_owner):
    n_head = lax.axis_size("head")
    n_tok = lax.axis_size("tok")
    here = qkv.shape[0]
    width = qkv.shape[2] // n_head
    toks = here * n_head
    scale = 1.0 / math.sqrt(HD)
    bands = width // BAND
    parts = 1
    each = bands // parts
    cols = each * BAND
    capacity = 3 * toks // n_tok
    rows = n_tok * capacity
    planes = jnp.transpose(qkv, (1, 0, 2)).reshape(3, here, n_head, width)
    queries = [
        exchange(
            jnp.stack([qkv[:, 0, h * width:(h + 1) * width] for h in range(n_head)]), "head"
        ).reshape(toks, cols)
        for p in range(parts)
    ]
    kv_send = jnp.transpose(planes[1:], (2, 0, 1, 3))

    lengths = suffix_lengths[0]
    groups = request_groups[0]
    requests = lengths.shape[0]
    ends = jnp.sum(jnp.where(jnp.arange(requests)[:, None] <= jnp.arange(requests)[None, :], lengths[:, None], 0), axis=0)
    starts = ends - lengths
    slots = jnp.sum(jnp.where(groups[:, None] == jnp.arange(n_tok)[None, :], prefix_owner[None, :], 0), axis=1)
    position = jnp.arange(toks, dtype=jnp.int32)
    request = jnp.sum((position[:, None] >= ends[None, :]).astype(jnp.int32), axis=1)
    base = slots * capacity - starts
    inside = request[:, None] == jnp.arange(requests, dtype=jnp.int32)[None, :]
    target = (position + jnp.sum(jnp.where(inside, base[None, :], 0), axis=1)).astype(jnp.int32)
    target_row = target[None, :]
    target_col = target[:, None]
    reqc, reqr = request[:, None], request[None, :]

    prefix_len = prefix_cache.shape[1]
    queries[0], cache_keys, cache_values = lax.optimization_barrier(
        (queries[0], prefix_cache[0, :, 0], prefix_cache[0, :, 1])
    )
    received = []
    for p in range(parts):
        outgoing = pl.pallas_call(
            spread_kernel,
            grid=(each,),
            out_shape=jax.ShapeDtypeStruct((rows, cols), jnp.bfloat16),
            in_specs=[whole_block(target_row), band_block(toks)],
            out_specs=band_block(rows),
            cost_estimate=cost(2 * rows * toks * cols, 2 * (rows + toks) * cols),
            compiler_params=room(),
            name="spread",
        )(target_row, queries[p])
        if p == 0:
            outgoing, kv_send = lax.optimization_barrier((outgoing, kv_send))
        received.append(exchange(outgoing.reshape(n_tok, capacity, cols), "tok").reshape(rows, cols))
    kv = shift_exchange(kv_send, "head")

    back = []
    for p in range(parts):
        mixed = pl.pallas_call(
            functools.partial(prefix_kernel, scale),
            grid=(each,),
            out_shape=jax.ShapeDtypeStruct((rows, cols + LANES), jnp.bfloat16),
            in_specs=[band_block(rows), band_block(prefix_len, p * each), band_block(prefix_len, p * each)],
            out_specs=pl.BlockSpec((rows, cols + LANES), lambda g: (0, 0)),
            scratch_shapes=[pltpu.VMEM((rows, LANES), jnp.float32)],
            cost_estimate=cost(4 * rows * prefix_len * cols, 4 * (rows + prefix_len) * cols),
            compiler_params=room(),
            name="prefix",
        )(received[p], cache_keys, cache_values)
        back.append(exchange(mixed.reshape(n_tok, capacity, cols + LANES), "tok").reshape(rows, cols + LANES))

    finals = []
    for p in range(parts):
        key_spec = pl.BlockSpec((n_head, None, here, BAND), lambda g, p=p: (0, 0, 0, g + p * each))
        value_spec = pl.BlockSpec((n_head, None, here, BAND), lambda g, p=p: (0, 1, 0, g + p * each))
        mixed_s, stats_s = pl.pallas_call(
            functools.partial(suffix_kernel, scale),
            grid=(each,),
            out_shape=[
                jax.ShapeDtypeStruct((toks, cols), jnp.float32),
                jax.ShapeDtypeStruct((toks, LANES), jnp.float32),
            ],
            in_specs=[whole_block(reqc), whole_block(reqr), band_block(toks), key_spec, value_spec],
            out_specs=[band_block(toks), pl.BlockSpec((toks, LANES), lambda g: (0, 0))],
            cost_estimate=cost(4 * toks * toks * cols, 10 * toks * cols),
            compiler_params=room(),
            name="suffix",
        )(reqc, reqr, queries[p], kv, kv)
        merged = pl.pallas_call(
            merge_kernel,
            grid=(each,),
            out_shape=jax.ShapeDtypeStruct((toks, cols), jnp.bfloat16),
            in_specs=[
                whole_block(target_col),
                band_block(rows),
                pl.BlockSpec((rows, LANES), lambda g: (0, cols // LANES)),
                band_block(toks),
                whole_block(stats_s),
            ],
            out_specs=band_block(toks),
            cost_estimate=cost(2 * rows * toks * cols, 2 * (rows + 3 * toks) * cols),
            compiler_params=room(),
            name="merge",
        )(target_col, back[p], back[p], mixed_s, stats_s)
        finals.append(exchange(merged.reshape(n_head, here, cols), "head"))
    attended = jnp.transpose(jnp.stack(finals, axis=2), (1, 0, 2, 3)).reshape(here, n_head * width)
    suffix_cache = jnp.transpose(kv, (0, 2, 1, 3)).reshape(toks, 2, width)
    return (attended, suffix_cache)


TEAM = 4
FEATURES = 7168
CODE = 1024
FAR = (192, 208, 240)
NEAR = 256
MOST = 384
BLOCKS = 8
INNER = ((0, 512), (512, 768), (768, 896))
OUTER = ((0, 384), (384, 640), (640, 896))
TURNS = ((0, 1), (2,), (3,))
PARTS = len(TURNS)
FIRST = INNER[0][1]
STAT = 8
MESH = pl.DeviceIdType.MESH


def place():
    tok = lax.axis_index("tok")
    half = lax.axis_index("head")
    return lax.div(tok, TEAM), lax.rem(tok, TEAM), half


def team_at(member, level):
    return {"tok": level * TEAM + lax.rem(member, TEAM), "head": lax.div(member, TEAM)}


def team_rows(member, rows):
    at = (lax.rem(member, TEAM) * 2 + lax.div(member, TEAM)) * rows
    return pl.ds(pl.multiple_of(at, 16), rows)


def band_cols(member, low=0, wide=BAND):
    return pl.ds(pl.multiple_of(member * BAND + low, LANES), wide)


def layout(sizes):
    starts = [sum(sizes[:d]) for d in range(TEAM)]
    total = sum(sizes)
    return starts, total, -(-total // (16 * BLOCKS)) * 16


def note_layout(sizes):
    high = [-(-size // LANES) * STAT for size in sizes]
    return [sum(high[:d]) for d in range(TEAM)], high


def masked_window(query, j):
    low, high = window(j)
    cols = lane_iota((query.shape[0], high - low)) + low
    keep = (cols >= j * HD) & (cols < (j + 1) * HD)
    return jnp.where(keep, query, jnp.zeros((), query.dtype))


def tables_kernel(
    far_sizes, lengths_ref, groups_ref, owner_ref, qkv_ref, cache_ref,
    pool_ref, kv_ref, slot_ref, code_ref, req_ref, peak_ref,
    meta, table, cache, sm, rm, sq, rq, sl,
):
    level, work, half = place()
    tok = level * TEAM + work
    team = 2 * TEAM
    mine = half * TEAM + work
    n = lax.axis_size("tok")
    rows = qkv_ref.shape[1]
    width = kv_ref.shape[2]

    def tok_peer(d):
        return {"tok": lax.rem(tok + d, n), "head": half}

    def meta_copy(d, landing):
        return pltpu.make_async_remote_copy(
            src_ref=meta, dst_ref=table.at[landing], send_sem=sm.at[d], recv_sem=rm.at[d],
            device_id=tok_peer(d), device_id_type=MESH,
        )

    def query_copy(e, landing):
        peer = lax.rem(mine + e, team)
        return pltpu.make_async_remote_copy(
            src_ref=qkv_ref.at[0, :, band_cols(peer, 0, FIRST)],
            dst_ref=pool_ref.at[team_rows(landing, rows), :],
            send_sem=sq.at[e], recv_sem=rq.at[e],
            device_id=team_at(peer, level), device_id_type=MESH,
        )

    def each(body, count):
        def step(d, carry):
            body(d)
            return carry

        lax.fori_loop(1, count, step, 0)

    barrier = pltpu.get_barrier_semaphore()
    each(lambda d: pl.semaphore_signal(barrier, inc=1, device_id=tok_peer(d), device_id_type=MESH), n)
    for w in range(TEAM):
        pl.semaphore_signal(
            barrier, inc=1, device_id={"tok": level * TEAM + w, "head": 1 - half}, device_id_type=MESH
        )
    bring = pltpu.make_async_copy(cache_ref.at[0], cache, sl.at[0])
    bring.start()
    own = pltpu.make_async_copy(
        qkv_ref.at[0, :, band_cols(mine, 0, FIRST)], pool_ref.at[team_rows(mine, rows), :], sl.at[1]
    )
    own.start()
    count = lengths_ref.shape[1]
    meta[...] = jnp.zeros_like(meta)
    meta[0:1, 0:count] = lengths_ref[...]
    meta[1:2, 0:count] = groups_ref[...]
    pl.semaphore_wait(barrier, n - 1 + TEAM)
    each(lambda d: meta_copy(d, tok).start(), n)
    each(lambda e: query_copy(e, mine).start(), team)
    table[tok] = meta[...]
    bring.wait()
    past = kv_ref.shape[1]
    aim = lax.broadcasted_iota(jnp.int32, (past, 2 * past), 1)
    source = 2 * lax.broadcasted_iota(jnp.int32, (past, 2 * past), 0)
    even = jnp.where(aim == source, 1.0, 0.0).astype(jnp.bfloat16)
    odd = jnp.where(aim == source + 1, 1.0, 0.0).astype(jnp.bfloat16)

    def split(c, carry):
        span = pl.ds(pl.multiple_of(c * 2 * LANES, LANES), 2 * LANES)
        both = cache[:, :, span].reshape(2 * past, 2 * LANES)
        kv_ref[0, :, span] = dot_nn(even, both).astype(jnp.bfloat16)
        kv_ref[1, :, span] = dot_nn(odd, both).astype(jnp.bfloat16)
        return carry

    lax.fori_loop(0, width // (2 * LANES), split, 0)
    each(lambda d: meta_copy(d, lax.rem(tok + n - d, n)).wait_recv(), n)

    lengths = table[:, 0, :]
    groups = table[:, 1, :]
    slots = jnp.zeros_like(groups)
    owners = owner_ref[...]
    for g in range(owners.shape[1]):
        slots = jnp.where(groups == g, owners[:, g:g + 1], slots)
    spot = lane_iota((n, LANES))
    slot = jnp.zeros((n, LANES), jnp.int32)
    request = jnp.zeros((n, LANES), jnp.int32)
    end = jnp.zeros((n, 1), jnp.int32)
    for r in range(REQUESTS):
        start = end
        end = start + lengths[:, r:r + 1]
        inside = (spot >= start) & (spot < end)
        slot = jnp.where(inside, slots[:, r:r + 1], slot)
        request = jnp.where(inside, r, request)
    goal = lax.div(slot, TEAM)
    marks = [jnp.where(goal == z, 1.0, 0.0) for z in range(TEAM)]
    hot = jnp.concatenate(marks, axis=0).astype(jnp.bfloat16)
    down = lax.broadcasted_iota(jnp.int32, (LANES, LANES), 0)
    upto = jnp.where(down <= lane_iota((LANES, LANES)), 1.0, 0.0).astype(jnp.bfloat16)
    running = dot_nn(hot, upto)
    totals = dot_nn(hot, jnp.ones((LANES, LANES), jnp.bfloat16))
    m = TEAM * n
    a = lax.broadcasted_iota(jnp.int32, (m, m), 0)
    b = lax.broadcasted_iota(jnp.int32, (m, m), 1)
    earlier = (lax.div(a, TEAM) == lax.div(b, TEAM)) & (b < a)
    before = dot_nn(jnp.where(earlier, 1.0, 0.0).astype(jnp.bfloat16), totals.astype(jnp.bfloat16))
    count = (running + before).astype(jnp.int32)
    code = jnp.zeros((n, LANES), jnp.int32)
    for z in range(TEAM):
        code = jnp.where(goal == z, z * CODE + count[z * n:(z + 1) * n] - 1, code)
    slot = slot - goal * TEAM
    for z in range(TEAM):
        part = slice(z * TEAM, (z + 1) * TEAM)
        slot_ref[z] = slot[part]
        code_ref[z] = code[part]
        req_ref[z] = request[part]
    aim = lax.div(lax.broadcasted_iota(jnp.int32, (m, LANES), 0), n)
    source = lax.div(lax.rem(lax.broadcasted_iota(jnp.int32, (m, LANES), 0), n), TEAM)
    far = lax.div(aim, 2) != lax.div(source, 2)
    need = jnp.where(far, count, jnp.where(count > NEAR, MOST, 0))
    most = jnp.max(need)
    choice = jnp.int32(0)
    for size in far_sizes:
        choice = choice + (most > size).astype(jnp.int32)
    peak_ref[0, 0] = choice

    own.wait()
    each(lambda e: query_copy(e, lax.rem(mine + team - e, team)).wait_recv(), team)
    each(lambda d: meta_copy(d, tok).wait_send(), n)
    each(lambda e: query_copy(e, mine).wait_send(), team)


def pool_kernel(
    scale, sizes, early_ref, kv_ref, slot_ref, code_ref, req_ref, qkv_ref, out_ref, pair_ref,
    pool_ref, mixed, local, outgo, income, result, back, stats, cols, keep, fresh, final,
    note_out, note_in, notes, picks, pair,
    s1, r1, s2, r2, s3, r3, s4, r4, s5, r5, s6, r6, s7, r7, s8, r8, sl,
):
    level, work, half = place()
    team = 2 * TEAM
    mine = half * TEAM + work
    rows = qkv_ref.shape[1]
    toks = 2 * rows
    width = kv_ref.shape[2]
    starts, total_rows, block = layout(sizes)
    note_starts, note_sizes = note_layout(sizes)
    partners = (
        level, level + 1 - 2 * lax.rem(level, 2), lax.rem(level + 2, TEAM), TEAM - 1 - level,
    )
    order = (2, 3, 1)
    inner, outer = INNER, OUTER

    def rows_of(d):
        return slice(starts[d], starts[d] + sizes[d])

    def note_rows(d):
        return slice(note_starts[d], note_starts[d] + note_sizes[d])

    def level_id(d):
        return {"tok": partners[d] * TEAM + work, "head": half}

    def query_copy(e, landing):
        peer = lax.rem(mine + e, team)
        return pltpu.make_async_remote_copy(
            src_ref=qkv_ref.at[0, :, band_cols(peer, FIRST, BAND - FIRST)],
            dst_ref=pool_ref.at[team_rows(landing, rows), FIRST:BAND],
            send_sem=s8.at[e], recv_sem=r8.at[e],
            device_id=team_at(peer, level), device_id_type=MESH,
        )

    def forth_copy(d, part):
        span = slice(*inner[part])
        return pltpu.make_async_remote_copy(
            src_ref=outgo.at[rows_of(d), span], dst_ref=income.at[rows_of(d), span],
            send_sem=s1.at[part, d], recv_sem=r1.at[part, d],
            device_id=level_id(d), device_id_type=MESH,
        )

    def back_copy(d, part):
        span = slice(*outer[part])
        return pltpu.make_async_remote_copy(
            src_ref=result.at[rows_of(d), span], dst_ref=back.at[rows_of(d), span],
            send_sem=s2.at[part, d], recv_sem=r2.at[part, d],
            device_id=level_id(d), device_id_type=MESH,
        )

    def note_copy(d, part):
        return pltpu.make_async_remote_copy(
            src_ref=note_out.at[part, note_rows(d), :], dst_ref=note_in.at[part, note_rows(d), :],
            send_sem=s6.at[part, d], recv_sem=r6.at[part, d],
            device_id=level_id(d), device_id_type=MESH,
        )

    def cache_copy(e, part, landing):
        peer = lax.rem(work + e, TEAM)
        low, high = inner[part]
        return pltpu.make_async_remote_copy(
            src_ref=kv_ref.at[:, :, band_cols(peer, low, high - low)],
            dst_ref=keep.at[landing, :, :, low:high],
            send_sem=s3.at[part, e], recv_sem=r3.at[part, e],
            device_id={"tok": level * TEAM + peer, "head": half}, device_id_type=MESH,
        )

    def fresh_copy(e, part, landing):
        peer = lax.rem(mine + e, team)
        low, high = inner[part]
        return pltpu.make_async_remote_copy(
            src_ref=qkv_ref.at[1:3, :, band_cols(peer, low, high - low)],
            dst_ref=fresh.at[:, team_rows(landing, rows), low:high],
            send_sem=s4.at[part, e], recv_sem=r4.at[part, e],
            device_id=team_at(peer, level), device_id_type=MESH,
        )

    def final_copy(e, part, landing):
        peer = lax.rem(mine + e, team)
        low, high = outer[part]
        return pltpu.make_async_remote_copy(
            src_ref=final.at[team_rows(peer, rows), low:high],
            dst_ref=out_ref.at[:, band_cols(landing, low, high - low)],
            send_sem=s5.at[part, e], recv_sem=r5.at[part, e],
            device_id=team_at(peer, level), device_id_type=MESH,
        )

    def half_cols(which):
        return pl.ds(pl.multiple_of(which * width, LANES), width)

    swap = pltpu.make_async_remote_copy(
        src_ref=qkv_ref.at[1:3, :, half_cols(1 - half)], dst_ref=pair.at[1],
        send_sem=s7.at[0], recv_sem=r7.at[0],
        device_id={"tok": level * TEAM + work, "head": 1 - half}, device_id_type=MESH,
    )

    def weave(which, owner):
        where = pl.ds(pl.multiple_of(owner * rows, 16), rows)

        def step(c, carry):
            span = pl.ds(pl.multiple_of(c * LANES, LANES), LANES)
            pair_ref[where, 0, span] = pair[which, 0, :, span]
            pair_ref[where, 1, span] = pair[which, 1, :, span]
            return carry

        lax.fori_loop(0, width // LANES, step, 0)

    def each(count, step):
        def run(e, carry):
            step(e)
            return carry

        lax.fori_loop(1, count, run, 0)

    barrier = pltpu.get_barrier_semaphore()
    for e in range(1, team):
        pl.semaphore_signal(barrier, inc=1, device_id=team_at(lax.rem(mine + e, team), level), device_id_type=MESH)
    for d in range(1, TEAM):
        pl.semaphore_signal(barrier, inc=1, device_id=level_id(d), device_id_type=MESH)
    own_query = pltpu.make_async_copy(
        qkv_ref.at[0, :, band_cols(mine, FIRST, BAND - FIRST)],
        pool_ref.at[team_rows(mine, rows), FIRST:BAND], sl.at[4],
    )
    own_query.start()
    early = pltpu.make_async_copy(early_ref, pool_ref.at[:, 0:FIRST], sl.at[3])
    early.start()
    own_fresh = pltpu.make_async_copy(
        qkv_ref.at[1:3, :, band_cols(mine)], fresh.at[:, team_rows(mine, rows), :], sl.at[1]
    )
    own_fresh.start()
    own_pair = pltpu.make_async_copy(qkv_ref.at[1:3, :, half_cols(half)], pair.at[0], sl.at[2])
    own_pair.start()
    own_cache = pltpu.make_async_copy(kv_ref.at[:, :, band_cols(work)], keep.at[work], sl.at[0])
    own_cache.start()

    def flat(ref, z):
        entry = ref[z]
        return jnp.concatenate([entry[i:i + 1] for i in range(TEAM)], axis=1)

    code = flat(code_ref, level)

    def packed(d, part):
        source = early_ref[...] if part == 0 else pool_ref[:, FIRST:BAND]
        down = lax.broadcasted_iota(jnp.int32, (sizes[d], TEAM * toks), 0)
        pick = jnp.where(down == code - partners[d] * CODE, 1.0, 0.0).astype(jnp.bfloat16)
        return dot_nn(pick, source).astype(jnp.bfloat16)

    for d in order:
        outgo[rows_of(d), 0:FIRST] = packed(d, 0)
    pl.semaphore_wait(barrier, team - 1 + TEAM - 1)
    for d in order:
        forth_copy(d, 0).start()
    each(team, lambda e: query_copy(e, mine).start())
    for part in range(PARTS):
        each(TEAM, lambda e, part=part: cache_copy(e, part, work).start())
    for late in range(PARTS):
        each(team, lambda e, part=late: fresh_copy(e, part, mine).start())
    swap.start()
    own_query.wait()
    early.wait()
    each(team, lambda e: query_copy(e, lax.rem(mine + team - e, team)).wait_recv())
    for d in order:
        outgo[rows_of(d), FIRST:BAND] = packed(d, 1)
        forth_copy(d, 1).start()
    for part in range(2, PARTS):
        for d in order:
            forth_copy(d, part).start()
    income[rows_of(0), 0:FIRST] = packed(0, 0)
    income[rows_of(0), FIRST:BAND] = packed(0, 1)
    for d in range(TEAM):
        down = lax.broadcasted_iota(jnp.int32, (sizes[d], TEAM * toks), 0)
        hit = down == flat(code_ref, partners[d]) - level * CODE
        seats = flat(slot_ref, partners[d]).astype(jnp.float32)
        found = jnp.sum(jnp.where(hit, seats, 0.0), axis=1, keepdims=True)
        cols[rows_of(d), :] = jnp.broadcast_to(found, (sizes[d], LANES))
    spare = BLOCKS * block - total_rows
    if spare:
        income[total_rows:BLOCKS * block, :] = jnp.zeros((spare, BAND), jnp.bfloat16)
        cols[total_rows:BLOCKS * block, :] = jnp.zeros((spare, LANES), jnp.float32)
    stats[...] = jnp.zeros_like(stats)
    own_pair.wait()
    weave(0, half)
    own_cache.wait()

    def heads_of(part):
        return TURNS[part]

    def assemble(part, outs, old, keep_tile):
        stop = -(-(TURNS[part][-1] + 1) * HD // LANES)
        for tile in range(outer[part][0] // LANES, stop):
            owners = owners_of(tile)
            first, last = owners[0], owners[-1]

            def cut(j):
                return outs[j][:, tile * LANES - window(j)[0]:][:, :LANES]

            if last not in outs:
                values = cut(first)
            elif first in outs:
                values = by_tile(tile, cut)
            else:
                before = old(tile)
                values = jnp.where(lane_iota(before.shape) < last * HD - tile * LANES, before, cut(last))
            keep_tile(tile, values)

    def prefix(part):
        def run(b, carry):
            span = pl.ds(pl.multiple_of(b * block, 16), block)
            which = cols[span, :][:, :1]
            lanes = lane_iota((block, LANES))
            noted = stats[span, :]
            outs = {}
            for j in heads_of(part):
                low, high = window(j)
                asked = masked_window(income[span, low:high], j)
                scores = None
                for s in range(TEAM):
                    some = dot_nt(asked, keep[s, 0, :, low:high])
                    scores = some if s == 0 else jnp.where(which == s, some, scores)
                scores = scores * scale
                top = jnp.max(scores, axis=1, keepdims=True)
                raised = jnp.exp(scores - top)
                total = jnp.sum(raised, axis=1, keepdims=True)
                out = None
                for s in range(TEAM):
                    weights = jnp.where(which == s, raised, 0.0).astype(jnp.bfloat16)
                    term = dot_nn(weights, keep[s, 1, :, low:high])
                    out = term if s == 0 else out + term
                outs[j] = out / total
                noted = jnp.where(lanes == j, top, noted)
                noted = jnp.where(lanes == PER + j, total, noted)

            def put(tile, values):
                result[span, tile * LANES:(tile + 1) * LANES] = values.astype(jnp.bfloat16)

            def old(tile):
                return result[span, tile * LANES:(tile + 1) * LANES].astype(jnp.float32)

            assemble(part, outs, old, put)
            stats[span, :] = noted
            return carry

        lax.fori_loop(0, BLOCKS, run, 0)
        for d in order:
            back_copy(d, part).start()
        for d in range(TEAM):
            high = note_sizes[d]
            folded = None
            for k in range(LANES // STAT):
                piece = stats[starts[d] + k * high:starts[d] + (k + 1) * high, :]
                folded = piece if k == 0 else folded + pltpu.roll(piece, k * STAT, 1)
            note_out[part, note_rows(d), :] = folded
            if d:
                note_copy(d, part).start()

    for part in range(PARTS):
        for d in order:
            forth_copy(d, part).wait_recv()
        each(TEAM, lambda e, part=part: cache_copy(e, part, lax.rem(work + TEAM - e, TEAM)).wait_recv())
        prefix(part)
        if part == 0:
            swap.wait_recv()
            weave(1, 1 - half)
    back[rows_of(0), :] = result[rows_of(0), :]
    note_in[:, note_rows(0), :] = note_out[:, note_rows(0), :]
    own_fresh.wait()

    eye = lax.broadcasted_iota(jnp.int32, (toks, toks), 0) == lane_iota((toks, toks))
    causal = lane_iota((toks, toks)) <= lax.broadcasted_iota(jnp.int32, (toks, toks), 0)
    lanes = lane_iota((toks, LANES))

    def column(row):
        return jnp.sum(jnp.where(eye, row, 0.0), axis=1, keepdims=True)

    def choose(i, carry):
        span = pl.ds(pl.multiple_of(i * toks, toks), toks)
        codes = code_ref[level, pl.ds(i, 1), :]
        goal = lax.div(codes, CODE)
        seat = codes - goal * CODE
        for d in range(1, TEAM):
            seat = jnp.where(goal == partners[d], seat + starts[d], seat)
        seat = column(seat.astype(jnp.float32)).astype(jnp.int32)
        picks[span, :] = jnp.where(lane_iota((toks, total_rows)) == seat, 1.0, 0.0).astype(jnp.bfloat16)
        local[span, :] = jnp.zeros((toks, LANES), jnp.float32)
        return carry

    lax.fori_loop(0, TEAM, choose, 0)

    def suffix(part):
        def run(i, carry):
            span = pl.ds(pl.multiple_of(i * toks, toks), toks)
            asks = req_ref[level, pl.ds(i, 1), :].astype(jnp.float32)
            allowed = (column(asks) == asks) & causal
            noted = local[span, :]
            outs = {}
            for j in heads_of(part):
                low, high = window(j)
                scores = dot_nt(masked_window(pool_ref[span, low:high], j), fresh[0, span, low:high]) * scale
                scores = jnp.where(allowed, scores, -jnp.inf)
                peak = jnp.max(scores, axis=1, keepdims=True)
                raised = jnp.exp(scores - peak)
                total = jnp.sum(raised, axis=1, keepdims=True)
                outs[j] = dot_nn(raised.astype(jnp.bfloat16), fresh[1, span, low:high])
                noted = jnp.where(lanes == j, peak, noted)
                noted = jnp.where(lanes == PER + j, total, noted)

            def put(tile, values):
                mixed[span, tile * LANES:(tile + 1) * LANES] = values

            def old(tile):
                return mixed[span, tile * LANES:(tile + 1) * LANES]

            assemble(part, outs, old, put)
            local[span, :] = noted
            return carry

        lax.fori_loop(0, TEAM, run, 0)

    def unfold(part):
        for d in range(TEAM):
            piece = note_in[part, note_rows(d), :]
            turned = [piece] + [pltpu.roll(piece, LANES - k * STAT, 1) for k in range(1, LANES // STAT)]
            full = jnp.concatenate(turned, axis=0)[:sizes[d]]
            full = jnp.where(lane_iota((sizes[d], LANES)) < STAT, full, 0.0)
            high = full.astype(jnp.bfloat16).astype(jnp.float32)
            rest = full - high
            mid = rest.astype(jnp.bfloat16).astype(jnp.float32)
            packed = high + pltpu.roll(mid, STAT, 1) + pltpu.roll(rest - mid, 2 * STAT, 1)
            notes[rows_of(d), :] = packed.astype(jnp.bfloat16)

    def finish(part):
        low, high = outer[part]

        def run(turn, carry):
            k = lax.rem(turn + 1, TEAM)
            span = pl.ds(pl.multiple_of(lax.rem(work + k, TEAM) * toks, toks), toks)
            pick = picks[span, :]
            packed = dot_nn(pick, notes[...])
            prior = (packed + pltpu.roll(packed, LANES - STAT, 1)) + pltpu.roll(packed, LANES - 2 * STAT, 1)
            ready = dot_nn(pick, back[:, low:high])
            noted = local[span, :]
            top = jnp.maximum(prior, noted)
            first = pltpu.roll(prior, LANES - PER, 1) * jnp.exp(prior - top)
            second = jnp.exp(noted - top)
            below = first + second * pltpu.roll(noted, LANES - PER, 1)
            wp = first / below
            ws = second / below
            for tile in range(low // LANES, high // LANES):
                at = slice(tile * LANES, (tile + 1) * LANES)
                values = (
                    by_tile(tile, lambda j: wp[:, j:j + 1]) * ready[:, tile * LANES - low:][:, :LANES]
                    + by_tile(tile, lambda j: ws[:, j:j + 1]) * mixed[span, at]
                )
                final[span, at] = values.astype(jnp.bfloat16)

            @pl.when(k > 0)
            def _():
                final_copy(k, part, mine).start()

            final_copy(k + TEAM, part, mine).start()
            return carry

        lax.fori_loop(0, TEAM, run, 0)

    for part in range(PARTS):
        each(team, lambda e, part=part: fresh_copy(e, part, lax.rem(mine + team - e, team)).wait_recv())
        suffix(part)
        for d in order:
            back_copy(d, part).wait_recv()
            note_copy(d, part).wait_recv()
        unfold(part)
        finish(part)
    out_ref[:, band_cols(mine)] = final[team_rows(mine, rows), :]
    for part in range(PARTS):
        each(team, lambda e, part=part: final_copy(e, part, lax.rem(mine + team - e, team)).wait_recv())
    swap.wait_send()
    each(team, lambda e: query_copy(e, mine).wait_send())
    for part in range(PARTS):
        for d in range(1, TEAM):
            note_copy(d, part).wait_send()
            forth_copy(d, part).wait_send()
            back_copy(d, part).wait_send()
        each(TEAM, lambda e, part=part: cache_copy(e, part, work).wait_send())
        each(team, lambda e, part=part: fresh_copy(e, part, mine).wait_send())
        each(team, lambda e, part=part: final_copy(e, part, mine).wait_send())


REQUESTS = 8


def pooled_device(qkv, prefix_cache, suffix_lengths, request_groups, prefix_owner):
    n_head = lax.axis_size("head")
    n_tok = lax.axis_size("tok")
    here = qkv.shape[0]
    width = qkv.shape[2] // n_head
    toks = here * n_head
    scale = 1.0 / math.sqrt(HD)
    past = prefix_cache.shape[1]
    planes = jnp.transpose(qkv, (1, 0, 2))
    vmem = pl.BlockSpec(memory_space=pltpu.VMEM)
    smem = pl.BlockSpec(memory_space=pltpu.SMEM)
    hbm = pl.BlockSpec(memory_space=pltpu.HBM)
    free = pl.BlockSpec(memory_space=pl.ANY)
    dma = pltpu.SemaphoreType.DMA
    table = jax.ShapeDtypeStruct((TEAM, TEAM, LANES), jnp.int32)

    early, kv, slot, code, request, peak = pl.pallas_call(
        functools.partial(tables_kernel, FAR),
        out_shape=[
            jax.ShapeDtypeStruct((TEAM * toks, FIRST), jnp.bfloat16),
            jax.ShapeDtypeStruct((2, past, width), jnp.bfloat16),
            table, table, table, jax.ShapeDtypeStruct((1, 1), jnp.int32),
        ],
        in_specs=[vmem, vmem, vmem, hbm, hbm],
        out_specs=[vmem] * 5 + [smem],
        scratch_shapes=[
            pltpu.VMEM((8, LANES), jnp.int32),
            pltpu.VMEM((n_tok, 8, LANES), jnp.int32),
            pltpu.VMEM((past, 2, width), jnp.bfloat16),
            dma((n_tok,)), dma((n_tok,)), dma((2 * TEAM,)), dma((2 * TEAM,)), dma((2,)),
        ],
        compiler_params=pltpu.CompilerParams(
            collective_id=0, has_side_effects=True, vmem_limit_bytes=62 * 1024 * 1024
        ),
        name="tables",
    )(suffix_lengths, request_groups, prefix_owner[None], planes, prefix_cache)

    def pooled(sizes, number):
        total, block = layout(sizes)[1:]
        marks = sum(note_layout(sizes)[1])
        bf16, f32 = jnp.bfloat16, jnp.float32
        two, team = (PARTS, TEAM), (PARTS, 2 * TEAM)

        def call(early, kv, slot, code, request, planes):
            return pl.pallas_call(
                functools.partial(pool_kernel, scale, sizes),
                out_shape=[
                    jax.ShapeDtypeStruct((here, n_head * width), bf16),
                    jax.ShapeDtypeStruct((toks, 2, width), bf16),
                ],
                in_specs=[vmem, free, vmem, vmem, vmem, hbm],
                out_specs=[vmem] * 2,
                scratch_shapes=[
                    pltpu.VMEM((TEAM * toks, BAND), bf16),
                    pltpu.VMEM((TEAM * toks, BAND), f32),
                    pltpu.VMEM((TEAM * toks, LANES), f32),
                    pltpu.VMEM((total, BAND), bf16),
                    pltpu.VMEM((BLOCKS * block, BAND), bf16),
                    pltpu.VMEM((BLOCKS * block, BAND), bf16),
                    pltpu.VMEM((total, BAND), bf16),
                    pltpu.VMEM((BLOCKS * block + LANES, LANES), f32),
                    pltpu.VMEM((BLOCKS * block, LANES), f32),
                    pltpu.VMEM((TEAM, 2, past, BAND), bf16),
                    pltpu.VMEM((2, TEAM * toks, BAND), bf16),
                    pltpu.VMEM((TEAM * toks, BAND), bf16),
                    pltpu.VMEM((PARTS, marks, LANES), f32),
                    pltpu.VMEM((PARTS, marks, LANES), f32),
                    pltpu.VMEM((total, LANES), bf16),
                    pltpu.VMEM((TEAM * toks, total), bf16),
                    pltpu.VMEM((2, 2, here, width), bf16),
                    dma(two), dma(two), dma(two), dma(two), dma(two), dma(two),
                    dma(team), dma(team), dma(team), dma(team), dma(two), dma(two),
                    dma((1,)), dma((1,)), dma((2 * TEAM,)), dma((2 * TEAM,)), dma((5,)),
                ],
                compiler_params=pltpu.CompilerParams(
                    collective_id=number, has_side_effects=True, vmem_limit_bytes=52 * 1024 * 1024
                ),
                name="pooled",
            )(early, kv, slot, code, request, planes)

        return call

    choices = [(NEAR, NEAR, size, size) for size in FAR] + [(MOST,) * TEAM]
    return lax.switch(
        peak[0, 0], [pooled(sizes, 1 + i) for i, sizes in enumerate(choices)],
        early, kv, slot, code, request, planes,
    )


def solution(mesh):
    in_specs = (
        P(("tok", "head"), None, None),
        P("tok", None, None, "head"),
        P("tok", None),
        P("tok", None),
        P(),
    )
    out_specs = (P(("tok", "head"), None), P("tok", None, "head"))
    pooled = mesh.shape["tok"] == TEAM * TEAM and BAND * TEAM * mesh.shape["head"] == FEATURES
    body = pooled_device if pooled else generic_device
    return jax.shard_map(
        body, mesh=mesh, in_specs=in_specs, out_specs=out_specs, check_vma=False
    )
```

```python
import functools
import math

import jax
import jax.numpy as jnp
from jax import lax
from jax.experimental import pallas as pl
from jax.experimental.pallas import tpu as pltpu
from jax.sharding import PartitionSpec as P

HD = 224
LANES = 128
BAND = math.lcm(HD, LANES)
PER = BAND // HD
LSPLIT = 16
PIECE = 2 * LSPLIT


def window(j):
    low = j * HD // LANES * LANES
    high = -(-(j + 1) * HD // LANES) * LANES
    return low, high


def owners_of(tile):
    first = tile * LANES // HD
    last = ((tile + 1) * LANES - 1) // HD
    return first, last


def lane_iota(shape):
    return lax.broadcasted_iota(jnp.int32, shape, len(shape) - 1)


def by_tile(tile, pick):
    first, last = owners_of(tile)
    left = pick(first)
    if first == last:
        return left
    right = pick(last)
    edge = last * HD - tile * LANES
    return jnp.where(lane_iota((right.shape[0], LANES)) < edge, left, right)


def masked_query(query, j):
    low, high = window(j)
    cols = lane_iota((query.shape[0], high - low)) + low
    keep = (cols >= j * HD) & (cols < (j + 1) * HD)
    return jnp.where(keep, query[:, low:high], jnp.zeros((), query.dtype))


def dot_nt(a, b):
    return lax.dot_general(a, b, (((1,), (1,)), ((), ())), preferred_element_type=jnp.float32)


def dot_nn(a, b):
    return lax.dot_general(a, b, (((1,), (0,)), ((), ())), preferred_element_type=jnp.float32)


def spread_kernel(target_ref, query_ref, out_ref):
    rows = out_ref.shape[0]
    toks = target_ref.shape[1]
    place = lax.broadcasted_iota(jnp.int32, (rows, toks), 0)
    pick = jnp.where(place == target_ref[...], 1.0, 0.0).astype(jnp.bfloat16)
    out_ref[...] = dot_nn(pick, query_ref[...]).astype(jnp.bfloat16)


def attend(query, keys, values, allowed, scale, normalise, put, stats_ref, band=None):
    band = pl.program_id(0) if band is None else band
    rows = query.shape[0]
    lanes = lane_iota((rows, LANES))

    if isinstance(band, int):
        stats = jnp.zeros_like(stats_ref) if band == 0 else stats_ref[...]
    else:

        @pl.when(band == 0)
        def _():
            stats_ref[...] = jnp.zeros_like(stats_ref)

        stats = stats_ref[...]
    mixed = []
    for j in range(PER):
        low, high = window(j)
        scores = dot_nt(masked_query(query, j), keys[:, low:high]) * scale
        if allowed is not None:
            scores = jnp.where(allowed, scores, -jnp.inf)
        peak = jnp.max(scores, axis=1, keepdims=True)
        raised = jnp.exp(scores - peak)
        total = jnp.sum(raised, axis=1, keepdims=True)
        out = dot_nn(raised.astype(jnp.bfloat16), values[:, low:high])
        if normalise:
            out = out / total
        mixed.append(out)
        head = band * PER + j
        stats = jnp.where(lanes == head, peak, stats)
        stats = jnp.where(lanes == head + LSPLIT, total, stats)
    stats_ref[...] = stats
    for tile in range(BAND // LANES):
        put(tile, by_tile(tile, lambda j: mixed[j][:, tile * LANES - window(j)[0]:][:, :LANES]))


def prefix_kernel(scale, query_ref, key_ref, value_ref, out_ref, stats_ref):
    band = pl.program_id(0)
    bands = pl.num_programs(0)
    width = out_ref.shape[1] - LANES

    def put(tile, cols):
        at = pl.multiple_of(band * BAND + tile * LANES, LANES)
        out_ref[:, pl.ds(at, LANES)] = cols.astype(out_ref.dtype)

    attend(query_ref[...], key_ref[...], value_ref[...], None, scale, True, put, stats_ref)

    @pl.when(band == bands - 1)
    def _():
        full = stats_ref[...]
        high = full.astype(jnp.bfloat16).astype(jnp.float32)
        rest = full - high
        mid = rest.astype(jnp.bfloat16).astype(jnp.float32)
        low = rest - mid
        packed = high + pltpu.roll(mid, PIECE, 1) + pltpu.roll(low, 2 * PIECE, 1)
        out_ref[:, width:] = packed.astype(out_ref.dtype)


def suffix_kernel(scale, reqc_ref, reqr_ref, query_ref, key_ref, value_ref, out_ref, stats_ref):
    toks = query_ref.shape[0]
    shape = (toks, toks)
    allowed = (reqc_ref[...] == reqr_ref[...]) & (
        lax.broadcasted_iota(jnp.int32, shape, 1) <= lax.broadcasted_iota(jnp.int32, shape, 0)
    )

    def put(tile, cols):
        out_ref[:, tile * LANES:(tile + 1) * LANES] = cols

    keys = key_ref[...].reshape(toks, BAND)
    values = value_ref[...].reshape(toks, BAND)
    attend(query_ref[...], keys, values, allowed, scale, False, put, stats_ref)


def merge_kernel(target_ref, back_ref, pstats_ref, mixed_ref, sstats_ref, out_ref):
    band = pl.program_id(0)
    rows = back_ref.shape[0]
    toks = target_ref.shape[0]
    place = lane_iota((toks, rows))
    pick = jnp.where(place == target_ref[...], 1.0, 0.0).astype(jnp.bfloat16)
    packed = dot_nn(pick, pstats_ref[...])
    prefix = (packed + pltpu.roll(packed, LANES - PIECE, 1)) + pltpu.roll(
        packed, LANES - 2 * PIECE, 1
    )
    suffix = sstats_ref[...]
    top = jnp.maximum(prefix, suffix)
    first = pltpu.roll(prefix, LANES - LSPLIT, 1) * jnp.exp(prefix - top)
    second = jnp.exp(suffix - top)
    below = first + second * pltpu.roll(suffix, LANES - LSPLIT, 1)
    wp = first / below
    ws = second / below
    lanes = lane_iota((toks, LANES))

    def column(weights, j):
        return jnp.sum(jnp.where(lanes == band * PER + j, weights, 0.0), axis=1, keepdims=True)

    cp = [column(wp, j) for j in range(PER)]
    cs = [column(ws, j) for j in range(PER)]
    for tile in range(BAND // LANES):
        cols = slice(tile * LANES, (tile + 1) * LANES)
        back = dot_nn(pick, back_ref[:, cols])
        merged = by_tile(tile, lambda j: cp[j]) * back + by_tile(tile, lambda j: cs[j]) * mixed_ref[:, cols]
        out_ref[:, cols] = merged.astype(out_ref.dtype)


def whole_block(array):
    return pl.BlockSpec(array.shape, lambda g: (0,) * array.ndim)


def band_block(rows, off=0):
    return pl.BlockSpec((rows, BAND), lambda g: (0, g + off))


def cost(flops, moved):
    return pl.CostEstimate(flops=flops, bytes_accessed=moved, transcendentals=0)


def room():
    return pltpu.CompilerParams(vmem_limit_bytes=48 * 1024 * 1024)


def exchange(x, axis):
    return lax.all_to_all(x, axis, split_axis=0, concat_axis=0, tiled=True)


def shift_exchange(x, axis):
    n = lax.axis_size(axis)
    me = lax.axis_index(axis)
    parts = [lax.dynamic_index_in_dim(x, me, 0, keepdims=False)]
    for d in range(1, n):
        ring = [(i, (i + d) % n) for i in range(n)]
        sent = lax.dynamic_index_in_dim(x, lax.rem(me + d, n), 0, keepdims=False)
        parts.append(lax.ppermute(sent, axis, ring))
    out = []
    for source in range(n):
        picked = parts[0]
        for d in range(1, n):
            picked = jnp.where(lax.rem(me + n - source, n) == d, parts[d], picked)
        out.append(picked)
    return jnp.stack(out)


def generic_device(qkv, prefix_cache, suffix_lengths, request_groups, prefix_owner):
    n_head = lax.axis_size("head")
    n_tok = lax.axis_size("tok")
    here = qkv.shape[0]
    width = qkv.shape[2] // n_head
    toks = here * n_head
    scale = 1.0 / math.sqrt(HD)
    bands = width // BAND
    parts = 1
    each = bands // parts
    cols = each * BAND
    capacity = 3 * toks // n_tok
    rows = n_tok * capacity
    planes = jnp.transpose(qkv, (1, 0, 2)).reshape(3, here, n_head, width)
    queries = [
        exchange(
            jnp.stack([qkv[:, 0, h * width:(h + 1) * width] for h in range(n_head)]), "head"
        ).reshape(toks, cols)
        for p in range(parts)
    ]
    kv_send = jnp.transpose(planes[1:], (2, 0, 1, 3))

    lengths = suffix_lengths[0]
    groups = request_groups[0]
    requests = lengths.shape[0]
    ends = jnp.sum(jnp.where(jnp.arange(requests)[:, None] <= jnp.arange(requests)[None, :], lengths[:, None], 0), axis=0)
    starts = ends - lengths
    slots = jnp.sum(jnp.where(groups[:, None] == jnp.arange(n_tok)[None, :], prefix_owner[None, :], 0), axis=1)
    position = jnp.arange(toks, dtype=jnp.int32)
    request = jnp.sum((position[:, None] >= ends[None, :]).astype(jnp.int32), axis=1)
    base = slots * capacity - starts
    inside = request[:, None] == jnp.arange(requests, dtype=jnp.int32)[None, :]
    target = (position + jnp.sum(jnp.where(inside, base[None, :], 0), axis=1)).astype(jnp.int32)
    target_row = target[None, :]
    target_col = target[:, None]
    reqc, reqr = request[:, None], request[None, :]

    prefix_len = prefix_cache.shape[1]
    queries[0], cache_keys, cache_values = lax.optimization_barrier(
        (queries[0], prefix_cache[0, :, 0], prefix_cache[0, :, 1])
    )
    received = []
    for p in range(parts):
        outgoing = pl.pallas_call(
            spread_kernel,
            grid=(each,),
            out_shape=jax.ShapeDtypeStruct((rows, cols), jnp.bfloat16),
            in_specs=[whole_block(target_row), band_block(toks)],
            out_specs=band_block(rows),
            cost_estimate=cost(2 * rows * toks * cols, 2 * (rows + toks) * cols),
            compiler_params=room(),
            name="spread",
        )(target_row, queries[p])
        if p == 0:
            outgoing, kv_send = lax.optimization_barrier((outgoing, kv_send))
        received.append(exchange(outgoing.reshape(n_tok, capacity, cols), "tok").reshape(rows, cols))
    kv = shift_exchange(kv_send, "head")

    back = []
    for p in range(parts):
        mixed = pl.pallas_call(
            functools.partial(prefix_kernel, scale),
            grid=(each,),
            out_shape=jax.ShapeDtypeStruct((rows, cols + LANES), jnp.bfloat16),
            in_specs=[band_block(rows), band_block(prefix_len, p * each), band_block(prefix_len, p * each)],
            out_specs=pl.BlockSpec((rows, cols + LANES), lambda g: (0, 0)),
            scratch_shapes=[pltpu.VMEM((rows, LANES), jnp.float32)],
            cost_estimate=cost(4 * rows * prefix_len * cols, 4 * (rows + prefix_len) * cols),
            compiler_params=room(),
            name="prefix",
        )(received[p], cache_keys, cache_values)
        back.append(exchange(mixed.reshape(n_tok, capacity, cols + LANES), "tok").reshape(rows, cols + LANES))

    finals = []
    for p in range(parts):
        key_spec = pl.BlockSpec((n_head, None, here, BAND), lambda g, p=p: (0, 0, 0, g + p * each))
        value_spec = pl.BlockSpec((n_head, None, here, BAND), lambda g, p=p: (0, 1, 0, g + p * each))
        mixed_s, stats_s = pl.pallas_call(
            functools.partial(suffix_kernel, scale),
            grid=(each,),
            out_shape=[
                jax.ShapeDtypeStruct((toks, cols), jnp.float32),
                jax.ShapeDtypeStruct((toks, LANES), jnp.float32),
            ],
            in_specs=[whole_block(reqc), whole_block(reqr), band_block(toks), key_spec, value_spec],
            out_specs=[band_block(toks), pl.BlockSpec((toks, LANES), lambda g: (0, 0))],
            cost_estimate=cost(4 * toks * toks * cols, 10 * toks * cols),
            compiler_params=room(),
            name="suffix",
        )(reqc, reqr, queries[p], kv, kv)
        merged = pl.pallas_call(
            merge_kernel,
            grid=(each,),
            out_shape=jax.ShapeDtypeStruct((toks, cols), jnp.bfloat16),
            in_specs=[
                whole_block(target_col),
                band_block(rows),
                pl.BlockSpec((rows, LANES), lambda g: (0, cols // LANES)),
                band_block(toks),
                whole_block(stats_s),
            ],
            out_specs=band_block(toks),
            cost_estimate=cost(2 * rows * toks * cols, 2 * (rows + 3 * toks) * cols),
            compiler_params=room(),
            name="merge",
        )(target_col, back[p], back[p], mixed_s, stats_s)
        finals.append(exchange(merged.reshape(n_head, here, cols), "head"))
    attended = jnp.transpose(jnp.stack(finals, axis=2), (1, 0, 2, 3)).reshape(here, n_head * width)
    suffix_cache = jnp.transpose(kv, (0, 2, 1, 3)).reshape(toks, 2, width)
    return (attended, suffix_cache)


TEAM = 4
FEATURES = 7168
CODE = 1024
FAR = (208, 224, 240)
NEAR = 256
MOST = 384
BLOCKS = 8
INNER = ((0, 512), (512, 768), (768, 896))
OUTER = ((0, 384), (384, 640), (640, 896))
TURNS = ((0, 1), (2,), (3,))
PARTS = len(TURNS)
FIRST = INNER[0][1]
STAT = 8
MESH = pl.DeviceIdType.MESH


def place():
    tok = lax.axis_index("tok")
    half = lax.axis_index("head")
    return lax.div(tok, TEAM), lax.rem(tok, TEAM), half


def team_at(member, level):
    return {"tok": level * TEAM + lax.rem(member, TEAM), "head": lax.div(member, TEAM)}


def team_rows(member, rows):
    at = (lax.rem(member, TEAM) * 2 + lax.div(member, TEAM)) * rows
    return pl.ds(pl.multiple_of(at, 16), rows)


def band_cols(member, low=0, wide=BAND):
    return pl.ds(pl.multiple_of(member * BAND + low, LANES), wide)


def layout(sizes):
    starts = [sum(sizes[:d]) for d in range(TEAM)]
    total = sum(sizes)
    return starts, total, -(-total // (16 * BLOCKS)) * 16


def note_layout(sizes):
    high = [-(-size // LANES) * STAT for size in sizes]
    return [sum(high[:d]) for d in range(TEAM)], high


def masked_window(query, j):
    low, high = window(j)
    cols = lane_iota((query.shape[0], high - low)) + low
    keep = (cols >= j * HD) & (cols < (j + 1) * HD)
    return jnp.where(keep, query, jnp.zeros((), query.dtype))


def tables_kernel(
    far_sizes, lengths_ref, groups_ref, owner_ref, qkv_ref, cache_ref,
    pool_ref, kv_ref, slot_ref, code_ref, req_ref, peak_ref,
    meta, table, cache, sm, rm, sq, rq, sl,
):
    level, work, half = place()
    tok = level * TEAM + work
    team = 2 * TEAM
    mine = half * TEAM + work
    n = lax.axis_size("tok")
    rows = qkv_ref.shape[1]
    width = kv_ref.shape[2]

    def tok_peer(d):
        return {"tok": lax.rem(tok + d, n), "head": half}

    def meta_copy(d, landing):
        return pltpu.make_async_remote_copy(
            src_ref=meta, dst_ref=table.at[landing], send_sem=sm.at[d], recv_sem=rm.at[d],
            device_id=tok_peer(d), device_id_type=MESH,
        )

    def query_copy(e, landing):
        peer = lax.rem(mine + e, team)
        return pltpu.make_async_remote_copy(
            src_ref=qkv_ref.at[0, :, band_cols(peer, 0, FIRST)],
            dst_ref=pool_ref.at[team_rows(landing, rows), :],
            send_sem=sq.at[e], recv_sem=rq.at[e],
            device_id=team_at(peer, level), device_id_type=MESH,
        )

    def each(body, count):
        def step(d, carry):
            body(d)
            return carry

        lax.fori_loop(1, count, step, 0)

    barrier = pltpu.get_barrier_semaphore()
    each(lambda d: pl.semaphore_signal(barrier, inc=1, device_id=tok_peer(d), device_id_type=MESH), n)
    for w in range(TEAM):
        pl.semaphore_signal(
            barrier, inc=1, device_id={"tok": level * TEAM + w, "head": 1 - half}, device_id_type=MESH
        )
    bring = pltpu.make_async_copy(cache_ref.at[0], cache, sl.at[0])
    bring.start()
    own = pltpu.make_async_copy(
        qkv_ref.at[0, :, band_cols(mine, 0, FIRST)], pool_ref.at[team_rows(mine, rows), :], sl.at[1]
    )
    own.start()
    count = lengths_ref.shape[1]
    meta[...] = jnp.zeros_like(meta)
    meta[0:1, 0:count] = lengths_ref[...]
    meta[1:2, 0:count] = groups_ref[...]
    pl.semaphore_wait(barrier, n - 1 + TEAM)
    each(lambda d: meta_copy(d, tok).start(), n)
    each(lambda e: query_copy(e, mine).start(), team)
    table[tok] = meta[...]
    bring.wait()
    past = kv_ref.shape[1]
    aim = lax.broadcasted_iota(jnp.int32, (past, 2 * past), 1)
    source = 2 * lax.broadcasted_iota(jnp.int32, (past, 2 * past), 0)
    even = jnp.where(aim == source, 1.0, 0.0).astype(jnp.bfloat16)
    odd = jnp.where(aim == source + 1, 1.0, 0.0).astype(jnp.bfloat16)

    def split(c, carry):
        span = pl.ds(pl.multiple_of(c * 2 * LANES, LANES), 2 * LANES)
        both = cache[:, :, span].reshape(2 * past, 2 * LANES)
        kv_ref[0, :, span] = dot_nn(even, both).astype(jnp.bfloat16)
        kv_ref[1, :, span] = dot_nn(odd, both).astype(jnp.bfloat16)
        return carry

    lax.fori_loop(0, width // (2 * LANES), split, 0)
    each(lambda d: meta_copy(d, lax.rem(tok + n - d, n)).wait_recv(), n)

    lengths = table[:, 0, :]
    groups = table[:, 1, :]
    slots = jnp.zeros_like(groups)
    owners = owner_ref[...]
    for g in range(owners.shape[1]):
        slots = jnp.where(groups == g, owners[:, g:g + 1], slots)
    spot = lane_iota((n, LANES))
    slot = jnp.zeros((n, LANES), jnp.int32)
    request = jnp.zeros((n, LANES), jnp.int32)
    end = jnp.zeros((n, 1), jnp.int32)
    for r in range(REQUESTS):
        start = end
        end = start + lengths[:, r:r + 1]
        inside = (spot >= start) & (spot < end)
        slot = jnp.where(inside, slots[:, r:r + 1], slot)
        request = jnp.where(inside, r, request)
    goal = lax.div(slot, TEAM)
    marks = [jnp.where(goal == z, 1.0, 0.0) for z in range(TEAM)]
    hot = jnp.concatenate(marks, axis=0).astype(jnp.bfloat16)
    down = lax.broadcasted_iota(jnp.int32, (LANES, LANES), 0)
    upto = jnp.where(down <= lane_iota((LANES, LANES)), 1.0, 0.0).astype(jnp.bfloat16)
    running = dot_nn(hot, upto)
    totals = dot_nn(hot, jnp.ones((LANES, LANES), jnp.bfloat16))
    m = TEAM * n
    a = lax.broadcasted_iota(jnp.int32, (m, m), 0)
    b = lax.broadcasted_iota(jnp.int32, (m, m), 1)
    earlier = (lax.div(a, TEAM) == lax.div(b, TEAM)) & (b < a)
    before = dot_nn(jnp.where(earlier, 1.0, 0.0).astype(jnp.bfloat16), totals.astype(jnp.bfloat16))
    count = (running + before).astype(jnp.int32)
    code = jnp.zeros((n, LANES), jnp.int32)
    for z in range(TEAM):
        code = jnp.where(goal == z, z * CODE + count[z * n:(z + 1) * n] - 1, code)
    slot = slot - goal * TEAM
    for z in range(TEAM):
        part = slice(z * TEAM, (z + 1) * TEAM)
        slot_ref[z] = slot[part]
        code_ref[z] = code[part]
        req_ref[z] = request[part]
    aim = lax.div(lax.broadcasted_iota(jnp.int32, (m, LANES), 0), n)
    source = lax.div(lax.rem(lax.broadcasted_iota(jnp.int32, (m, LANES), 0), n), TEAM)
    far = lax.div(aim, 2) != lax.div(source, 2)
    need = jnp.where(far, count, jnp.where(count > NEAR, MOST, 0))
    most = jnp.max(need)
    choice = jnp.int32(0)
    for size in far_sizes:
        choice = choice + (most > size).astype(jnp.int32)
    peak_ref[0, 0] = choice

    own.wait()
    each(lambda d: meta_copy(d, tok).wait_send(), n)
    each(lambda e: query_copy(e, mine).wait_send(), team)
    each(lambda e: query_copy(e, lax.rem(mine + team - e, team)).wait_recv(), team)


def pool_kernel(
    scale, sizes, early_ref, kv_ref, slot_ref, code_ref, req_ref, qkv_ref, out_ref, pair_ref,
    pool_ref, mixed, local, outgo, income, result, back, stats, cols, keep, fresh, final,
    note_out, note_in, notes, picks, pair,
    s1, r1, s2, r2, s3, r3, s4, r4, s5, r5, s6, r6, s7, r7, s8, r8, sl,
):
    level, work, half = place()
    team = 2 * TEAM
    mine = half * TEAM + work
    rows = qkv_ref.shape[1]
    toks = 2 * rows
    width = kv_ref.shape[2]
    starts, total_rows, block = layout(sizes)
    note_starts, note_sizes = note_layout(sizes)
    partners = (
        level, level + 1 - 2 * lax.rem(level, 2), lax.rem(level + 2, TEAM), TEAM - 1 - level,
    )
    order = (2, 3, 1)
    inner, outer = INNER, OUTER

    def rows_of(d):
        return slice(starts[d], starts[d] + sizes[d])

    def note_rows(d):
        return slice(note_starts[d], note_starts[d] + note_sizes[d])

    def level_id(d):
        return {"tok": partners[d] * TEAM + work, "head": half}

    def query_copy(e, landing):
        peer = lax.rem(mine + e, team)
        return pltpu.make_async_remote_copy(
            src_ref=qkv_ref.at[0, :, band_cols(peer, FIRST, BAND - FIRST)],
            dst_ref=pool_ref.at[team_rows(landing, rows), FIRST:BAND],
            send_sem=s8.at[e], recv_sem=r8.at[e],
            device_id=team_at(peer, level), device_id_type=MESH,
        )

    def forth_copy(d, part):
        span = slice(*inner[part])
        return pltpu.make_async_remote_copy(
            src_ref=outgo.at[rows_of(d), span], dst_ref=income.at[rows_of(d), span],
            send_sem=s1.at[part, d], recv_sem=r1.at[part, d],
            device_id=level_id(d), device_id_type=MESH,
        )

    def back_copy(d, part):
        span = slice(*outer[part])
        return pltpu.make_async_remote_copy(
            src_ref=result.at[rows_of(d), span], dst_ref=back.at[rows_of(d), span],
            send_sem=s2.at[part, d], recv_sem=r2.at[part, d],
            device_id=level_id(d), device_id_type=MESH,
        )

    def note_copy(d, part):
        return pltpu.make_async_remote_copy(
            src_ref=note_out.at[part, note_rows(d), :], dst_ref=note_in.at[part, note_rows(d), :],
            send_sem=s6.at[part, d], recv_sem=r6.at[part, d],
            device_id=level_id(d), device_id_type=MESH,
        )

    def cache_copy(e, part, landing):
        peer = lax.rem(work + e, TEAM)
        low, high = inner[part]
        return pltpu.make_async_remote_copy(
            src_ref=kv_ref.at[:, :, band_cols(peer, low, high - low)],
            dst_ref=keep.at[landing, :, :, low:high],
            send_sem=s3.at[part, e], recv_sem=r3.at[part, e],
            device_id={"tok": level * TEAM + peer, "head": half}, device_id_type=MESH,
        )

    def fresh_copy(e, part, landing):
        peer = lax.rem(mine + e, team)
        low, high = inner[part]
        return pltpu.make_async_remote_copy(
            src_ref=qkv_ref.at[1:3, :, band_cols(peer, low, high - low)],
            dst_ref=fresh.at[:, team_rows(landing, rows), low:high],
            send_sem=s4.at[part, e], recv_sem=r4.at[part, e],
            device_id=team_at(peer, level), device_id_type=MESH,
        )

    def final_copy(e, part, landing):
        peer = lax.rem(mine + e, team)
        low, high = outer[part]
        return pltpu.make_async_remote_copy(
            src_ref=final.at[team_rows(peer, rows), low:high],
            dst_ref=out_ref.at[:, band_cols(landing, low, high - low)],
            send_sem=s5.at[part, e], recv_sem=r5.at[part, e],
            device_id=team_at(peer, level), device_id_type=MESH,
        )

    def half_cols(which):
        return pl.ds(pl.multiple_of(which * width, LANES), width)

    swap = pltpu.make_async_remote_copy(
        src_ref=qkv_ref.at[1:3, :, half_cols(1 - half)], dst_ref=pair.at[1],
        send_sem=s7.at[0], recv_sem=r7.at[0],
        device_id={"tok": level * TEAM + work, "head": 1 - half}, device_id_type=MESH,
    )

    def weave(which, owner):
        where = pl.ds(pl.multiple_of(owner * rows, 16), rows)

        def step(c, carry):
            span = pl.ds(pl.multiple_of(c * LANES, LANES), LANES)
            pair_ref[where, 0, span] = pair[which, 0, :, span]
            pair_ref[where, 1, span] = pair[which, 1, :, span]
            return carry

        lax.fori_loop(0, width // LANES, step, 0)

    def each(count, step):
        def run(e, carry):
            step(e)
            return carry

        lax.fori_loop(1, count, run, 0)

    barrier = pltpu.get_barrier_semaphore()
    for e in range(1, team):
        pl.semaphore_signal(barrier, inc=1, device_id=team_at(lax.rem(mine + e, team), level), device_id_type=MESH)
    for d in range(1, TEAM):
        pl.semaphore_signal(barrier, inc=1, device_id=level_id(d), device_id_type=MESH)
    own_query = pltpu.make_async_copy(
        qkv_ref.at[0, :, band_cols(mine, FIRST, BAND - FIRST)],
        pool_ref.at[team_rows(mine, rows), FIRST:BAND], sl.at[4],
    )
    own_query.start()
    early = pltpu.make_async_copy(early_ref, pool_ref.at[:, 0:FIRST], sl.at[3])
    early.start()
    own_fresh = pltpu.make_async_copy(
        qkv_ref.at[1:3, :, band_cols(mine)], fresh.at[:, team_rows(mine, rows), :], sl.at[1]
    )
    own_fresh.start()
    own_pair = pltpu.make_async_copy(qkv_ref.at[1:3, :, half_cols(half)], pair.at[0], sl.at[2])
    own_pair.start()
    own_cache = pltpu.make_async_copy(kv_ref.at[:, :, band_cols(work)], keep.at[work], sl.at[0])
    own_cache.start()

    def flat(ref, z):
        entry = ref[z]
        return jnp.concatenate([entry[i:i + 1] for i in range(TEAM)], axis=1)

    code = flat(code_ref, level)

    def packed(d, part):
        source = early_ref[...] if part == 0 else pool_ref[:, FIRST:BAND]
        down = lax.broadcasted_iota(jnp.int32, (sizes[d], TEAM * toks), 0)
        pick = jnp.where(down == code - partners[d] * CODE, 1.0, 0.0).astype(jnp.bfloat16)
        return dot_nn(pick, source).astype(jnp.bfloat16)

    for d in order:
        outgo[rows_of(d), 0:FIRST] = packed(d, 0)
    pl.semaphore_wait(barrier, team - 1 + TEAM - 1)
    for d in order:
        forth_copy(d, 0).start()
    each(team, lambda e: query_copy(e, mine).start())
    for part in range(PARTS):
        each(TEAM, lambda e, part=part: cache_copy(e, part, work).start())
    for late in range(PARTS):
        each(team, lambda e, part=late: fresh_copy(e, part, mine).start())
    swap.start()
    own_query.wait()
    early.wait()
    each(team, lambda e: query_copy(e, lax.rem(mine + team - e, team)).wait_recv())
    for d in order:
        outgo[rows_of(d), FIRST:BAND] = packed(d, 1)
        forth_copy(d, 1).start()
    for part in range(2, PARTS):
        for d in order:
            forth_copy(d, part).start()
    income[rows_of(0), 0:FIRST] = packed(0, 0)
    income[rows_of(0), FIRST:BAND] = packed(0, 1)
    for d in range(TEAM):
        down = lax.broadcasted_iota(jnp.int32, (sizes[d], TEAM * toks), 0)
        hit = down == flat(code_ref, partners[d]) - level * CODE
        seats = flat(slot_ref, partners[d]).astype(jnp.float32)
        found = jnp.sum(jnp.where(hit, seats, 0.0), axis=1, keepdims=True)
        cols[rows_of(d), :] = jnp.broadcast_to(found, (sizes[d], LANES))
    spare = BLOCKS * block - total_rows
    if spare:
        income[total_rows:BLOCKS * block, :] = jnp.zeros((spare, BAND), jnp.bfloat16)
        cols[total_rows:BLOCKS * block, :] = jnp.zeros((spare, LANES), jnp.float32)
    stats[...] = jnp.zeros_like(stats)
    own_pair.wait()
    weave(0, half)
    own_cache.wait()

    def heads_of(part):
        return TURNS[part]

    def assemble(part, outs, old, keep_tile):
        stop = -(-(TURNS[part][-1] + 1) * HD // LANES)
        for tile in range(outer[part][0] // LANES, stop):
            owners = owners_of(tile)
            first, last = owners[0], owners[-1]

            def cut(j):
                return outs[j][:, tile * LANES - window(j)[0]:][:, :LANES]

            if last not in outs:
                values = cut(first)
            elif first in outs:
                values = by_tile(tile, cut)
            else:
                before = old(tile)
                values = jnp.where(lane_iota(before.shape) < last * HD - tile * LANES, before, cut(last))
            keep_tile(tile, values)

    def prefix(part):
        def run(b, carry):
            span = pl.ds(pl.multiple_of(b * block, 16), block)
            which = cols[span, :][:, :1]
            lanes = lane_iota((block, LANES))
            noted = stats[span, :]
            outs = {}
            for j in heads_of(part):
                low, high = window(j)
                asked = masked_window(income[span, low:high], j)
                scores = None
                for s in range(TEAM):
                    some = dot_nt(asked, keep[s, 0, :, low:high])
                    scores = some if s == 0 else jnp.where(which == s, some, scores)
                scores = scores * scale
                top = jnp.max(scores, axis=1, keepdims=True)
                raised = jnp.exp(scores - top)
                total = jnp.sum(raised, axis=1, keepdims=True)
                out = None
                for s in range(TEAM):
                    weights = jnp.where(which == s, raised, 0.0).astype(jnp.bfloat16)
                    term = dot_nn(weights, keep[s, 1, :, low:high])
                    out = term if s == 0 else out + term
                outs[j] = out / total
                noted = jnp.where(lanes == j, top, noted)
                noted = jnp.where(lanes == PER + j, total, noted)

            def put(tile, values):
                result[span, tile * LANES:(tile + 1) * LANES] = values.astype(jnp.bfloat16)

            def old(tile):
                return result[span, tile * LANES:(tile + 1) * LANES].astype(jnp.float32)

            assemble(part, outs, old, put)
            stats[span, :] = noted
            return carry

        lax.fori_loop(0, BLOCKS, run, 0)
        for d in order:
            back_copy(d, part).start()
        for d in range(TEAM):
            high = note_sizes[d]
            folded = None
            for k in range(LANES // STAT):
                piece = stats[starts[d] + k * high:starts[d] + (k + 1) * high, :]
                folded = piece if k == 0 else folded + pltpu.roll(piece, k * STAT, 1)
            note_out[part, note_rows(d), :] = folded
            if d:
                note_copy(d, part).start()

    for part in range(PARTS):
        for d in order:
            forth_copy(d, part).wait_recv()
        each(TEAM, lambda e, part=part: cache_copy(e, part, lax.rem(work + TEAM - e, TEAM)).wait_recv())
        prefix(part)
        if part == 0:
            swap.wait_recv()
            weave(1, 1 - half)
    back[rows_of(0), :] = result[rows_of(0), :]
    note_in[:, note_rows(0), :] = note_out[:, note_rows(0), :]
    own_fresh.wait()

    eye = lax.broadcasted_iota(jnp.int32, (toks, toks), 0) == lane_iota((toks, toks))
    causal = lane_iota((toks, toks)) <= lax.broadcasted_iota(jnp.int32, (toks, toks), 0)
    lanes = lane_iota((toks, LANES))

    def column(row):
        return jnp.sum(jnp.where(eye, row, 0.0), axis=1, keepdims=True)

    def choose(i, carry):
        span = pl.ds(pl.multiple_of(i * toks, toks), toks)
        codes = code_ref[level, pl.ds(i, 1), :]
        goal = lax.div(codes, CODE)
        seat = codes - goal * CODE
        for d in range(1, TEAM):
            seat = jnp.where(goal == partners[d], seat + starts[d], seat)
        seat = column(seat.astype(jnp.float32)).astype(jnp.int32)
        picks[span, :] = jnp.where(lane_iota((toks, total_rows)) == seat, 1.0, 0.0).astype(jnp.bfloat16)
        local[span, :] = jnp.zeros((toks, LANES), jnp.float32)
        return carry

    lax.fori_loop(0, TEAM, choose, 0)

    def suffix(part):
        def run(i, carry):
            span = pl.ds(pl.multiple_of(i * toks, toks), toks)
            asks = req_ref[level, pl.ds(i, 1), :].astype(jnp.float32)
            allowed = (column(asks) == asks) & causal
            noted = local[span, :]
            outs = {}
            for j in heads_of(part):
                low, high = window(j)
                scores = dot_nt(masked_window(pool_ref[span, low:high], j), fresh[0, span, low:high]) * scale
                scores = jnp.where(allowed, scores, -jnp.inf)
                peak = jnp.max(scores, axis=1, keepdims=True)
                raised = jnp.exp(scores - peak)
                total = jnp.sum(raised, axis=1, keepdims=True)
                outs[j] = dot_nn(raised.astype(jnp.bfloat16), fresh[1, span, low:high])
                noted = jnp.where(lanes == j, peak, noted)
                noted = jnp.where(lanes == PER + j, total, noted)

            def put(tile, values):
                mixed[span, tile * LANES:(tile + 1) * LANES] = values

            def old(tile):
                return mixed[span, tile * LANES:(tile + 1) * LANES]

            assemble(part, outs, old, put)
            local[span, :] = noted
            return carry

        lax.fori_loop(0, TEAM, run, 0)

    def unfold(part):
        for d in range(TEAM):
            piece = note_in[part, note_rows(d), :]
            turned = [piece] + [pltpu.roll(piece, LANES - k * STAT, 1) for k in range(1, LANES // STAT)]
            full = jnp.concatenate(turned, axis=0)[:sizes[d]]
            full = jnp.where(lane_iota((sizes[d], LANES)) < STAT, full, 0.0)
            high = full.astype(jnp.bfloat16).astype(jnp.float32)
            rest = full - high
            mid = rest.astype(jnp.bfloat16).astype(jnp.float32)
            packed = high + pltpu.roll(mid, STAT, 1) + pltpu.roll(rest - mid, 2 * STAT, 1)
            notes[rows_of(d), :] = packed.astype(jnp.bfloat16)

    def finish(part):
        low, high = outer[part]

        def run(turn, carry):
            k = lax.rem(turn + 1, TEAM)
            span = pl.ds(pl.multiple_of(lax.rem(work + k, TEAM) * toks, toks), toks)
            pick = picks[span, :]
            packed = dot_nn(pick, notes[...])
            prior = (packed + pltpu.roll(packed, LANES - STAT, 1)) + pltpu.roll(packed, LANES - 2 * STAT, 1)
            ready = dot_nn(pick, back[:, low:high])
            noted = local[span, :]
            top = jnp.maximum(prior, noted)
            first = pltpu.roll(prior, LANES - PER, 1) * jnp.exp(prior - top)
            second = jnp.exp(noted - top)
            below = first + second * pltpu.roll(noted, LANES - PER, 1)
            wp = first / below
            ws = second / below
            for tile in range(low // LANES, high // LANES):
                at = slice(tile * LANES, (tile + 1) * LANES)
                values = (
                    by_tile(tile, lambda j: wp[:, j:j + 1]) * ready[:, tile * LANES - low:][:, :LANES]
                    + by_tile(tile, lambda j: ws[:, j:j + 1]) * mixed[span, at]
                )
                final[span, at] = values.astype(jnp.bfloat16)

            @pl.when(k > 0)
            def _():
                final_copy(k, part, mine).start()

            final_copy(k + TEAM, part, mine).start()
            return carry

        lax.fori_loop(0, TEAM, run, 0)

    for part in range(PARTS):
        each(team, lambda e, part=part: fresh_copy(e, part, lax.rem(mine + team - e, team)).wait_recv())
        suffix(part)
        for d in order:
            back_copy(d, part).wait_recv()
            note_copy(d, part).wait_recv()
        unfold(part)
        finish(part)
    out_ref[:, band_cols(mine)] = final[team_rows(mine, rows), :]
    swap.wait_send()
    each(team, lambda e: query_copy(e, mine).wait_send())
    for part in range(PARTS):
        for d in range(1, TEAM):
            note_copy(d, part).wait_send()
            forth_copy(d, part).wait_send()
            back_copy(d, part).wait_send()
        each(TEAM, lambda e, part=part: cache_copy(e, part, work).wait_send())
        each(team, lambda e, part=part: fresh_copy(e, part, mine).wait_send())
    for part in range(PARTS):
        each(team, lambda e, part=part: final_copy(e, part, mine).wait_send())
    for part in range(PARTS):
        each(team, lambda e, part=part: final_copy(e, part, lax.rem(mine + team - e, team)).wait_recv())


REQUESTS = 8


def pooled_device(qkv, prefix_cache, suffix_lengths, request_groups, prefix_owner):
    n_head = lax.axis_size("head")
    n_tok = lax.axis_size("tok")
    here = qkv.shape[0]
    width = qkv.shape[2] // n_head
    toks = here * n_head
    scale = 1.0 / math.sqrt(HD)
    past = prefix_cache.shape[1]
    planes = jnp.transpose(qkv, (1, 0, 2))
    vmem = pl.BlockSpec(memory_space=pltpu.VMEM)
    smem = pl.BlockSpec(memory_space=pltpu.SMEM)
    hbm = pl.BlockSpec(memory_space=pltpu.HBM)
    free = pl.BlockSpec(memory_space=pl.ANY)
    dma = pltpu.SemaphoreType.DMA
    table = jax.ShapeDtypeStruct((TEAM, TEAM, LANES), jnp.int32)

    early, kv, slot, code, request, peak = pl.pallas_call(
        functools.partial(tables_kernel, FAR),
        out_shape=[
            jax.ShapeDtypeStruct((TEAM * toks, FIRST), jnp.bfloat16),
            jax.ShapeDtypeStruct((2, past, width), jnp.bfloat16),
            table, table, table, jax.ShapeDtypeStruct((1, 1), jnp.int32),
        ],
        in_specs=[vmem, vmem, vmem, hbm, hbm],
        out_specs=[vmem] * 5 + [smem],
        scratch_shapes=[
            pltpu.VMEM((8, LANES), jnp.int32),
            pltpu.VMEM((n_tok, 8, LANES), jnp.int32),
            pltpu.VMEM((past, 2, width), jnp.bfloat16),
            dma((n_tok,)), dma((n_tok,)), dma((2 * TEAM,)), dma((2 * TEAM,)), dma((2,)),
        ],
        compiler_params=pltpu.CompilerParams(
            collective_id=0, has_side_effects=True, vmem_limit_bytes=62 * 1024 * 1024
        ),
        name="tables",
    )(suffix_lengths, request_groups, prefix_owner[None], planes, prefix_cache)

    def pooled(sizes, number):
        total, block = layout(sizes)[1:]
        marks = sum(note_layout(sizes)[1])
        bf16, f32 = jnp.bfloat16, jnp.float32
        two, team = (PARTS, TEAM), (PARTS, 2 * TEAM)

        def call(early, kv, slot, code, request, planes):
            return pl.pallas_call(
                functools.partial(pool_kernel, scale, sizes),
                out_shape=[
                    jax.ShapeDtypeStruct((here, n_head * width), bf16),
                    jax.ShapeDtypeStruct((toks, 2, width), bf16),
                ],
                in_specs=[vmem, free, vmem, vmem, vmem, hbm],
                out_specs=[vmem] * 2,
                scratch_shapes=[
                    pltpu.VMEM((TEAM * toks, BAND), bf16),
                    pltpu.VMEM((TEAM * toks, BAND), f32),
                    pltpu.VMEM((TEAM * toks, LANES), f32),
                    pltpu.VMEM((total, BAND), bf16),
                    pltpu.VMEM((BLOCKS * block, BAND), bf16),
                    pltpu.VMEM((BLOCKS * block, BAND), bf16),
                    pltpu.VMEM((total, BAND), bf16),
                    pltpu.VMEM((BLOCKS * block + LANES, LANES), f32),
                    pltpu.VMEM((BLOCKS * block, LANES), f32),
                    pltpu.VMEM((TEAM, 2, past, BAND), bf16),
                    pltpu.VMEM((2, TEAM * toks, BAND), bf16),
                    pltpu.VMEM((TEAM * toks, BAND), bf16),
                    pltpu.VMEM((PARTS, marks, LANES), f32),
                    pltpu.VMEM((PARTS, marks, LANES), f32),
                    pltpu.VMEM((total, LANES), bf16),
                    pltpu.VMEM((TEAM * toks, total), bf16),
                    pltpu.VMEM((2, 2, here, width), bf16),
                    dma(two), dma(two), dma(two), dma(two), dma(two), dma(two),
                    dma(team), dma(team), dma(team), dma(team), dma(two), dma(two),
                    dma((1,)), dma((1,)), dma((2 * TEAM,)), dma((2 * TEAM,)), dma((5,)),
                ],
                compiler_params=pltpu.CompilerParams(
                    collective_id=number, has_side_effects=True, vmem_limit_bytes=52 * 1024 * 1024
                ),
                name="pooled",
            )(early, kv, slot, code, request, planes)

        return call

    choices = [(NEAR, NEAR, size, size) for size in FAR] + [(MOST,) * TEAM]
    return lax.switch(
        peak[0, 0], [pooled(sizes, 1 + i) for i, sizes in enumerate(choices)],
        early, kv, slot, code, request, planes,
    )


def solution(mesh):
    in_specs = (
        P(("tok", "head"), None, None),
        P("tok", None, None, "head"),
        P("tok", None),
        P("tok", None),
        P(),
    )
    out_specs = (P(("tok", "head"), None), P("tok", None, "head"))
    pooled = mesh.shape["tok"] == TEAM * TEAM and BAND * TEAM * mesh.shape["head"] == FEATURES
    body = pooled_device if pooled else generic_device
    return jax.shard_map(
        body, mesh=mesh, in_specs=in_specs, out_specs=out_specs, check_vma=False
    )
```
